32 devices in a mesh: ctx: 8 (over z, y), fsdp: 4 (over x, core).
Axes of the slice: x: 2, y: 2, z: 4, core: 2. Of those that a mesh axis runs over, the one named last changes fastest.
Arguments:
- inputs: bfloat16 [8, 2048, 768], P('fsdp', 'ctx'), may hold values from -6 to 6
- earlier: bfloat16 [4, 8, 2048, 768], P(None, 'fsdp', 'ctx'), may hold values from -6 to 6
- input_proj: bfloat16 [768, 2304], P('fsdp'), may hold values from -0.21875 to 0.21875
- output_proj: bfloat16 [768, 768], P('fsdp'), may hold values from -6 to 6
- up_proj: bfloat16 [768, 3072], P('fsdp'), may hold values from -0.21875 to 0.21875
- down_proj: bfloat16 [3072, 768], P('fsdp'), may hold values from -0.109375 to 0.109375
- norm1_gain: float32 [768], P('fsdp'), may hold values from 0.5 to 1.5
- norm1_bias: float32 [768], P('fsdp'), may hold values from -1.75 to 1.75
- norm2_gain: float32 [768], P('fsdp'), may hold values from 0.5 to 1.5
- norm2_bias: float32 [768], P('fsdp'), may hold values from -1.75 to 1.75
- mixing: float32 [5], replicated, may hold values from 0.3 to 1
- block_order: int32 [2, 8], replicated, may hold values from 0 to 7, each once within a row
- grad_next: bfloat16 [8, 2048, 768], P('fsdp', 'ctx'), may hold values from -6 to 6
Outputs:
- next_input: bfloat16 [8, 2048, 768], P('fsdp', 'ctx')
- grad_input: bfloat16 [8, 2048, 768], P('fsdp', 'ctx')
- grad_earlier: bfloat16 [4, 8, 2048, 768], P(None, 'fsdp', 'ctx')
- grad_input_proj: float32 [768, 2304], P('fsdp')
- grad_output_proj: float32 [768, 768], P('fsdp')
- grad_up_proj: float32 [768, 3072], P('fsdp')
- grad_down_proj: float32 [3072, 768], P('fsdp')
- grad_norm1_gain: float32 [768], P('fsdp')
- grad_norm1_bias: float32 [768], P('fsdp')
- grad_norm2_gain: float32 [768], P('fsdp')
- grad_norm2_bias: float32 [768], P('fsdp')
- grad_mixing: float32 [5], replicated
The draws below stay inside these ranges and needn't reach their ends.
Inputs may be any that keep to these rules, and one draw needn't show every extreme that they name: `block_order`: each row is an ordering of the 8 blocks of a sequence: entry c names the block held at index c of ctx, each block once.
All inputs are finite; a program needn't handle non-finite values.
Results may differ from the reference program's by a relative error of at most 0.034.
Values may be sent and summed in bfloat16 or wider, within the bound.
No kernel may reach another device: no remote copies, remote signals or barrier semaphores. Data moves between devices by JAX's collectives and lax.ppermute only.
A program may use at most 256 MiB of HBM per device.

```python
import math
import jax
import jax.numpy as jnp
from jax import lax

D = 768
HEADS = 12
HEAD_DIM = 64
FF = 3072
BLOCK = 256
STREAMS = 4
MB = 2
SEQ_LEN = 2048
SEQS = 8
N_CTX = 8


def block_scale(key, extent, cuts, least, top_value):
    level, own = 1.0, jax.random.fold_in(key, 6)
    for position, blocks in cuts:
        steps = jnp.exp(jax.random.uniform(jax.random.fold_in(own, position), (blocks,), jnp.float32, least / len(cuts), top_value / len(cuts)))
        level = level * jnp.repeat(steps, extent[position] // blocks).reshape([-1 if axis == position else 1 for axis in range(len(extent))])
    return level


def gaussian(key, dims, scale, limit, pieces=(), kind=jnp.bfloat16):
    array = scale * jax.random.normal(key, dims, jnp.float32)
    if pieces:
        array = array * block_scale(key, dims, pieces, -0.22, 0.18)
    return jnp.clip(array, -limit, limit).astype(kind)


def setup_inputs(seed: int = 0) -> dict:
    splits = jax.random.split(jax.random.key(seed), 14)
    return {
        "inputs": gaussian(splits[0], (SEQS, SEQ_LEN, D), 1.0, 6.0, ((0, 4), (1, 8))),
        "earlier": gaussian(splits[1], (STREAMS, SEQS, SEQ_LEN, D), 1.0, 6.0, ((1, 4), (2, 8))),
        "input_proj": gaussian(splits[2], (D, 3 * D), D ** -0.5, 0.21875, ((0, 4),)),
        "output_proj": gaussian(splits[3], (D, D), (max(1, D * 4 // SEQ_LEN)) ** -0.5, 6.0, ((0, 4),)),
        "up_proj": gaussian(splits[4], (D, FF), D ** -0.5, 0.21875, ((0, 4),)),
        "down_proj": gaussian(splits[5], (FF, D), FF ** -0.5, 0.109375, ((0, 4),)),
        "norm1_gain": jnp.clip(1.0 + 0.1 * jax.random.normal(splits[6], (D,), jnp.float32), 0.5, 1.5),
        "norm1_bias": gaussian(splits[7], (D,), 0.3, 1.75, ((0, 4),), jnp.float32),
        "norm2_gain": jnp.clip(1.0 + 0.1 * jax.random.normal(splits[8], (D,), jnp.float32), 0.5, 1.5),
        "norm2_bias": gaussian(splits[9], (D,), 0.3, 1.75, ((0, 4),), jnp.float32),
        "mixing": jnp.clip(jax.random.uniform(splits[10], (STREAMS + 1,), jnp.float32, 0.3, 1.0), 0.3, 1.0),
        "block_order": jax.vmap(lambda own: jax.random.permutation(own, N_CTX))(jax.random.split(splits[11], MB)).reshape((MB, N_CTX)).astype(jnp.int32),
        "grad_next": gaussian(splits[12], (SEQS, SEQ_LEN, D), 1.0, 6.0, ((0, 4), (1, 8))),
    }


@jax.custom_vjp
def low(v):
    return lax.optimization_barrier(v.astype(jnp.bfloat16)).astype(jnp.float32)

@jax.custom_vjp
def low_back(v):
    return v

def low_keep(v):
    return (low(v), None)

def low_pass(kept, grad):
    return (grad,)

def back_keep(v):
    return (v, None)

def back_low(kept, grad):
    return (low(grad),)
low.defvjp(low_keep, low_pass)
low_back.defvjp(back_keep, back_low)

def layer_norm(values, gain, bias):
    mean_value = lax.optimization_barrier(jnp.mean(values, axis=-1, keepdims=True))
    centered = values - mean_value
    variance = lax.optimization_barrier(jnp.mean(centered * centered, axis=-1, keepdims=True))
    return centered * lax.rsqrt(variance + 1e-05) * gain + bias

def rotate(values, cosine, sine):
    half_dim = values.shape[-1] // 2
    first_half = values[..., :half_dim]
    second_half = values[..., half_dim:]
    return jnp.concatenate([first_half * cosine - second_half * sine, second_half * cosine + first_half * sine], axis=-1)

def attend_block(query_block, query_id, keys, values, key_ids):
    scores = jnp.einsum('qhe,khe->hqk', query_block, keys, precision=lax.Precision.HIGHEST) * HEAD_DIM ** (-0.5)
    scores = low_back(scores)
    scores = jnp.where((key_ids <= query_id)[None, None, :], scores, -1e+30)
    probs = low(jax.nn.softmax(scores, axis=-1))
    return jnp.einsum('hqk,khe->qhe', probs, values, precision=lax.Precision.HIGHEST)

def one_sequence(block_input, previous, order_row, weights):
    input_proj, output_proj, up_proj, down_proj, gain_one, bias_one, gain_two, bias_two, mixing = weights
    highest = lax.Precision.HIGHEST
    row_ids = jnp.repeat(order_row, BLOCK)
    offsets = jnp.tile(jnp.arange(BLOCK, dtype=jnp.int32), N_CTX)
    positions = (row_ids * BLOCK + offsets).astype(jnp.float32)
    freqs = jnp.exp(jnp.arange(HEAD_DIM // 2, dtype=jnp.float32) * (-2.0 * math.log(10000.0) / HEAD_DIM))
    angle = positions[:, None] * freqs[None, :]
    cosine = jnp.cos(angle)[:, None, :]
    sine_table = jnp.sin(angle)[:, None, :]
    normed_one = low(layer_norm(block_input, gain_one, bias_one))
    projected = low_back(jnp.dot(normed_one, input_proj, precision=highest))
    query = projected[:, :D].reshape(SEQ_LEN, HEADS, HEAD_DIM)
    keys = projected[:, D:2 * D].reshape(SEQ_LEN, HEADS, HEAD_DIM)
    values = projected[:, 2 * D:].reshape(SEQ_LEN, HEADS, HEAD_DIM)
    query = low(rotate(query, cosine, sine_table))
    keys = low(rotate(keys, cosine, sine_table))
    values = low(values)
    query_blocks = query.reshape(N_CTX, BLOCK, HEADS, HEAD_DIM)
    attend = jax.checkpoint(attend_block)
    attended = lax.map(lambda pair: attend(pair[0], pair[1], keys, values, row_ids), (query_blocks, order_row))
    attended = low(low_back(attended.reshape(SEQ_LEN, D)))
    branch = low_back(jnp.dot(attended, output_proj, precision=highest))
    middle = block_input + branch
    normed_two = low(layer_norm(middle, gain_two, bias_two))
    hidden_pre = low_back(jnp.dot(normed_two, up_proj, precision=highest))
    hidden = low(jax.nn.gelu(hidden_pre))
    result = middle + low_back(jnp.dot(hidden, down_proj, precision=highest))
    return lax.optimization_barrier(jnp.sum(mixing[:STREAMS, None, None] * previous, axis=0)) + mixing[STREAMS] * result

def reference(inputs, earlier, input_proj, output_proj, up_proj, down_proj, norm1_gain, norm1_bias, norm2_gain, norm2_bias, mixing, block_order, grad_next):
    rows_order = block_order[jnp.arange(SEQS, dtype=jnp.int32) % MB]
    sequence_step = jax.checkpoint(one_sequence)

    def forward(block_inputs, previous, *weights):

        def scan_body(carry, items):
            return (carry, sequence_step(items[0], items[1], items[2], weights))
        _, outputs = lax.scan(scan_body, jnp.zeros((), jnp.float32), (block_inputs, jnp.moveaxis(previous, 1, 0), rows_order))
        return outputs
    float_args = (inputs.astype(jnp.float32), earlier.astype(jnp.float32), input_proj.astype(jnp.float32), output_proj.astype(jnp.float32), up_proj.astype(jnp.float32), down_proj.astype(jnp.float32), norm1_gain, norm1_bias, norm2_gain, norm2_bias, mixing)
    primal, pullback = jax.vjp(forward, *float_args)
    grads = pullback(grad_next.astype(jnp.float32))
    return (primal.astype(jnp.bfloat16), grads[0].astype(jnp.bfloat16), grads[1].astype(jnp.bfloat16), grads[2], grads[3], grads[4], grads[5], grads[6], grads[7], grads[8], grads[9], grads[10])
```

```python
import functools
import math

import jax
import jax.numpy as jnp
from jax import lax
from jax.experimental import pallas as pl
from jax.experimental.pallas import tpu as pltpu
from jax.sharding import PartitionSpec as P

HEADS = 12


def passed_along(value, axis, steps):
    count = lax.axis_size(axis)
    pairs = [(source, (source + steps) % count) for source in range(count)]
    return lax.ppermute(value, axis, pairs)


def norm_parts(values, gain, bias):
    mean_value = jnp.mean(values, axis=-1, keepdims=True)
    centered = values - mean_value
    inv_std = lax.rsqrt(jnp.mean(centered * centered, axis=-1, keepdims=True) + 1e-05)
    normed = centered * inv_std
    return (normed * gain + bias, normed, inv_std)


def norm_back(grad_out, normed, inv_std, gain):
    scaled = grad_out * gain
    mean_one = jnp.mean(scaled, axis=-1, keepdims=True)
    mean_two = jnp.mean(scaled * normed, axis=-1, keepdims=True)
    return inv_std * (scaled - mean_one - normed * mean_two)


def rotary_tables(block_id, block_rows, head_dim):
    half_dim = head_dim // 2
    positions = (block_id * block_rows + lax.iota(jnp.int32, block_rows)).astype(jnp.float32)
    freqs = jnp.exp(lax.iota(jnp.float32, half_dim) * (-2.0 * math.log(10000.0) / head_dim))
    angle = positions[:, None] * freqs[None, :]
    return (jnp.cos(angle)[:, None, :], jnp.sin(angle)[:, None, :])


def rotate(values, cosine, sine_table):
    half_dim = values.shape[-1] // 2
    first_half = values[..., :half_dim]
    second_half = values[..., half_dim:]
    return jnp.concatenate(
        [
            first_half * cosine - second_half * sine_table,
            second_half * cosine + first_half * sine_table,
        ],
        axis=-1,
    )


def unrotate(grads, cosine, sine_table):
    half_dim = grads.shape[-1] // 2
    first_half = grads[..., :half_dim]
    second_half = grads[..., half_dim:]
    return jnp.concatenate(
        [
            first_half * cosine + second_half * sine_table,
            second_half * cosine - first_half * sine_table,
        ],
        axis=-1,
    )


def head_view(values, head_count):
    return values.reshape(values.shape[0], head_count, values.shape[1] // head_count)


def forward_visit(state, local_query, block_keys, block_values, head_count, score_scale):
    run_max, run_sum, accum = state
    query_heads = head_view(local_query, head_count)
    key_heads = head_view(block_keys, head_count)
    value_heads = head_view(block_values, head_count)
    scores = (
        jnp.einsum("qhe,khe->hqk", query_heads, key_heads, preferred_element_type=jnp.float32)
        * score_scale
    )
    new_max = jnp.maximum(run_max, jnp.max(scores, axis=-1))
    weights = jnp.exp(scores - new_max[:, :, None])
    factor = jnp.exp(run_max - new_max)
    new_sum = run_sum * factor + jnp.sum(weights, axis=-1)
    update = jnp.einsum(
        "hqk,khe->qhe",
        weights.astype(jnp.bfloat16),
        value_heads,
        preferred_element_type=jnp.float32,
    )
    return (new_max, new_sum, accum * jnp.transpose(factor)[:, :, None] + update)


def backward_pair(
    query_rows, key_rows, value_rows, grad_rows, log_total, row_delta, head_count, score_scale
):
    query_heads = head_view(query_rows, head_count)
    key_heads = head_view(key_rows, head_count)
    value_heads = head_view(value_rows, head_count)
    grad_heads = head_view(grad_rows, head_count)
    scores = (
        jnp.einsum("qhe,khe->hqk", query_heads, key_heads, preferred_element_type=jnp.float32)
        * score_scale
    )
    probs = jnp.exp(scores - log_total[:, :, None])
    grad_probs = jnp.einsum(
        "qhe,khe->hqk", grad_heads, value_heads, preferred_element_type=jnp.float32
    )
    grad_scores = (probs * (grad_probs - row_delta[:, :, None])).astype(jnp.bfloat16)
    grad_query = (
        jnp.einsum("hqk,khe->qhe", grad_scores, key_heads, preferred_element_type=jnp.float32)
        * score_scale
    )
    grad_keys = (
        jnp.einsum("hqk,qhe->khe", grad_scores, query_heads, preferred_element_type=jnp.float32)
        * score_scale
    )
    grad_values = jnp.einsum(
        "hqk,qhe->khe", probs.astype(jnp.bfloat16), grad_heads, preferred_element_type=jnp.float32
    )
    return (
        grad_query.reshape(query_rows.shape[0], -1),
        grad_keys.reshape(key_rows.shape[0], -1),
        grad_values.reshape(key_rows.shape[0], -1),
    )


def body(
    inputs,
    earlier,
    input_proj,
    output_proj,
    up_proj,
    down_proj,
    norm1_gain,
    norm1_bias,
    norm2_gain,
    norm2_bias,
    mixing,
    block_order,
    grad_next,
):
    head_count = HEADS
    batch_count = inputs.shape[0]
    block_rows = inputs.shape[1]
    model_width = inputs.shape[2]
    head_dim = model_width // head_count
    score_scale = head_dim ** (-0.5)
    stream_count = earlier.shape[0]
    cycle_size = lax.axis_size("ctx")
    cycle_place = lax.axis_index("ctx")
    norm_stack = jnp.stack([norm1_gain, norm1_bias, norm2_gain, norm2_bias])
    full_in, full_out, full_up, full_down, full_norms = (
        lax.all_gather(input_proj, "fsdp", axis=0, tiled=True),
        lax.all_gather(output_proj, "fsdp", axis=0, tiled=True),
        lax.all_gather(up_proj, "fsdp", axis=0, tiled=True),
        lax.all_gather(down_proj, "fsdp", axis=0, tiled=True),
        lax.all_gather(norm_stack.astype(jnp.bfloat16), "fsdp", axis=1, tiled=True).astype(
            norm_stack.dtype
        ),
    )
    gain_one = full_norms[0]
    bias_one = full_norms[1]
    gain_two = full_norms[2]
    bias_two = full_norms[3]
    next_list = []
    grad_in_list = []
    earlier_list = []
    totals = None
    for batch in range(batch_count):
        block_input = inputs[batch].astype(jnp.float32)
        order_row = block_order[batch]
        own_block = order_row[cycle_place]
        cosine, sine_table = rotary_tables(own_block, block_rows, head_dim)
        normed_in, normed_one, inv_one = norm_parts(block_input, gain_one, bias_one)
        normed_in_b = normed_in.astype(jnp.bfloat16)
        projected = jnp.dot(normed_in_b, full_in, preferred_element_type=jnp.float32)
        local_query = (
            rotate(head_view(projected[:, :model_width], head_count), cosine, sine_table)
            .reshape(block_rows, model_width)
            .astype(jnp.bfloat16)
        )
        local_keys = (
            rotate(
                head_view(projected[:, model_width : 2 * model_width], head_count),
                cosine,
                sine_table,
            )
            .reshape(block_rows, model_width)
            .astype(jnp.bfloat16)
        )
        local_values = projected[:, 2 * model_width :].astype(jnp.bfloat16)
        start_state = (
            jnp.full((head_count, block_rows), -1e30, jnp.float32),
            jnp.zeros((head_count, block_rows), jnp.float32),
            jnp.zeros((block_rows, head_count, head_dim), jnp.float32),
        )
        piece_keys = lax.all_gather(local_keys, "ctx", axis=0, tiled=True)
        piece_values = lax.all_gather(local_values, "ctx", axis=0, tiled=True)
        count = piece_keys.shape[0] // block_rows

        def one_block(index, state_now):
            block_keys = lax.dynamic_slice_in_dim(piece_keys, index * block_rows, block_rows, 0)
            block_values = lax.dynamic_slice_in_dim(piece_values, index * block_rows, block_rows, 0)
            return lax.cond(
                order_row[index] <= own_block,
                lambda held: forward_visit(
                    held, local_query, block_keys, block_values, head_count, score_scale
                ),
                lambda held: held,
                state_now,
            )

        run_max, run_sum, accum = lax.fori_loop(0, count, one_block, start_state)
        log_total = run_max + jnp.log(run_sum)
        attended = accum / jnp.transpose(run_sum)[:, :, None]
        attended_b = attended.reshape(block_rows, model_width).astype(jnp.bfloat16)
        middle = block_input + jnp.dot(attended_b, full_out, preferred_element_type=jnp.float32)
        normed_mid, normed_two, inv_two = norm_parts(middle, gain_two, bias_two)
        normed_mid_b = normed_mid.astype(jnp.bfloat16)
        hidden_pre = jnp.dot(normed_mid_b, full_up, preferred_element_type=jnp.float32)
        hidden_b = jax.nn.gelu(hidden_pre).astype(jnp.bfloat16)
        result = middle + jnp.dot(hidden_b, full_down, preferred_element_type=jnp.float32)
        previous = earlier[:, batch].astype(jnp.float32)
        mixed_out = (
            jnp.sum(mixing[:stream_count, None, None] * previous, axis=0)
            + mixing[stream_count] * result
        )
        next_list.append(mixed_out.astype(jnp.bfloat16))
        grad_out = grad_next[batch].astype(jnp.float32)
        earlier_list.append(
            (mixing[:stream_count, None, None] * grad_out[None]).astype(jnp.bfloat16)
        )
        mix_grad = jnp.concatenate(
            [jnp.sum(previous * grad_out[None], axis=(1, 2)), jnp.sum(result * grad_out)[None]]
        )
        grad_result = mixing[stream_count] * grad_out
        grad_result_b = grad_result.astype(jnp.bfloat16)
        grad_down = jnp.einsum(
            "rf,rd->fd", hidden_b, grad_result_b, preferred_element_type=jnp.float32
        )
        grad_hidden = jnp.einsum(
            "rd,fd->rf", grad_result_b, full_down, preferred_element_type=jnp.float32
        )
        grad_pre = jax.vjp(jax.nn.gelu, hidden_pre)[1](grad_hidden)[0]
        grad_pre_b = grad_pre.astype(jnp.bfloat16)
        grad_up = jnp.einsum(
            "rd,rf->df", normed_mid_b, grad_pre_b, preferred_element_type=jnp.float32
        )
        grad_norm_mid = jnp.einsum(
            "rf,df->rd", grad_pre_b, full_up, preferred_element_type=jnp.float32
        )
        grad_gain_two = jnp.sum(grad_norm_mid * normed_two, axis=0)
        grad_bias_two = jnp.sum(grad_norm_mid, axis=0)
        grad_middle = grad_result + norm_back(grad_norm_mid, normed_two, inv_two, gain_two)
        grad_middle_b = grad_middle.astype(jnp.bfloat16)
        grad_out_proj = jnp.einsum(
            "rd,re->de", attended_b, grad_middle_b, preferred_element_type=jnp.float32
        )
        grad_att_b = jnp.einsum(
            "re,de->rd", grad_middle_b, full_out, preferred_element_type=jnp.float32
        ).astype(jnp.bfloat16)
        row_delta = jnp.einsum(
            "qhe,qhe->hq", head_view(grad_att_b, head_count).astype(jnp.float32), attended
        )
        zero_rows = jnp.zeros((block_rows, model_width), jnp.float32)

        def key_visit(offset, grad_query, cycle_keys, cycle_values, cycle_dk, cycle_dv):
            their_block = order_row[(cycle_place - offset) % cycle_size]

            def add_pair(held):
                part_q, part_k, part_v = backward_pair(
                    local_query,
                    cycle_keys,
                    cycle_values,
                    grad_att_b,
                    log_total,
                    row_delta,
                    head_count,
                    score_scale,
                )
                return (held[0] + part_q, held[1] + part_k, held[2] + part_v)

            return lax.cond(
                their_block <= own_block,
                add_pair,
                lambda held: held,
                (grad_query, cycle_dk, cycle_dv),
            )

        def key_turn(offset, carry):
            grad_query, cycle_keys, cycle_values, cycle_dk, cycle_dv = carry
            grad_query, cycle_dk, cycle_dv = key_visit(
                offset, grad_query, cycle_keys, cycle_values, cycle_dk, cycle_dv
            )
            cycle_keys, cycle_values = passed_along((cycle_keys, cycle_values), "ctx", 1)
            cycle_dk, cycle_dv = (
                passed_along(cycle_dk.astype(jnp.bfloat16), "ctx", 1).astype(cycle_dk.dtype),
                passed_along(cycle_dv.astype(jnp.bfloat16), "ctx", 1).astype(cycle_dv.dtype),
            )
            return (grad_query, cycle_keys, cycle_values, cycle_dk, cycle_dv)

        grad_query, cycle_keys, cycle_values, cycle_dk, cycle_dv = lax.fori_loop(
            0, cycle_size - 1, key_turn, (zero_rows, local_keys, local_values, zero_rows, zero_rows)
        )
        grad_query, cycle_dk, cycle_dv = key_visit(
            cycle_size - 1, grad_query, cycle_keys, cycle_values, cycle_dk, cycle_dv
        )
        grad_keys, grad_values = (
            passed_along(cycle_dk.astype(jnp.bfloat16), "ctx", 1).astype(cycle_dk.dtype),
            passed_along(cycle_dv.astype(jnp.bfloat16), "ctx", 1).astype(cycle_dv.dtype),
        )
        grad_query_pre = unrotate(head_view(grad_query, head_count), cosine, sine_table).reshape(
            block_rows, model_width
        )
        grad_keys_pre = unrotate(head_view(grad_keys, head_count), cosine, sine_table).reshape(
            block_rows, model_width
        )
        grad_proj_b = jnp.concatenate([grad_query_pre, grad_keys_pre, grad_values], axis=1).astype(
            jnp.bfloat16
        )
        grad_in_proj = jnp.einsum(
            "rd,rf->df", normed_in_b, grad_proj_b, preferred_element_type=jnp.float32
        )
        grad_norm_in = jnp.einsum(
            "rf,df->rd", grad_proj_b, full_in, preferred_element_type=jnp.float32
        )
        grad_gain_one = jnp.sum(grad_norm_in * normed_one, axis=0)
        grad_bias_one = jnp.sum(grad_norm_in, axis=0)
        grad_block_in = grad_middle + norm_back(grad_norm_in, normed_one, inv_one, gain_one)
        grad_in_list.append(grad_block_in.astype(jnp.bfloat16))
        norm_grads = jnp.stack([grad_gain_one, grad_bias_one, grad_gain_two, grad_bias_two])
        mix_tiled = jnp.broadcast_to(mix_grad[None, :], (lax.axis_size("fsdp"), stream_count + 1))
        grad_terms = (grad_in_proj, grad_out_proj, grad_up, grad_down, norm_grads, mix_tiled)
        shares = (
            lax.psum_scatter(
                grad_terms[0].astype(jnp.bfloat16), "fsdp", scatter_dimension=0, tiled=True
            ).astype(jnp.float32),
            lax.psum_scatter(
                grad_terms[1].astype(jnp.bfloat16), "fsdp", scatter_dimension=0, tiled=True
            ).astype(jnp.float32),
            lax.psum_scatter(
                grad_terms[2].astype(jnp.bfloat16), "fsdp", scatter_dimension=0, tiled=True
            ).astype(jnp.float32),
            lax.psum_scatter(
                grad_terms[3].astype(jnp.bfloat16), "fsdp", scatter_dimension=0, tiled=True
            ).astype(jnp.float32),
            lax.psum_scatter(
                grad_terms[4].astype(jnp.bfloat16), "fsdp", scatter_dimension=1, tiled=True
            ).astype(jnp.float32),
            lax.psum_scatter(
                grad_terms[5].astype(jnp.bfloat16), "fsdp", scatter_dimension=0, tiled=True
            ).astype(jnp.float32),
        )
        totals = (
            shares
            if totals is None
            else tuple((first + second for first, second in zip(totals, shares)))
        )
    totals = lax.psum(totals, "ctx")
    norm_total = totals[4]
    return (
        jnp.stack(next_list),
        jnp.stack(grad_in_list),
        jnp.stack(earlier_list, axis=1),
        totals[0],
        totals[1],
        totals[2],
        totals[3],
        norm_total[0],
        norm_total[1],
        norm_total[2],
        norm_total[3],
        totals[5].reshape(-1),
    )


F32 = jnp.float32
BF16 = jnp.bfloat16
LOG2E = math.log2(math.e)
GELU_C = math.sqrt(2.0 / math.pi)
GELU_A = 0.044715
ANY = pl.ANY
VMEM = pltpu.VMEM
SMEM = pltpu.SMEM
MIB = 1 << 20


def mm(left, right, left_dim, right_dim):
    return lax.dot_general(
        left, right, (((left_dim,), (right_dim,)), ((), ())), preferred_element_type=F32
    )


def spec(space):
    return pl.BlockSpec(memory_space=space)


def shape_of(dims, kind):
    return jax.ShapeDtypeStruct(dims, kind)


def run_kernel(kernel, name, operands, spaces, outs, scratch, flops, limit=56):
    moved = sum(o.size * o.dtype.itemsize for o in operands) + sum(
        math.prod(o.shape) * jnp.dtype(o.dtype).itemsize for o in outs
    )
    return pl.pallas_call(
        kernel,
        name=name,
        in_specs=[spec(s) for s in spaces],
        out_specs=[spec(VMEM) for _ in outs],
        out_shape=outs,
        scratch_shapes=scratch,
        compiler_params=pltpu.CompilerParams(vmem_limit_bytes=limit * MIB),
        cost_estimate=pl.CostEstimate(
            flops=int(flops), bytes_accessed=int(moved), transcendentals=0
        ),
    )(*operands)


def block_index(scalars, order):
    place = scalars[1]
    return lax.bitwise_xor(place, jnp.int32((0, 2, 1, 3)[order]))


def early_kernel(mix, earlier, grad, out_grad, out_prev, out_mix):
    streams = earlier.shape[0]
    rows = grad.shape[0]
    step = 128

    out_mix[...] = jnp.zeros_like(out_mix)

    def one(index, carry):
        here = pl.ds(pl.multiple_of(index * step, step), step)
        g = grad[here, :].astype(F32)
        total = None
        for k in range(streams):
            e = earlier[k, here, :].astype(F32)
            out_grad[k, here, :] = (mix[k] * g).astype(BF16)
            out_mix[k : k + 1, :] += jnp.sum(e * g, axis=0, keepdims=True)
            total = mix[k] * e if total is None else total + mix[k] * e
        out_prev[here, :] = total
        return carry

    lax.fori_loop(0, rows // step, one, 0)


def qkv_kernel(hps, batches, has_x, *refs):
    if has_x:
        scalars, x, norms, cosine, sine, w0, w1, w2, w3 = refs[:9]
        outs = refs[9:-3]
        n1t, weight, pairs = refs[-3:]
        v = x[...].astype(F32)
        center = v - jnp.mean(v, axis=-1, keepdims=True)
        inv = lax.rsqrt(jnp.mean(center * center, axis=-1, keepdims=True) + 1e-05)
        n1 = center * inv * norms[0:1, :] + norms[1:2, :]
        n1t[...] = n1.astype(BF16).T
    else:
        scalars, n1t, cosine, sine, w0, w1, w2, w3 = refs[:8]
        outs = refs[8:-2]
        weight, pairs = refs[-2:]
    rows = w0.shape[0]
    for order, piece in enumerate((w0, w1, w2, w3)):
        start = pl.multiple_of(block_index(scalars, order) * rows, rows)
        weight[pl.ds(start, rows), :] = piece[...]
    width = weight.shape[1] // 3
    size = width // hps
    half = size // 2
    tokens = n1t.shape[1] // batches
    for part in range(3):
        cols = mm(weight[:, part * width : (part + 1) * width], n1t[...], 0, 0)
        for head in range(hps):
            for batch in range(batches):
                lanes = slice(batch * tokens, (batch + 1) * tokens)
                top = cols[head * size : head * size + half, lanes]
                low = cols[head * size + half : (head + 1) * size, lanes]
                if part < 2:
                    c = cosine[batch]
                    s = sine[batch]
                    top, low = top * c - low * s, low * c + top * s
                slot = batch * hps + head
                pairs[slot, part * size : part * size + half, :] = top.astype(BF16)
                pairs[slot, part * size + half : (part + 1) * size, :] = low.astype(BF16)
    for delta, out in enumerate(outs):
        out[...] = pairs[lax.bitwise_xor(scalars[0], jnp.int32(delta))]


def attend_kernel(count, scale, ids, *refs):
    ins = refs[:count]
    outs = refs[count : 2 * count]
    ot, lse, qt, kk, vt, scores, top, total, acc = refs[2 * count :]
    size = qt.shape[1]
    factor = scale * LOG2E
    for d in range(count):
        slot = ids[d]
        qt[slot] = ins[d][0:size, :]
        kk[slot] = ins[d][size : 2 * size, :].T
        vt[slot] = ins[d][2 * size :, :]
    acc[...] = jnp.zeros_like(acc)
    total[...] = jnp.zeros_like(total)
    top[...] = jnp.full_like(top, -1e30)
    scores[0] = mm(kk[0], qt[0], 1, 0) * factor

    def step(index, carry):
        i, j = carry
        last = j == i
        next_i = jnp.where(last, i + 1, i)
        next_j = jnp.where(last, 0, j + 1)
        ahead = jnp.minimum(next_i, count - 1)
        scores[(index + 1) % 2] = mm(kk[next_j], qt[ahead], 1, 0) * factor
        s = scores[index % 2]
        old = jnp.where(j == 0, -1e30, top[...])
        new = jnp.maximum(old, jnp.max(s, axis=0, keepdims=True))
        shrink = jnp.exp2(old - new)
        p = jnp.exp2(s - new)
        run = total[...] * shrink + jnp.sum(p, axis=0, keepdims=True)
        out = acc[...] * shrink + mm(vt[j], p.astype(BF16), 1, 0)
        top[...] = new
        total[...] = run
        acc[...] = out

        @pl.when(last)
        def _():
            ot[i] = out / run
            lse[i] = new + jnp.log2(run)

        return (next_i, next_j)

    lax.fori_loop(0, count * (count + 1) // 2, step, (jnp.int32(0), jnp.int32(0)))
    for d in range(count):
        outs[d][...] = ot[ids[d]].astype(BF16)


def attend_back_kernel(count, scale, ids, *refs):
    ins = refs[:count]
    grads = refs[count : 2 * count]
    ot, lse = refs[2 * count : 2 * count + 2]
    outs = refs[2 * count + 2 : 3 * count + 2]
    qt, qq, kt, kk, vv, gt, gg, delta, scores, gains, dq, dk, dv = refs[3 * count + 2 :]
    size = qt.shape[1]
    factor = scale * LOG2E
    for d in range(count):
        slot = ids[d]
        block = ins[d][...]
        q = block[0:size]
        k = block[size : 2 * size]
        qt[slot] = q
        kt[slot] = k
        qq[slot] = q.T
        kk[slot] = k.T
        vv[slot] = block[2 * size :].T
        g = grads[d][...]
        gt[slot] = g
        gg[slot] = g.T
        delta[slot] = jnp.sum(g.astype(F32) * ot[slot], axis=0, keepdims=True)
    dq[...] = jnp.zeros_like(dq)
    dk[...] = jnp.zeros_like(dk)
    dv[...] = jnp.zeros_like(dv)
    scores[0] = mm(kk[0], qt[0], 1, 0)
    gains[0] = mm(vv[0], gt[0], 1, 0)

    def step(index, carry):
        i, j = carry
        last = j == i
        next_i = jnp.where(last, i + 1, i)
        next_j = jnp.where(last, 0, j + 1)
        ahead = jnp.minimum(next_i, count - 1)
        later = (index + 1) % 2
        scores[later] = mm(kk[next_j], qt[ahead], 1, 0)
        gains[later] = mm(vv[next_j], gt[ahead], 1, 0)
        now = index % 2
        p = jnp.exp2(scores[now] * factor - lse[i])
        ds = (p * (gains[now] - delta[i])).astype(BF16)
        dq[i] += mm(kt[j], ds, 1, 0)
        dk[j] += mm(ds, qq[i], 1, 0)
        dv[j] += mm(p.astype(BF16), gg[i], 1, 0)
        return (next_i, next_j)

    lax.fori_loop(0, count * (count + 1) // 2, step, (jnp.int32(0), jnp.int32(0)))
    for d in range(count):
        slot = ids[d]
        outs[d][0:size, :] = (dq[slot] * scale).astype(BF16)
        outs[d][size : 2 * size, :] = (dk[slot] * scale).T.astype(BF16)
        outs[d][2 * size :, :] = dv[slot].T.astype(BF16)


def gather_rows(scalars, pieces, target, sems, base):
    copies = []
    rows = pieces[0].shape[0]
    for order, piece in enumerate(pieces):
        start = pl.multiple_of(block_index(scalars, order) * rows, rows)
        copy = pltpu.make_async_copy(piece, target.at[pl.ds(start, rows), :], sems.at[base + order])
        copy.start()
        copies.append(copy)
    return copies


def mlp_kernel(count, stages, hps, batches, scalars, mix, x, grad, norms, *refs):
    heads = refs[: count * stages]
    refs = refs[count * stages :]
    w_out, w_up, w_down = refs[0:4], refs[4:8], refs[8:12]
    hidden, dhidden, n2_out, mid_out, dmid_out, dmid_low, ot, norm_grads = refs[12:20]
    head_grads = refs[20 : 20 + count * stages]
    out_scr, up_scr, down_scr, dn2, got, sems = refs[20 + count * stages :]
    copies_out = gather_rows(scalars, w_out, out_scr, sems, 0)
    copies_up = gather_rows(scalars, w_up, up_scr, sems, 4)
    copies_down = gather_rows(scalars, w_down, down_scr, sems, 8)
    me = scalars[0]
    for stage in range(stages):
        for d in range(count):
            slot = lax.bitwise_xor(me, jnp.int32(d))
            batch = lax.div(slot, jnp.int32(hps))
            head = stage * hps + lax.rem(slot, jnp.int32(hps))
            ot[batch, head] = heads[stage * count + d][...]
    for copy in copies_out:
        copy.wait()
    tokens = x.shape[0] // batches
    width = x.shape[1]
    for batch in range(batches):
        rows = slice(batch * tokens, (batch + 1) * tokens)
        attended = ot[batch].reshape(width, tokens)
        middle = x[rows, :].astype(F32) + mm(attended, out_scr[...], 0, 0)
        mid_out[rows, :] = middle
        center = middle - jnp.mean(middle, axis=-1, keepdims=True)
        inv = lax.rsqrt(jnp.mean(center * center, axis=-1, keepdims=True) + 1e-05)
        n2_out[rows, :] = (center * inv * norms[2:3, :] + norms[3:4, :]).astype(BF16)
    for copy in copies_up + copies_down:
        copy.wait()
    dn2[...] = jnp.zeros_like(dn2)
    dy = (mix[mix.shape[0] - 1] * grad[...].astype(F32)).astype(BF16)
    step = 512 if up_scr.shape[1] % 512 == 0 else 128

    def one(index, carry):
        here = pl.ds(pl.multiple_of(index * step, step), step)
        up = up_scr[:, here]
        u = mm(n2_out[...], up, 1, 0)
        da = mm(dy, down_scr[here, :], 1, 1)
        square = u * u
        bend = jnp.tanh(u * (GELU_C + (GELU_C * GELU_A) * square))
        gate = 0.5 + 0.5 * bend
        hidden[:, here] = (u * gate).astype(BF16)
        slope = gate + (0.5 * u) * (1.0 - bend * bend) * (
            GELU_C + (3.0 * GELU_C * GELU_A) * square
        )
        du = (da * slope).astype(BF16)
        dhidden[:, here] = du
        dn2[...] += mm(du, up, 1, 1)
        return carry

    lax.fori_loop(0, up_scr.shape[1] // step, one, 0)
    gain_sum = None
    for batch in range(batches):
        rows = slice(batch * tokens, (batch + 1) * tokens)
        middle = mid_out[rows, :]
        center = middle - jnp.mean(middle, axis=-1, keepdims=True)
        inv = lax.rsqrt(jnp.mean(center * center, axis=-1, keepdims=True) + 1e-05)
        z = center * inv
        dn = dn2[rows, :]
        part_gain = jnp.sum(dn * z, axis=0, keepdims=True)
        part_bias = jnp.sum(dn, axis=0, keepdims=True)
        gain_sum = part_gain if gain_sum is None else gain_sum + part_gain
        bias_sum = part_bias if batch == 0 else bias_sum + part_bias
        h = dn * norms[2:3, :]
        back = inv * (
            h - jnp.mean(h, axis=-1, keepdims=True) - z * jnp.mean(h * z, axis=-1, keepdims=True)
        )
        dmid = mix[mix.shape[0] - 1] * grad[rows, :].astype(F32) + back
        dmid_out[rows, :] = dmid
        low = dmid.astype(BF16)
        dmid_low[rows, :] = low
        got[batch] = mm(out_scr[...], low, 1, 1).astype(BF16).reshape(got.shape[1:])
    norm_grads[...] = jnp.zeros_like(norm_grads)
    norm_grads[0:1, :] = gain_sum
    norm_grads[1:2, :] = bias_sum
    for stage in range(stages):
        for d in range(count):
            slot = lax.bitwise_xor(me, jnp.int32(d))
            batch = lax.div(slot, jnp.int32(hps))
            head = stage * hps + lax.rem(slot, jnp.int32(hps))
            head_grads[stage * count + d][...] = got[batch, head]


def result_kernel(scalars, mix, hidden, mid, prev, grad, w0, w1, w2, w3, out, out_mix, acc):
    acc[...] = mid[...]
    rows = w0.shape[0]
    for order, piece in enumerate((w0, w1, w2, w3)):
        start = pl.multiple_of(block_index(scalars, order) * rows, rows)
        acc[...] += mm(hidden[:, pl.ds(start, rows)], piece[...], 1, 0)
    y = acc[...]
    out[...] = (prev[...] + mix[mix.shape[0] - 1] * y).astype(BF16)
    out_mix[...] = jnp.zeros_like(out_mix)
    out_mix[0:1, :] = jnp.sum(grad[...].astype(F32) * y, axis=0, keepdims=True)


def put_pieces(me, value, outs, order, count, lanes):
    keep, send = outs
    target = (keep, keep, send, send)[order]
    rows = value.shape[0] // count
    low = value.astype(BF16)
    for sub in range(count):
        slot = lax.bitwise_xor(me, jnp.int32(sub))
        target[order % 2, slot, :, lanes] = low[sub * rows : (sub + 1) * rows, :]


def down_grad_kernel(count, scalars, mix, hidden, grad, keep, send):
    dy = (mix[mix.shape[0] - 1] * grad[...].astype(F32)).astype(BF16)
    rows = keep.shape[1] * keep.shape[2]
    for order in range(4):
        start = pl.multiple_of(block_index(scalars, order) * rows, rows)
        value = mm(hidden[:, pl.ds(start, rows)], dy, 0, 0)
        put_pieces(scalars[0], value, (keep, send), order, count, slice(None))


def up_out_grad_kernel(count, scalars, n2, dhidden, ot, dmid, keep, send, left, left_out):
    batches = ot.shape[0]
    width = n2.shape[1]
    tokens = ot.shape[3]
    rows = width // 4
    flipped = n2[...].T
    for order in range(4):
        here = pl.ds(pl.multiple_of(block_index(scalars, order) * rows, rows), rows)
        left_out[order * rows : (order + 1) * rows, :] = jnp.zeros(
            (rows, left_out.shape[1]), BF16
        )
    left_out[...] = flipped
    for order in range(4):
        here = pl.ds(pl.multiple_of(block_index(scalars, order) * rows, rows), rows)
        left[order * rows : (order + 1) * rows, :] = left_out[here, :]
    inner = dhidden.shape[1]
    step = 768 if inner % 768 == 0 else 256

    def one(index, carry):
        start = pl.multiple_of(index * step, step)
        value = mm(left[...], dhidden[:, pl.ds(start, step)], 1, 0)
        for order in range(4):
            put_pieces(
                scalars[0],
                value[order * rows : (order + 1) * rows, :],
                (keep, send),
                order,
                count,
                pl.ds(start, step),
            )
        return carry

    lax.fori_loop(0, inner // step, one, 0)
    for batch in range(batches):
        left_out[:, batch * tokens : (batch + 1) * tokens] = ot[batch].reshape(width, tokens)
    for order in range(4):
        here = pl.ds(pl.multiple_of(block_index(scalars, order) * rows, rows), rows)
        left[order * rows : (order + 1) * rows, :] = left_out[here, :]
    value = mm(left[...], dmid[...], 1, 0)
    for order in range(4):
        put_pieces(
            scalars[0],
            value[order * rows : (order + 1) * rows, :],
            (keep, send),
            order,
            count,
            slice(inner, inner + value.shape[1]),
        )


def in_grad_kernel(count, hps, scalars, cosine, sine, n1t, *refs):
    grads = refs[:count]
    dt, keep, send, left = refs[count:]
    batches = dt.shape[0]
    size = dt.shape[3]
    half = size // 2
    tokens = dt.shape[4]
    me = scalars[0]
    for d in range(count):
        slot = lax.bitwise_xor(me, jnp.int32(d))
        batch = lax.div(slot, jnp.int32(hps))
        head = lax.rem(slot, jnp.int32(hps))
        c = cosine[batch]
        s = sine[batch]
        for part in range(2):
            top = grads[d][part * size : part * size + half, :].astype(F32)
            low = grads[d][part * size + half : (part + 1) * size, :].astype(F32)
            dt[batch, part, head, 0:half, :] = (top * c + low * s).astype(BF16)
            dt[batch, part, head, half:size, :] = (low * c - top * s).astype(BF16)
        dt[batch, 2, head] = grads[d][2 * size :, :]
    width = n1t.shape[0]
    rows = width // 4
    for order in range(4):
        here = pl.ds(pl.multiple_of(block_index(scalars, order) * rows, rows), rows)
        left[order * rows : (order + 1) * rows, :] = n1t[here, :]
    cols = 3 * hps * size
    value = None
    for batch in range(batches):
        term = mm(
            left[:, batch * tokens : (batch + 1) * tokens], dt[batch].reshape(cols, tokens), 1, 1
        )
        value = term if value is None else value + term
    for order in range(4):
        put_pieces(
            me, value[order * rows : (order + 1) * rows, :], (keep, send), order, count, slice(None)
        )


def input_grad_kernel(stages, scalars, x, norms, dmid, *refs):
    dts = refs[:stages]
    pieces = refs[stages : stages + 4 * stages]
    out, norm_grads, weights, sems = refs[5 * stages :]
    copies = []
    for stage in range(stages):
        copies.append(
            gather_rows(
                scalars,
                pieces[4 * stage : 4 * stage + 4],
                weights.at[stage],
                sems,
                4 * stage,
            )
        )
    for group in copies:
        for copy in group:
            copy.wait()
    batches = dts[0].shape[0]
    tokens = dts[0].shape[4]
    cols = weights.shape[2]
    gain_sum = bias_sum = None
    for batch in range(batches):
        rows = slice(batch * tokens, (batch + 1) * tokens)
        dnt = None
        for stage in range(stages):
            term = mm(weights[stage], dts[stage][batch].reshape(cols, tokens), 1, 0)
            dnt = term if dnt is None else dnt + term
        dn = dnt.T
        v = x[rows, :].astype(F32)
        center = v - jnp.mean(v, axis=-1, keepdims=True)
        inv = lax.rsqrt(jnp.mean(center * center, axis=-1, keepdims=True) + 1e-05)
        z = center * inv
        part_gain = jnp.sum(dn * z, axis=0, keepdims=True)
        part_bias = jnp.sum(dn, axis=0, keepdims=True)
        gain_sum = part_gain if batch == 0 else gain_sum + part_gain
        bias_sum = part_bias if batch == 0 else bias_sum + part_bias
        h = dn * norms[0:1, :]
        back = inv * (
            h - jnp.mean(h, axis=-1, keepdims=True) - z * jnp.mean(h * z, axis=-1, keepdims=True)
        )
        out[rows, :] = (dmid[rows, :] + back).astype(BF16)
    norm_grads[...] = jnp.zeros_like(norm_grads)
    norm_grads[0:1, :] = gain_sum
    norm_grads[1:2, :] = bias_sum


def place_kernel(count, groups, scalars, *refs):
    pieces = refs[: count * len(groups)]
    outs = refs[count * len(groups) :]
    for g, moves in enumerate(groups):
        for d in range(count):
            slot = lax.bitwise_xor(scalars[0], jnp.int32(d))
            piece = pieces[g * count + d]
            for out, begin, wide, to in moves:
                outs[out][slot, :, to : to + wide] = piece[:, begin : begin + wide].astype(F32)


def exchange(value, axis, bit):
    size = lax.axis_size(axis)
    return lax.ppermute(value, axis, [(i, i ^ bit) for i in range(size)])


def added(left, right):
    return (left.astype(F32) + right.astype(F32)).astype(BF16)


def reduce_blocks(keep, send):
    got = exchange(send, "fsdp", 1)
    passed = added(keep[1], got[1])
    own = added(keep[0], got[0])
    own = added(own, exchange(passed, "fsdp", 2))
    bit = 1
    while bit < lax.axis_size("ctx"):
        pairs = own.reshape(own.shape[0] // 2, 2, *own.shape[1:])
        own = added(pairs[:, 0], exchange(pairs[:, 1], "ctx", bit))
        bit *= 2
    return own[0]


def gather_blocks(own):
    count = lax.axis_size("ctx")
    held = {0: own}
    bit = count // 2
    while bit:
        for index in list(held):
            held[index ^ bit] = exchange(held[index], "ctx", bit)
        bit //= 2
    return [held[index] for index in range(count)]


def gathered(shard):
    other_chip = exchange(shard, "fsdp", 2)
    return [shard, other_chip, exchange(shard, "fsdp", 1), exchange(other_chip, "fsdp", 1)]


def head_body(
    inputs,
    earlier,
    input_proj,
    output_proj,
    up_proj,
    down_proj,
    norm1_gain,
    norm1_bias,
    norm2_gain,
    norm2_bias,
    mixing,
    block_order,
    grad_next,
):
    batches, tokens, width = inputs.shape
    rows = batches * tokens
    heads = HEADS
    size = width // heads
    scale = size ** (-0.5)
    streams = earlier.shape[0]
    count = lax.axis_size("ctx")
    hps = count // batches
    stages = heads // hps
    inner = down_proj.shape[0] * 4
    me = lax.axis_index("ctx").astype(jnp.int32)
    place = lax.axis_index("fsdp").astype(jnp.int32)
    scalars = jnp.stack([me, place])
    own_batch = me // hps
    ids = block_order[own_batch][me ^ jnp.arange(count, dtype=jnp.int32)].astype(jnp.int32)
    x = inputs.reshape(rows, width)
    grad = grad_next.reshape(rows, width)

    norm_stack = jnp.stack([norm1_gain, norm1_bias, norm2_gain, norm2_bias])
    norms = lax.all_gather(norm_stack, "fsdp", axis=1, tiled=True)
    chunks = input_proj.reshape(width // 4, 3, stages, hps * size)
    w_in = [gathered(chunks[:, :, s].reshape(width // 4, 3 * hps * size)) for s in range(stages)]
    w_out = gathered(output_proj)
    w_up = gathered(up_proj)
    w_down = gathered(down_proj)

    half = size // 2
    own_blocks = block_order[:, me]
    positions = (own_blocks[:, None] * tokens + lax.iota(jnp.int32, tokens)[None]).astype(F32)
    freqs = jnp.exp(lax.iota(F32, half) * (-2.0 * math.log(10000.0) / size))
    angle = freqs[None, :, None] * positions[:, None, :]
    cosine = jnp.cos(angle)
    sine = jnp.sin(angle)

    grad_earlier, prev, mix_early = run_kernel(
        early_kernel,
        "early",
        [mixing, earlier.reshape(streams, rows, width), grad],
        [SMEM, VMEM, VMEM],
        [
            shape_of((streams, rows, width), BF16),
            shape_of((rows, width), F32),
            shape_of((8, width), F32),
        ],
        [],
        6 * streams * rows * width,
    )

    pair_shape = shape_of((3 * size, tokens), BF16)
    held = []
    n1t = None
    for s in range(stages):
        first = s == 0
        operands = [scalars] + ([x, norms] if first else [n1t]) + [cosine, sine] + w_in[s]
        outs = [pair_shape] * count + ([shape_of((width, rows), BF16)] if first else [])
        result = run_kernel(
            functools.partial(qkv_kernel, hps, batches, first),
            "qkv",
            operands,
            [SMEM] + [VMEM] * (len(operands) - 1),
            outs,
            [
                pltpu.VMEM((width, 3 * hps * size), BF16),
                pltpu.VMEM((count, 3 * size, tokens), BF16),
            ],
            2 * rows * width * 3 * hps * size,
        )
        if first:
            n1t = result[count]
        sent = result[:count]
        held.append([sent[0]] + [exchange(sent[d], "ctx", d) for d in range(1, count)])

    tiles = count * (count + 1) // 2
    one = tokens * tokens * size * 2
    head_shape = shape_of((size, tokens), BF16)
    attended = []
    saved = []
    for s in range(stages):
        result = run_kernel(
            functools.partial(attend_kernel, count, scale),
            "attend",
            [ids] + held[s],
            [SMEM] + [VMEM] * count,
            [head_shape] * count
            + [shape_of((count, size, tokens), F32), shape_of((count, 1, tokens), F32)],
            [
                pltpu.VMEM((count, size, tokens), BF16),
                pltpu.VMEM((count, tokens, size), BF16),
                pltpu.VMEM((count, size, tokens), BF16),
                pltpu.VMEM((2, tokens, tokens), F32),
                pltpu.VMEM((1, tokens), F32),
                pltpu.VMEM((1, tokens), F32),
                pltpu.VMEM((size, tokens), F32),
            ],
            4 * 2 * one * tiles,
        )
        saved.append(result[count:])
        attended += [result[0]] + [exchange(result[d], "ctx", d) for d in range(1, count)]

    mlp_operands = [scalars, mixing, x, grad, norms] + attended + w_out + w_up + w_down
    result = run_kernel(
        functools.partial(mlp_kernel, count, stages, hps, batches),
        "mlp",
        mlp_operands,
        [SMEM, SMEM, VMEM, VMEM, VMEM] + [VMEM] * (count * stages) + [ANY] * 12,
        [
            shape_of((rows, inner), BF16),
            shape_of((rows, inner), BF16),
            shape_of((rows, width), BF16),
            shape_of((rows, width), F32),
            shape_of((rows, width), F32),
            shape_of((rows, width), BF16),
            shape_of((batches, heads, size, tokens), BF16),
            shape_of((8, width), F32),
        ]
        + [head_shape] * (count * stages),
        [
            pltpu.VMEM((width, width), BF16),
            pltpu.VMEM((width, inner), BF16),
            pltpu.VMEM((inner, width), BF16),
            pltpu.VMEM((rows, width), F32),
            pltpu.VMEM((batches, heads, size, tokens), BF16),
            pltpu.SemaphoreType.DMA((12,)),
        ],
        6 * rows * width * inner,
    )
    hidden, dhidden, n2, mid, dmid, dmid_low, ot, norm2_grads = result[:8]
    head_grads = result[8:]
    sent_grads = []
    for s in range(stages):
        mine = head_grads[s * count : (s + 1) * count]
        sent_grads.append([mine[0]] + [exchange(mine[d], "ctx", d) for d in range(1, count)])

    sub = inner // 4 // count
    down_keep, down_send = run_kernel(
        functools.partial(down_grad_kernel, count),
        "down_grad",
        [scalars, mixing, hidden, grad],
        [SMEM, SMEM, VMEM, VMEM],
        [shape_of((2, count, sub, width), BF16)] * 2,
        [],
        2 * rows * width * inner,
    )
    down_pieces = gather_blocks(reduce_blocks(down_keep, down_send))
    thin = width // 4 // count
    up_keep, up_send = run_kernel(
        functools.partial(up_out_grad_kernel, count),
        "up_out_grad",
        [scalars, n2, dhidden, ot, dmid_low],
        [SMEM] + [VMEM] * 4,
        [shape_of((2, count, thin, inner + width), BF16)] * 2,
        [pltpu.VMEM((width, rows), BF16), pltpu.VMEM((width, rows), BF16)],
        2 * rows * width * (inner + width),
    )
    up_pieces = gather_blocks(reduce_blocks(up_keep, up_send))

    next_input, mix_last = run_kernel(
        result_kernel,
        "result",
        [scalars, mixing, hidden, mid, prev, grad] + w_down,
        [SMEM, SMEM] + [VMEM] * 8,
        [shape_of((rows, width), BF16), shape_of((8, width), F32)],
        [pltpu.VMEM((rows, width), F32)],
        2 * rows * width * inner,
    )

    dts = []
    in_pieces = []
    cols = 3 * hps * size
    for s in range(stages):
        back = run_kernel(
            functools.partial(attend_back_kernel, count, scale),
            "attend_back",
            [ids] + held[s] + sent_grads[s] + list(saved[s]),
            [SMEM] + [VMEM] * (2 * count + 2),
            [pair_shape] * count,
            [
                pltpu.VMEM((count, size, tokens), BF16),
                pltpu.VMEM((count, tokens, size), BF16),
                pltpu.VMEM((count, size, tokens), BF16),
                pltpu.VMEM((count, tokens, size), BF16),
                pltpu.VMEM((count, tokens, size), BF16),
                pltpu.VMEM((count, size, tokens), BF16),
                pltpu.VMEM((count, tokens, size), BF16),
                pltpu.VMEM((count, 1, tokens), F32),
                pltpu.VMEM((2, tokens, tokens), F32),
                pltpu.VMEM((2, tokens, tokens), F32),
                pltpu.VMEM((count, size, tokens), F32),
                pltpu.VMEM((count, tokens, size), F32),
                pltpu.VMEM((count, tokens, size), F32),
            ],
            4 * 5 * one * tiles,
        )
        arrived = [back[0]] + [exchange(back[d], "ctx", d) for d in range(1, count)]
        dt, keep, send = run_kernel(
            functools.partial(in_grad_kernel, count, hps),
            "in_grad",
            [scalars, cosine, sine, n1t] + arrived,
            [SMEM] + [VMEM] * (3 + count),
            [shape_of((batches, 3, hps, size, tokens), BF16)]
            + [shape_of((2, count, thin, cols), BF16)] * 2,
            [pltpu.VMEM((width, rows), BF16)],
            2 * rows * width * cols,
        )
        dts.append(dt)
        in_pieces += gather_blocks(reduce_blocks(keep, send))

    flat_in = [piece for pieces in w_in for piece in pieces]
    grad_input, norm1_grads = run_kernel(
        functools.partial(input_grad_kernel, stages),
        "input_grad",
        [scalars, x, norms, dmid] + dts + flat_in,
        [SMEM] + [VMEM] * (3 + stages) + [ANY] * (4 * stages),
        [shape_of((rows, width), BF16), shape_of((8, width), F32)],
        [pltpu.VMEM((stages, width, cols), BF16), pltpu.SemaphoreType.DMA((4 * stages,))],
        2 * rows * width * 3 * width,
    )

    small = jnp.concatenate(
        [norm1_grads[:2], norm2_grads[:2], mix_early[:streams], mix_last[:1]], axis=0
    )
    for axis in ("fsdp", "ctx"):
        bit = 1
        while bit < lax.axis_size(axis):
            small = small + exchange(small, axis, bit)
            bit *= 2
    norm_total = lax.dynamic_slice_in_dim(small[:4], place * (width // 4), width // 4, 1)
    mix_total = jnp.sum(small[4:], axis=1)

    (grad_down,) = run_kernel(
        functools.partial(place_kernel, count, (((0, 0, width, 0),),)),
        "place_down",
        [scalars] + down_pieces,
        [SMEM] + [VMEM] * count,
        [shape_of((count, sub, width), F32)],
        [],
        0,
    )
    grad_up, grad_out = run_kernel(
        functools.partial(place_kernel, count, (((0, 0, inner, 0), (1, inner, width, 0)),)),
        "place_up",
        [scalars] + up_pieces,
        [SMEM] + [VMEM] * count,
        [shape_of((count, thin, inner), F32), shape_of((count, thin, width), F32)],
        [],
        0,
    )
    wide = hps * size
    groups = tuple(
        tuple((0, part * wide, wide, part * width + s * wide) for part in range(3))
        for s in range(stages)
    )
    (grad_in,) = run_kernel(
        functools.partial(place_kernel, count, groups),
        "place_in",
        [scalars] + in_pieces,
        [SMEM] + [VMEM] * (count * stages),
        [shape_of((count, thin, 3 * width), F32)],
        [],
        0,
    )
    return (
        next_input.reshape(batches, tokens, width),
        grad_input.reshape(batches, tokens, width),
        grad_earlier.reshape(streams, batches, tokens, width),
        grad_in.reshape(width // 4, 3 * width),
        grad_out.reshape(width // 4, width),
        grad_up.reshape(width // 4, inner),
        grad_down.reshape(inner // 4, width),
        norm_total[0],
        norm_total[1],
        norm_total[2],
        norm_total[3],
        mix_total,
    )


def heads_fit(batches):
    count = lax.axis_size("ctx")
    return (
        lax.axis_size("fsdp") == 4
        and count & (count - 1) == 0
        and count % batches == 0
        and HEADS % max(count // batches, 1) == 0
    )


def either_body(inputs, *rest):
    return (head_body if heads_fit(inputs.shape[0]) else body)(inputs, *rest)


def solution(mesh):
    placed = (
        P("fsdp", "ctx", None),
        P(None, "fsdp", "ctx", None),
        P("fsdp", None),
        P("fsdp", None),
        P("fsdp", None),
        P("fsdp", None),
        P("fsdp"),
        P("fsdp"),
        P("fsdp"),
        P("fsdp"),
        P(),
        P(),
        P("fsdp", "ctx", None),
    )
    return jax.shard_map(
        either_body,
        mesh=mesh,
        in_specs=placed,
        out_specs=(
            P("fsdp", "ctx", None),
            P("fsdp", "ctx", None),
            P(None, "fsdp", "ctx", None),
            P("fsdp", None),
            P("fsdp", None),
            P("fsdp", None),
            P("fsdp", None),
            P("fsdp"),
            P("fsdp"),
            P("fsdp"),
            P("fsdp"),
            P(),
        ),
        check_vma=False,
    )
```

```python
import functools
import math

import jax
import jax.numpy as jnp
from jax import lax
from jax.experimental import pallas as pl
from jax.experimental.pallas import tpu as pltpu
from jax.sharding import PartitionSpec as P

HEADS = 12


def passed_along(value, axis, steps):
    count = lax.axis_size(axis)
    pairs = [(source, (source + steps) % count) for source in range(count)]
    return lax.ppermute(value, axis, pairs)


def norm_parts(values, gain, bias):
    mean_value = jnp.mean(values, axis=-1, keepdims=True)
    centered = values - mean_value
    inv_std = lax.rsqrt(jnp.mean(centered * centered, axis=-1, keepdims=True) + 1e-05)
    normed = centered * inv_std
    return (normed * gain + bias, normed, inv_std)


def norm_back(grad_out, normed, inv_std, gain):
    scaled = grad_out * gain
    mean_one = jnp.mean(scaled, axis=-1, keepdims=True)
    mean_two = jnp.mean(scaled * normed, axis=-1, keepdims=True)
    return inv_std * (scaled - mean_one - normed * mean_two)


def rotary_tables(block_id, block_rows, head_dim):
    half_dim = head_dim // 2
    positions = (block_id * block_rows + lax.iota(jnp.int32, block_rows)).astype(jnp.float32)
    freqs = jnp.exp(lax.iota(jnp.float32, half_dim) * (-2.0 * math.log(10000.0) / head_dim))
    angle = positions[:, None] * freqs[None, :]
    return (jnp.cos(angle)[:, None, :], jnp.sin(angle)[:, None, :])


def rotate(values, cosine, sine_table):
    half_dim = values.shape[-1] // 2
    first_half = values[..., :half_dim]
    second_half = values[..., half_dim:]
    return jnp.concatenate(
        [
            first_half * cosine - second_half * sine_table,
            second_half * cosine + first_half * sine_table,
        ],
        axis=-1,
    )


def unrotate(grads, cosine, sine_table):
    half_dim = grads.shape[-1] // 2
    first_half = grads[..., :half_dim]
    second_half = grads[..., half_dim:]
    return jnp.concatenate(
        [
            first_half * cosine + second_half * sine_table,
            second_half * cosine - first_half * sine_table,
        ],
        axis=-1,
    )


def head_view(values, head_count):
    return values.reshape(values.shape[0], head_count, values.shape[1] // head_count)


def forward_visit(state, local_query, block_keys, block_values, head_count, score_scale):
    run_max, run_sum, accum = state
    query_heads = head_view(local_query, head_count)
    key_heads = head_view(block_keys, head_count)
    value_heads = head_view(block_values, head_count)
    scores = (
        jnp.einsum("qhe,khe->hqk", query_heads, key_heads, preferred_element_type=jnp.float32)
        * score_scale
    )
    new_max = jnp.maximum(run_max, jnp.max(scores, axis=-1))
    weights = jnp.exp(scores - new_max[:, :, None])
    factor = jnp.exp(run_max - new_max)
    new_sum = run_sum * factor + jnp.sum(weights, axis=-1)
    update = jnp.einsum(
        "hqk,khe->qhe",
        weights.astype(jnp.bfloat16),
        value_heads,
        preferred_element_type=jnp.float32,
    )
    return (new_max, new_sum, accum * jnp.transpose(factor)[:, :, None] + update)


def backward_pair(
    query_rows, key_rows, value_rows, grad_rows, log_total, row_delta, head_count, score_scale
):
    query_heads = head_view(query_rows, head_count)
    key_heads = head_view(key_rows, head_count)
    value_heads = head_view(value_rows, head_count)
    grad_heads = head_view(grad_rows, head_count)
    scores = (
        jnp.einsum("qhe,khe->hqk", query_heads, key_heads, preferred_element_type=jnp.float32)
        * score_scale
    )
    probs = jnp.exp(scores - log_total[:, :, None])
    grad_probs = jnp.einsum(
        "qhe,khe->hqk", grad_heads, value_heads, preferred_element_type=jnp.float32
    )
    grad_scores = (probs * (grad_probs - row_delta[:, :, None])).astype(jnp.bfloat16)
    grad_query = (
        jnp.einsum("hqk,khe->qhe", grad_scores, key_heads, preferred_element_type=jnp.float32)
        * score_scale
    )
    grad_keys = (
        jnp.einsum("hqk,qhe->khe", grad_scores, query_heads, preferred_element_type=jnp.float32)
        * score_scale
    )
    grad_values = jnp.einsum(
        "hqk,qhe->khe", probs.astype(jnp.bfloat16), grad_heads, preferred_element_type=jnp.float32
    )
    return (
        grad_query.reshape(query_rows.shape[0], -1),
        grad_keys.reshape(key_rows.shape[0], -1),
        grad_values.reshape(key_rows.shape[0], -1),
    )


def body(
    inputs,
    earlier,
    input_proj,
    output_proj,
    up_proj,
    down_proj,
    norm1_gain,
    norm1_bias,
    norm2_gain,
    norm2_bias,
    mixing,
    block_order,
    grad_next,
):
    head_count = HEADS
    batch_count = inputs.shape[0]
    block_rows = inputs.shape[1]
    model_width = inputs.shape[2]
    head_dim = model_width // head_count
    score_scale = head_dim ** (-0.5)
    stream_count = earlier.shape[0]
    cycle_size = lax.axis_size("ctx")
    cycle_place = lax.axis_index("ctx")
    norm_stack = jnp.stack([norm1_gain, norm1_bias, norm2_gain, norm2_bias])
    full_in, full_out, full_up, full_down, full_norms = (
        lax.all_gather(input_proj, "fsdp", axis=0, tiled=True),
        lax.all_gather(output_proj, "fsdp", axis=0, tiled=True),
        lax.all_gather(up_proj, "fsdp", axis=0, tiled=True),
        lax.all_gather(down_proj, "fsdp", axis=0, tiled=True),
        lax.all_gather(norm_stack.astype(jnp.bfloat16), "fsdp", axis=1, tiled=True).astype(
            norm_stack.dtype
        ),
    )
    gain_one = full_norms[0]
    bias_one = full_norms[1]
    gain_two = full_norms[2]
    bias_two = full_norms[3]
    next_list = []
    grad_in_list = []
    earlier_list = []
    totals = None
    for batch in range(batch_count):
        block_input = inputs[batch].astype(jnp.float32)
        order_row = block_order[batch]
        own_block = order_row[cycle_place]
        cosine, sine_table = rotary_tables(own_block, block_rows, head_dim)
        normed_in, normed_one, inv_one = norm_parts(block_input, gain_one, bias_one)
        normed_in_b = normed_in.astype(jnp.bfloat16)
        projected = jnp.dot(normed_in_b, full_in, preferred_element_type=jnp.float32)
        local_query = (
            rotate(head_view(projected[:, :model_width], head_count), cosine, sine_table)
            .reshape(block_rows, model_width)
            .astype(jnp.bfloat16)
        )
        local_keys = (
            rotate(
                head_view(projected[:, model_width : 2 * model_width], head_count),
                cosine,
                sine_table,
            )
            .reshape(block_rows, model_width)
            .astype(jnp.bfloat16)
        )
        local_values = projected[:, 2 * model_width :].astype(jnp.bfloat16)
        start_state = (
            jnp.full((head_count, block_rows), -1e30, jnp.float32),
            jnp.zeros((head_count, block_rows), jnp.float32),
            jnp.zeros((block_rows, head_count, head_dim), jnp.float32),
        )
        piece_keys = lax.all_gather(local_keys, "ctx", axis=0, tiled=True)
        piece_values = lax.all_gather(local_values, "ctx", axis=0, tiled=True)
        count = piece_keys.shape[0] // block_rows

        def one_block(index, state_now):
            block_keys = lax.dynamic_slice_in_dim(piece_keys, index * block_rows, block_rows, 0)
            block_values = lax.dynamic_slice_in_dim(piece_values, index * block_rows, block_rows, 0)
            return lax.cond(
                order_row[index] <= own_block,
                lambda held: forward_visit(
                    held, local_query, block_keys, block_values, head_count, score_scale
                ),
                lambda held: held,
                state_now,
            )

        run_max, run_sum, accum = lax.fori_loop(0, count, one_block, start_state)
        log_total = run_max + jnp.log(run_sum)
        attended = accum / jnp.transpose(run_sum)[:, :, None]
        attended_b = attended.reshape(block_rows, model_width).astype(jnp.bfloat16)
        middle = block_input + jnp.dot(attended_b, full_out, preferred_element_type=jnp.float32)
        normed_mid, normed_two, inv_two = norm_parts(middle, gain_two, bias_two)
        normed_mid_b = normed_mid.astype(jnp.bfloat16)
        hidden_pre = jnp.dot(normed_mid_b, full_up, preferred_element_type=jnp.float32)
        hidden_b = jax.nn.gelu(hidden_pre).astype(jnp.bfloat16)
        result = middle + jnp.dot(hidden_b, full_down, preferred_element_type=jnp.float32)
        previous = earlier[:, batch].astype(jnp.float32)
        mixed_out = (
            jnp.sum(mixing[:stream_count, None, None] * previous, axis=0)
            + mixing[stream_count] * result
        )
        next_list.append(mixed_out.astype(jnp.bfloat16))
        grad_out = grad_next[batch].astype(jnp.float32)
        earlier_list.append(
            (mixing[:stream_count, None, None] * grad_out[None]).astype(jnp.bfloat16)
        )
        mix_grad = jnp.concatenate(
            [jnp.sum(previous * grad_out[None], axis=(1, 2)), jnp.sum(result * grad_out)[None]]
        )
        grad_result = mixing[stream_count] * grad_out
        grad_result_b = grad_result.astype(jnp.bfloat16)
        grad_down = jnp.einsum(
            "rf,rd->fd", hidden_b, grad_result_b, preferred_element_type=jnp.float32
        )
        grad_hidden = jnp.einsum(
            "rd,fd->rf", grad_result_b, full_down, preferred_element_type=jnp.float32
        )
        grad_pre = jax.vjp(jax.nn.gelu, hidden_pre)[1](grad_hidden)[0]
        grad_pre_b = grad_pre.astype(jnp.bfloat16)
        grad_up = jnp.einsum(
            "rd,rf->df", normed_mid_b, grad_pre_b, preferred_element_type=jnp.float32
        )
        grad_norm_mid = jnp.einsum(
            "rf,df->rd", grad_pre_b, full_up, preferred_element_type=jnp.float32
        )
        grad_gain_two = jnp.sum(grad_norm_mid * normed_two, axis=0)
        grad_bias_two = jnp.sum(grad_norm_mid, axis=0)
        grad_middle = grad_result + norm_back(grad_norm_mid, normed_two, inv_two, gain_two)
        grad_middle_b = grad_middle.astype(jnp.bfloat16)
        grad_out_proj = jnp.einsum(
            "rd,re->de", attended_b, grad_middle_b, preferred_element_type=jnp.float32
        )
        grad_att_b = jnp.einsum(
            "re,de->rd", grad_middle_b, full_out, preferred_element_type=jnp.float32
        ).astype(jnp.bfloat16)
        row_delta = jnp.einsum(
            "qhe,qhe->hq", head_view(grad_att_b, head_count).astype(jnp.float32), attended
        )
        zero_rows = jnp.zeros((block_rows, model_width), jnp.float32)

        def key_visit(offset, grad_query, cycle_keys, cycle_values, cycle_dk, cycle_dv):
            their_block = order_row[(cycle_place - offset) % cycle_size]

            def add_pair(held):
                part_q, part_k, part_v = backward_pair(
                    local_query,
                    cycle_keys,
                    cycle_values,
                    grad_att_b,
                    log_total,
                    row_delta,
                    head_count,
                    score_scale,
                )
                return (held[0] + part_q, held[1] + part_k, held[2] + part_v)

            return lax.cond(
                their_block <= own_block,
                add_pair,
                lambda held: held,
                (grad_query, cycle_dk, cycle_dv),
            )

        def key_turn(offset, carry):
            grad_query, cycle_keys, cycle_values, cycle_dk, cycle_dv = carry
            grad_query, cycle_dk, cycle_dv = key_visit(
                offset, grad_query, cycle_keys, cycle_values, cycle_dk, cycle_dv
            )
            cycle_keys, cycle_values = passed_along((cycle_keys, cycle_values), "ctx", 1)
            cycle_dk, cycle_dv = (
                passed_along(cycle_dk.astype(jnp.bfloat16), "ctx", 1).astype(cycle_dk.dtype),
                passed_along(cycle_dv.astype(jnp.bfloat16), "ctx", 1).astype(cycle_dv.dtype),
            )
            return (grad_query, cycle_keys, cycle_values, cycle_dk, cycle_dv)

        grad_query, cycle_keys, cycle_values, cycle_dk, cycle_dv = lax.fori_loop(
            0, cycle_size - 1, key_turn, (zero_rows, local_keys, local_values, zero_rows, zero_rows)
        )
        grad_query, cycle_dk, cycle_dv = key_visit(
            cycle_size - 1, grad_query, cycle_keys, cycle_values, cycle_dk, cycle_dv
        )
        grad_keys, grad_values = (
            passed_along(cycle_dk.astype(jnp.bfloat16), "ctx", 1).astype(cycle_dk.dtype),
            passed_along(cycle_dv.astype(jnp.bfloat16), "ctx", 1).astype(cycle_dv.dtype),
        )
        grad_query_pre = unrotate(head_view(grad_query, head_count), cosine, sine_table).reshape(
            block_rows, model_width
        )
        grad_keys_pre = unrotate(head_view(grad_keys, head_count), cosine, sine_table).reshape(
            block_rows, model_width
        )
        grad_proj_b = jnp.concatenate([grad_query_pre, grad_keys_pre, grad_values], axis=1).astype(
            jnp.bfloat16
        )
        grad_in_proj = jnp.einsum(
            "rd,rf->df", normed_in_b, grad_proj_b, preferred_element_type=jnp.float32
        )
        grad_norm_in = jnp.einsum(
            "rf,df->rd", grad_proj_b, full_in, preferred_element_type=jnp.float32
        )
        grad_gain_one = jnp.sum(grad_norm_in * normed_one, axis=0)
        grad_bias_one = jnp.sum(grad_norm_in, axis=0)
        grad_block_in = grad_middle + norm_back(grad_norm_in, normed_one, inv_one, gain_one)
        grad_in_list.append(grad_block_in.astype(jnp.bfloat16))
        norm_grads = jnp.stack([grad_gain_one, grad_bias_one, grad_gain_two, grad_bias_two])
        mix_tiled = jnp.broadcast_to(mix_grad[None, :], (lax.axis_size("fsdp"), stream_count + 1))
        grad_terms = (grad_in_proj, grad_out_proj, grad_up, grad_down, norm_grads, mix_tiled)
        shares = (
            lax.psum_scatter(
                grad_terms[0].astype(jnp.bfloat16), "fsdp", scatter_dimension=0, tiled=True
            ).astype(jnp.float32),
            lax.psum_scatter(
                grad_terms[1].astype(jnp.bfloat16), "fsdp", scatter_dimension=0, tiled=True
            ).astype(jnp.float32),
            lax.psum_scatter(
                grad_terms[2].astype(jnp.bfloat16), "fsdp", scatter_dimension=0, tiled=True
            ).astype(jnp.float32),
            lax.psum_scatter(
                grad_terms[3].astype(jnp.bfloat16), "fsdp", scatter_dimension=0, tiled=True
            ).astype(jnp.float32),
            lax.psum_scatter(
                grad_terms[4].astype(jnp.bfloat16), "fsdp", scatter_dimension=1, tiled=True
            ).astype(jnp.float32),
            lax.psum_scatter(
                grad_terms[5].astype(jnp.bfloat16), "fsdp", scatter_dimension=0, tiled=True
            ).astype(jnp.float32),
        )
        totals = (
            shares
            if totals is None
            else tuple((first + second for first, second in zip(totals, shares)))
        )
    totals = lax.psum(totals, "ctx")
    norm_total = totals[4]
    return (
        jnp.stack(next_list),
        jnp.stack(grad_in_list),
        jnp.stack(earlier_list, axis=1),
        totals[0],
        totals[1],
        totals[2],
        totals[3],
        norm_total[0],
        norm_total[1],
        norm_total[2],
        norm_total[3],
        totals[5].reshape(-1),
    )


F32 = jnp.float32
BF16 = jnp.bfloat16
LOG2E = math.log2(math.e)
GELU_C = math.sqrt(2.0 / math.pi)
GELU_A = 0.044715
ANY = pl.ANY
VMEM = pltpu.VMEM
SMEM = pltpu.SMEM
MIB = 1 << 20


def mm(left, right, left_dim, right_dim):
    return lax.dot_general(
        left, right, (((left_dim,), (right_dim,)), ((), ())), preferred_element_type=F32
    )


def spec(space):
    return pl.BlockSpec(memory_space=space)


def shape_of(dims, kind):
    return jax.ShapeDtypeStruct(dims, kind)


def run_kernel(kernel, name, operands, spaces, outs, scratch, flops, limit=56):
    moved = sum(o.size * o.dtype.itemsize for o in operands) + sum(
        math.prod(o.shape) * jnp.dtype(o.dtype).itemsize for o in outs
    )
    return pl.pallas_call(
        kernel,
        name=name,
        in_specs=[spec(s) for s in spaces],
        out_specs=[spec(VMEM) for _ in outs],
        out_shape=outs,
        scratch_shapes=scratch,
        compiler_params=pltpu.CompilerParams(vmem_limit_bytes=limit * MIB),
        cost_estimate=pl.CostEstimate(
            flops=int(flops), bytes_accessed=int(moved), transcendentals=0
        ),
    )(*operands)


def block_index(scalars, order):
    place = scalars[1]
    return lax.bitwise_xor(place, jnp.int32((0, 2, 1, 3)[order]))


def early_kernel(mix, earlier, grad, out_grad, out_prev, out_mix):
    streams = earlier.shape[0]
    rows = grad.shape[0]
    step = 128

    out_mix[...] = jnp.zeros_like(out_mix)

    def one(index, carry):
        here = pl.ds(pl.multiple_of(index * step, step), step)
        g = grad[here, :].astype(F32)
        total = None
        for k in range(streams):
            e = earlier[k, here, :].astype(F32)
            out_grad[k, here, :] = (mix[k] * g).astype(BF16)
            out_mix[k : k + 1, :] += jnp.sum(e * g, axis=0, keepdims=True)
            total = mix[k] * e if total is None else total + mix[k] * e
        out_prev[here, :] = total
        return carry

    lax.fori_loop(0, rows // step, one, 0)


def full_rows(pieces, first, last):
    total = None
    for piece in pieces:
        term = piece[first:last, :].astype(F32)
        total = term if total is None else total + term
    return total


def qkv_kernel(hps, batches, has_x, offset, *refs):
    if has_x:
        scalars, x, cosine, sine, w0, w1, w2, w3 = refs[:8]
        out, n1t, norms, weight = refs[8:]
        rows = n1t.shape[0] // 4
        parts = full_rows((w0, w1, w2, w3), rows, rows + 16)
        norms[...] = parts[0:8, :] + parts[8:16, :]
        v = x[...].astype(F32)
        center = v - jnp.mean(v, axis=-1, keepdims=True)
        inv = lax.rsqrt(jnp.mean(center * center, axis=-1, keepdims=True) + 1e-05)
        n1 = center * inv * norms[0:1, :] + norms[1:2, :]
        n1t[...] = n1.astype(BF16).T
    else:
        scalars, n1t, cosine, sine, w0, w1, w2, w3 = refs[:8]
        out, weight = refs[8:]
        rows = n1t.shape[0] // 4
    for order, piece in enumerate((w0, w1, w2, w3)):
        start = pl.multiple_of(block_index(scalars, order) * rows, rows)
        weight[pl.ds(start, rows), :] = piece[offset : offset + rows, :]
    width = weight.shape[1] // 3
    size = width // hps
    half = size // 2
    tokens = n1t.shape[1] // batches
    for part in range(3):
        cols = mm(weight[:, part * width : (part + 1) * width], n1t[...], 0, 0)
        for head in range(hps):
            for batch in range(batches):
                lanes = slice(batch * tokens, (batch + 1) * tokens)
                top = cols[head * size : head * size + half, lanes]
                low = cols[head * size + half : (head + 1) * size, lanes]
                if part < 2:
                    c = cosine[batch]
                    s = sine[batch]
                    top, low = top * c - low * s, low * c + top * s
                slot = batch * hps + head
                out[slot, part * size : part * size + half, :] = top.astype(BF16)
                out[slot, part * size + half : (part + 1) * size, :] = low.astype(BF16)


def stream_tile(count, stream, step):
    long = count - stream
    late = step >= long
    query = jnp.where(late, stream, count - 1 - stream)
    return query, jnp.where(late, step - long, step)


def attend_kernel(count, scale, ids, ins, outs, ot, lse, qt, kk, vt, scores, *states):
    streams = count // 2
    tops, totals, accs = states[:streams], states[streams : 2 * streams], states[2 * streams :]
    size = qt.shape[1]
    factor = scale * LOG2E
    for d in range(count):
        slot = ids[d]
        qt[slot] = ins[d, 0:size, :]
        kk[slot] = ins[d, size : 2 * size, :].T
        vt[slot] = ins[d, 2 * size :, :]
    for r in range(streams):
        tops[r][...] = jnp.full_like(tops[r], -1e30)
        totals[r][...] = jnp.zeros_like(totals[r])
        accs[r][...] = jnp.zeros_like(accs[r])
        scores[0, r] = mm(kk[0], qt[count - 1 - r], 1, 0)

    def step(index, carry):
        for r in range(streams):
            i, j = stream_tile(count, r, jnp.minimum(index + 1, count))
            scores[(index + 1) % 2, r] = mm(kk[j], qt[i], 1, 0)
        for r in range(streams):
            i, j = stream_tile(count, r, index)
            half = jnp.where(index >= count - r, 1, 0)
            s = scores[index % 2, r]
            old = tops[r][half]
            new = jnp.maximum(old, jnp.max(s, axis=0, keepdims=True) * factor)
            shrink = jnp.exp2(old - new)
            p = jnp.exp2(s * factor - new)
            totals[r][half] = totals[r][half] * shrink + jnp.sum(p, axis=0, keepdims=True)
            accs[r][half] = accs[r][half] * shrink + mm(vt[j], p.astype(BF16), 1, 0)
            tops[r][half] = new
        return carry

    lax.fori_loop(0, count + 1, step, 0)
    for r in range(streams):
        for half, i in enumerate((count - 1 - r, r)):
            run = totals[r][half]
            ot[i] = accs[r][half] / run
            lse[i] = tops[r][half] + jnp.log2(run)
    for d in range(count):
        outs[d] = ot[ids[d]].astype(BF16)


def attend_back_kernel(
    count, scale, ids, ins, grads, ot, lse, outs, qt, qq, kt, kk, vv, gt, gg, delta, scores, gains, *sums
):
    streams = count // 2
    dqs, dks, dvs = sums[:streams], sums[streams : 2 * streams], sums[2 * streams :]
    size = qt.shape[1]
    factor = scale * LOG2E
    for d in range(count):
        slot = ids[d]
        block = ins[d]
        q = block[0:size]
        k = block[size : 2 * size]
        qt[slot] = q
        kt[slot] = k
        qq[slot] = q.T
        kk[slot] = k.T
        vv[slot] = block[2 * size :].T
        g = grads[d]
        gt[slot] = g
        gg[slot] = g.T
        delta[slot] = jnp.sum(g.astype(F32) * ot[slot], axis=0, keepdims=True)
    for r in range(streams):
        dqs[r][...] = jnp.zeros_like(dqs[r])
        dks[r][...] = jnp.zeros_like(dks[r])
        dvs[r][...] = jnp.zeros_like(dvs[r])
        scores[0, r] = mm(kk[0], qt[count - 1 - r], 1, 0)
        gains[0, r] = mm(vv[0], gt[count - 1 - r], 1, 0)

    def step(index, carry):
        for r in range(streams):
            i, j = stream_tile(count, r, jnp.minimum(index + 1, count))
            scores[(index + 1) % 2, r] = mm(kk[j], qt[i], 1, 0)
            gains[(index + 1) % 2, r] = mm(vv[j], gt[i], 1, 0)
        for r in range(streams):
            i, j = stream_tile(count, r, index)
            half = jnp.where(index >= count - r, 1, 0)
            p = jnp.exp2(scores[index % 2, r] * factor - lse[i])
            ds = (p * (gains[index % 2, r] - delta[i])).astype(BF16)
            dqs[r][half] += mm(kt[j], ds, 1, 0)
            dks[r][j] += mm(ds, qq[i], 1, 0)
            dvs[r][j] += mm(p.astype(BF16), gg[i], 1, 0)
        return carry

    lax.fori_loop(0, count + 1, step, 0)
    for r in range(streams):
        for half, i in enumerate((count - 1 - r, r)):
            qt[i] = (dqs[r][half] * scale).astype(BF16)
    for d in range(count):
        slot = ids[d]
        outs[d, 0:size, :] = qt[slot]
        dk = dks[0][slot]
        dv = dvs[0][slot]
        for r in range(1, streams):
            dk = dk + dks[r][slot]
            dv = dv + dvs[r][slot]
        outs[d, size : 2 * size, :] = (dk * scale).astype(BF16).T
        outs[d, 2 * size :, :] = dv.astype(BF16).T


def gather_rows(scalars, pieces, window, target, sems, base):
    copies = []
    first, rows = window
    for order, piece in enumerate(pieces):
        start = pl.multiple_of(block_index(scalars, order) * rows, rows)
        copy = pltpu.make_async_copy(
            piece.at[pl.ds(first, rows), :], target.at[pl.ds(start, rows), :], sems.at[base + order]
        )
        copy.start()
        copies.append(copy)
    return copies


def mlp_kernel(count, stages, hps, batches, scalars, mix, x, grad, norms, *refs):
    heads = refs[:stages]
    pieces = refs[stages : stages + 4]
    refs = refs[stages + 4 :]
    hidden, dhidden, n2_out, mid_out, dmid_out, dmid_low, ot, norm_grads = refs[:8]
    head_grads = refs[8 : 8 + stages]
    out_scr, up_scr, down_scr, dn2, got, sems = refs[8 + stages :]
    width = x.shape[1]
    share = width // 4
    groups = up_scr.shape[1] // width
    deep = down_scr.shape[0] // 4
    last = (groups * share) + deep
    copies_out = gather_rows(scalars, pieces, (last, share), out_scr, sems, 0)
    copies_up = []
    for group in range(groups):
        lanes = up_scr.at[:, pl.ds(group * width, width)]
        copies_up += gather_rows(scalars, pieces, (group * share, share), lanes, sems, 4 + 4 * group)
    copies_down = gather_rows(
        scalars, pieces, (groups * share, deep), down_scr, sems, 4 + 4 * groups
    )
    for stage in range(stages):
        for slot in range(count):
            ot[slot // hps, stage * hps + slot % hps] = heads[stage][slot]
    for copy in copies_out:
        copy.wait()
    tokens = x.shape[0] // batches
    for batch in range(batches):
        rows = slice(batch * tokens, (batch + 1) * tokens)
        attended = ot[batch].reshape(width, tokens)
        middle = x[rows, :].astype(F32) + mm(attended, out_scr[...], 0, 0)
        mid_out[rows, :] = middle
        center = middle - jnp.mean(middle, axis=-1, keepdims=True)
        inv = lax.rsqrt(jnp.mean(center * center, axis=-1, keepdims=True) + 1e-05)
        n2_out[rows, :] = (center * inv * norms[2:3, :] + norms[3:4, :]).astype(BF16)
    for copy in copies_up + copies_down:
        copy.wait()
    dn2[...] = jnp.zeros_like(dn2)
    dy = (mix[mix.shape[0] - 1] * grad[...].astype(F32)).astype(BF16)
    step = 512 if up_scr.shape[1] % 512 == 0 else 128

    def one(index, carry):
        here = pl.ds(pl.multiple_of(index * step, step), step)
        up = up_scr[:, here]
        u = mm(n2_out[...], up, 1, 0)
        da = mm(dy, down_scr[here, :], 1, 1)
        square = u * u
        bend = jnp.tanh(u * (GELU_C + (GELU_C * GELU_A) * square))
        gate = 0.5 + 0.5 * bend
        hidden[:, here] = (u * gate).astype(BF16)
        slope = gate + (0.5 * u) * (1.0 - bend * bend) * (
            GELU_C + (3.0 * GELU_C * GELU_A) * square
        )
        du = (da * slope).astype(BF16)
        dhidden[:, here] = du
        dn2[...] += mm(du, up, 1, 1)
        return carry

    lax.fori_loop(0, up_scr.shape[1] // step, one, 0)
    gain_sum = None
    for batch in range(batches):
        rows = slice(batch * tokens, (batch + 1) * tokens)
        middle = mid_out[rows, :]
        center = middle - jnp.mean(middle, axis=-1, keepdims=True)
        inv = lax.rsqrt(jnp.mean(center * center, axis=-1, keepdims=True) + 1e-05)
        z = center * inv
        dn = dn2[rows, :]
        part_gain = jnp.sum(dn * z, axis=0, keepdims=True)
        part_bias = jnp.sum(dn, axis=0, keepdims=True)
        gain_sum = part_gain if gain_sum is None else gain_sum + part_gain
        bias_sum = part_bias if batch == 0 else bias_sum + part_bias
        h = dn * norms[2:3, :]
        back = inv * (
            h - jnp.mean(h, axis=-1, keepdims=True) - z * jnp.mean(h * z, axis=-1, keepdims=True)
        )
        dmid = mix[mix.shape[0] - 1] * grad[rows, :].astype(F32) + back
        dmid_out[rows, :] = dmid
        low = dmid.astype(BF16)
        dmid_low[rows, :] = low
        got[batch] = mm(out_scr[...], low, 1, 1).astype(BF16).reshape(got.shape[1:])
    norm_grads[...] = jnp.zeros_like(norm_grads)
    norm_grads[0:1, :] = gain_sum
    norm_grads[1:2, :] = bias_sum
    for stage in range(stages):
        for slot in range(count):
            head_grads[stage][slot] = got[slot // hps, stage * hps + slot % hps]


def result_kernel(window, scalars, mix, hidden, mid, prev, grad, w0, w1, w2, w3, out, out_mix, acc):
    acc[...] = mid[...]
    first, rows = window
    for order, piece in enumerate((w0, w1, w2, w3)):
        start = pl.multiple_of(block_index(scalars, order) * rows, rows)
        acc[...] += mm(hidden[:, pl.ds(start, rows)], piece[first : first + rows, :], 1, 0)
    y = acc[...]
    out[...] = (prev[...] + mix[mix.shape[0] - 1] * y).astype(BF16)
    out_mix[...] = jnp.zeros_like(out_mix)
    out_mix[0:1, :] = jnp.sum(grad[...].astype(F32) * y, axis=0, keepdims=True)


def put_pieces(me, value, outs, order, count, first):
    target = outs[order // 2]
    rows = value.shape[0] // count
    low = value.astype(BF16)
    bit = lax.rem(me, jnp.int32(2))
    for sub in range(count):
        side = lax.bitwise_xor(bit, jnp.int32(sub % 2))
        target[order % 2, side, sub // 2, first : first + rows, :] = low[
            sub * rows : (sub + 1) * rows, :
        ]


def down_grad_kernel(count, scalars, mix, hidden, grad, keep, send):
    dy = (mix[mix.shape[0] - 1] * grad[...].astype(F32)).astype(BF16)
    rows = count * keep.shape[3]
    for order in range(4):
        start = pl.multiple_of(block_index(scalars, order) * rows, rows)
        value = mm(hidden[:, pl.ds(start, rows)], dy, 0, 0)
        put_pieces(scalars[0], value, (keep, send), order, count, 0)


def up_out_grad_kernel(count, scalars, n2, dhidden, ot, dmid, keep, send, left, whole):
    batches = ot.shape[0]
    width = n2.shape[1]
    tokens = ot.shape[3]
    rows = width // 4
    thin = rows // count

    def arrange():
        for order in range(4):
            here = pl.ds(pl.multiple_of(block_index(scalars, order) * rows, rows), rows)
            left[order * rows : (order + 1) * rows, :] = whole[here, :]

    whole[...] = n2[...].T
    arrange()
    groups = dhidden.shape[1] // width
    for group in range(groups):
        value = mm(left[...], dhidden[:, group * width : (group + 1) * width], 1, 0)
        for order in range(4):
            put_pieces(
                scalars[0],
                value[order * rows : (order + 1) * rows, :],
                (keep, send),
                order,
                count,
                group * thin,
            )
    for batch in range(batches):
        whole[:, batch * tokens : (batch + 1) * tokens] = ot[batch].reshape(width, tokens)
    arrange()
    value = mm(left[...], dmid[...], 1, 0)
    for order in range(4):
        put_pieces(
            scalars[0],
            value[order * rows : (order + 1) * rows, :],
            (keep, send),
            order,
            count,
            groups * thin,
        )


def in_grad_kernel(count, hps, scalars, cosine, sine, n1t, grads, dt, keep, send, left):
    batches = dt.shape[0]
    size = dt.shape[3]
    half = size // 2
    tokens = dt.shape[4]
    for slot in range(count):
        batch, head = slot // hps, slot % hps
        c = cosine[batch]
        s = sine[batch]
        for part in range(2):
            top = grads[slot, part * size : part * size + half, :].astype(F32)
            low = grads[slot, part * size + half : (part + 1) * size, :].astype(F32)
            dt[batch, part, head, 0:half, :] = (top * c + low * s).astype(BF16)
            dt[batch, part, head, half:size, :] = (low * c - top * s).astype(BF16)
        dt[batch, 2, head] = grads[slot, 2 * size :, :]
    width = n1t.shape[0]
    rows = width // 4
    thin = rows // count
    for order in range(4):
        here = pl.ds(pl.multiple_of(block_index(scalars, order) * rows, rows), rows)
        left[order * rows : (order + 1) * rows, :] = n1t[here, :]
    cols = 3 * hps * size
    value = None
    for batch in range(batches):
        term = mm(
            left[:, batch * tokens : (batch + 1) * tokens], dt[batch].reshape(cols, tokens), 1, 1
        )
        value = term if value is None else value + term
    low = value.astype(BF16)
    for order in range(4):
        target = (keep, send)[order // 2]
        for sub in range(count):
            start = order * rows + sub * thin
            target[order % 2, sub] = low[start : start + thin, :]


def input_grad_kernel(stages, windows, scalars, x, norms, dmid, *refs):
    dts = refs[:stages]
    pieces = refs[stages : stages + 4 * stages]
    out, norm_grads, weights, sems = refs[5 * stages :]
    copies = []
    for stage in range(stages):
        copies += gather_rows(
            scalars,
            pieces[4 * stage : 4 * stage + 4],
            windows[stage],
            weights.at[stage],
            sems,
            4 * stage,
        )
    for copy in copies:
        copy.wait()
    batches = dts[0].shape[0]
    tokens = dts[0].shape[4]
    cols = weights.shape[2]
    gain_sum = bias_sum = None
    for batch in range(batches):
        rows = slice(batch * tokens, (batch + 1) * tokens)
        dnt = None
        for stage in range(stages):
            term = mm(weights[stage], dts[stage][batch].reshape(cols, tokens), 1, 0)
            dnt = term if dnt is None else dnt + term
        dn = dnt.T
        v = x[rows, :].astype(F32)
        center = v - jnp.mean(v, axis=-1, keepdims=True)
        inv = lax.rsqrt(jnp.mean(center * center, axis=-1, keepdims=True) + 1e-05)
        z = center * inv
        part_gain = jnp.sum(dn * z, axis=0, keepdims=True)
        part_bias = jnp.sum(dn, axis=0, keepdims=True)
        gain_sum = part_gain if batch == 0 else gain_sum + part_gain
        bias_sum = part_bias if batch == 0 else bias_sum + part_bias
        h = dn * norms[0:1, :]
        back = inv * (
            h - jnp.mean(h, axis=-1, keepdims=True) - z * jnp.mean(h * z, axis=-1, keepdims=True)
        )
        out[rows, :] = (dmid[rows, :] + back).astype(BF16)
    norm_grads[...] = jnp.zeros_like(norm_grads)
    norm_grads[0:1, :] = gain_sum
    norm_grads[1:2, :] = bias_sum


def place_split_kernel(moves, scalars, near, far, *outs):
    bit = lax.rem(scalars[0], jnp.int32(2))
    for side, source in enumerate((near, far)):
        for sub in range(source.shape[0]):
            slot = 2 * sub + lax.bitwise_xor(bit, jnp.int32(side))
            for out, first, rows, to, wide in moves:
                outs[out][slot, :, to : to + wide] = source[sub, first : first + rows, :].astype(F32)


def place_in_kernel(width, wide, *refs):
    *pieces, out = refs
    for s, piece in enumerate(pieces):
        for sub in range(piece.shape[0]):
            for part in range(3):
                to = part * width + s * wide
                out[sub, :, to : to + wide] = piece[sub, :, part * wide : (part + 1) * wide].astype(F32)


def exchange(value, axis, bit):
    size = lax.axis_size(axis)
    return lax.ppermute(value, axis, [(i, i ^ bit) for i in range(size)])


def added(left, right):
    return (left.astype(F32) + right.astype(F32)).astype(BF16)


def swapped(value, groups=None):
    return lax.all_to_all(value, "ctx", 0, 0, axis_index_groups=groups)


def summed(value):
    return jnp.sum(value.astype(F32), axis=0).astype(BF16)


def spread(own, count, groups=None):
    return swapped(jnp.broadcast_to(own[None], (count, *own.shape)), groups)


def halved(keep, send):
    got = exchange(send, "fsdp", 1)
    passed = added(keep[1], got[1])
    own = added(keep[0], got[0])
    return added(own, exchange(passed, "fsdp", 2))


def other_bits():
    count = lax.axis_size("ctx")
    return [list(range(first, count, 2)) for first in range(2)]


def sum_far(own):
    groups = other_bits()
    part = summed(swapped(own, groups))
    near = spread(part, lax.axis_size("ctx") // 2, groups)
    return part, near, exchange(near, "ctx", 1)


def chip_first(keep, send):
    own = halved(keep, send)
    return own, added(own[0], exchange(own[1], "ctx", 1))


def chip_last(keep, send):
    both = added(keep, exchange(send, "fsdp", 1))
    both = added(both[:, 0], exchange(both[:, 1], "ctx", 1))
    return both, added(both[0], exchange(both[1], "fsdp", 2))


def reduce_whole(keep, send):
    return spread(summed(swapped(halved(keep, send))), lax.axis_size("ctx"))


def after(value, *others):
    return lax.optimization_barrier((value, *others))[0]


def gathered(shard):
    other_chip = exchange(shard, "fsdp", 2)
    return [shard, other_chip, exchange(shard, "fsdp", 1), exchange(other_chip, "fsdp", 1)]


def head_body(
    inputs,
    earlier,
    input_proj,
    output_proj,
    up_proj,
    down_proj,
    norm1_gain,
    norm1_bias,
    norm2_gain,
    norm2_bias,
    mixing,
    block_order,
    grad_next,
):
    batches, tokens, width = inputs.shape
    rows = batches * tokens
    heads = HEADS
    size = width // heads
    scale = size ** (-0.5)
    streams = earlier.shape[0]
    count = lax.axis_size("ctx")
    hps = count // batches
    stages = heads // hps
    inner = down_proj.shape[0] * 4
    me = lax.axis_index("ctx").astype(jnp.int32)
    place = lax.axis_index("fsdp").astype(jnp.int32)
    scalars = jnp.stack([me, place])
    ids = block_order[me // hps].astype(jnp.int32)
    x = inputs.reshape(rows, width)
    grad = grad_next.reshape(rows, width)

    share = width // 4
    cols = 3 * hps * size
    norm_stack = jnp.stack([norm1_gain, norm1_bias, norm2_gain, norm2_bias])
    coarse = lax.reduce_precision(norm_stack, 8, 7)
    norm_rows = jnp.zeros((16, width), BF16)
    norm_rows = lax.dynamic_update_slice(norm_rows, coarse.astype(BF16), (0, place * share))
    norm_rows = lax.dynamic_update_slice(
        norm_rows, (norm_stack - coarse).astype(BF16), (8, place * share)
    )
    wide = hps * size
    chunks = [
        jnp.concatenate(
            [input_proj[:, p * width + s * wide : p * width + (s + 1) * wide] for p in range(3)], 1
        )
        for s in range(stages)
    ]
    first_in = gathered(jnp.concatenate([chunks[0], jnp.pad(norm_rows, ((0, 0), (0, cols - width)))]))
    rest_in = gathered(jnp.concatenate(chunks[1:]))
    groups = inner // width
    up_rows = jnp.moveaxis(up_proj.reshape(share, groups, width), 1, 0).reshape(-1, width)
    packed = jnp.concatenate([up_rows, down_proj, output_proj])

    half = size // 2
    own_blocks = block_order[:, me]
    positions = (own_blocks[:, None] * tokens + lax.iota(jnp.int32, tokens)[None]).astype(F32)
    freqs = jnp.exp(lax.iota(F32, half) * (-2.0 * math.log(10000.0) / size))
    angle = freqs[None, :, None] * positions[:, None, :]
    cosine = jnp.cos(angle)
    sine = jnp.sin(angle)

    grad_earlier, prev, mix_early = run_kernel(
        early_kernel,
        "early",
        [mixing, earlier.reshape(streams, rows, width), grad],
        [SMEM, VMEM, VMEM],
        [
            shape_of((streams, rows, width), BF16),
            shape_of((rows, width), F32),
            shape_of((8, width), F32),
        ],
        [],
        6 * streams * rows * width,
    )

    pair_shape = shape_of((count, 3 * size, tokens), BF16)
    x = after(x, mix_early)
    weights = gathered(after(packed, rest_in[3]))
    held = []
    n1t = norms = None
    windows = [(0, share)] + [(share * s, share) for s in range(stages - 1)]
    for s in range(stages):
        first = s == 0
        operands = [scalars] + ([x] if first else [n1t]) + [cosine, sine]
        operands += first_in if first else rest_in
        outs = [pair_shape]
        if first:
            outs += [shape_of((width, rows), BF16), shape_of((8, width), F32)]
        result = run_kernel(
            functools.partial(qkv_kernel, hps, batches, first, windows[s][0]),
            "qkv",
            operands,
            [SMEM] + [VMEM] * (len(operands) - 1),
            outs,
            [pltpu.VMEM((width, cols), BF16)],
            2 * rows * width * cols,
        )
        if first:
            n1t, norms = result[1:]
        held.append(swapped(result[0]))

    tiles = count * (count + 1) // 2
    one = tokens * tokens * size * 2
    streams_in = count // 2
    head_shape = shape_of((count, size, tokens), BF16)
    attended = []
    saved = []
    for s in range(stages):
        result = run_kernel(
            functools.partial(attend_kernel, count, scale),
            "attend",
            [after(ids, saved[-1][1]) if saved else ids, held[s]],
            [SMEM, VMEM],
            [head_shape, shape_of((count, size, tokens), F32), shape_of((count, 1, tokens), F32)],
            [
                pltpu.VMEM((count, size, tokens), BF16),
                pltpu.VMEM((count, tokens, size), BF16),
                pltpu.VMEM((count, size, tokens), BF16),
                pltpu.VMEM((2, streams_in, tokens, tokens), F32),
            ]
            + [pltpu.VMEM((2, 1, tokens), F32)] * (2 * streams_in)
            + [pltpu.VMEM((2, size, tokens), F32)] * streams_in,
            4 * 2 * one * tiles,
        )
        saved.append(result[1:])
        attended.append(swapped(result[0]))

    result = run_kernel(
        functools.partial(mlp_kernel, count, stages, hps, batches),
        "mlp",
        [scalars, mixing, x, grad, norms] + attended + weights,
        [SMEM, SMEM, VMEM, VMEM, VMEM] + [VMEM] * stages + [ANY] * 4,
        [
            shape_of((rows, inner), BF16),
            shape_of((rows, inner), BF16),
            shape_of((rows, width), BF16),
            shape_of((rows, width), F32),
            shape_of((rows, width), F32),
            shape_of((rows, width), BF16),
            shape_of((batches, heads, size, tokens), BF16),
            shape_of((8, width), F32),
        ]
        + [head_shape] * stages,
        [
            pltpu.VMEM((width, width), BF16),
            pltpu.VMEM((width, inner), BF16),
            pltpu.VMEM((inner, width), BF16),
            pltpu.VMEM((rows, width), F32),
            pltpu.VMEM((batches, heads, size, tokens), BF16),
            pltpu.SemaphoreType.DMA((8 + 4 * groups,)),
        ],
        6 * rows * width * inner,
    )
    hidden, dhidden, n2, mid, dmid, dmid_low, ot, norm2_grads = result[:8]
    sent_grads = [swapped(value) for value in result[8:]]

    sub = inner // 4 // count
    thin = share // count
    down_sums = run_kernel(
        functools.partial(down_grad_kernel, count),
        "down_grad",
        [scalars, mixing, hidden, grad],
        [SMEM, SMEM, VMEM, VMEM],
        [shape_of((2, 2, count // 2, sub, width), BF16)] * 2,
        [],
        2 * rows * width * inner,
    )
    up_sums = run_kernel(
        functools.partial(up_out_grad_kernel, count),
        "up_out_grad",
        [scalars, n2, dhidden, ot, dmid_low],
        [SMEM] + [VMEM] * 4,
        [shape_of((2, 2, count // 2, thin * (groups + 1), width), BF16)] * 2,
        [pltpu.VMEM((width, rows), BF16), pltpu.VMEM((width, rows), BF16)],
        2 * rows * width * (inner + width),
    )
    down_chip, down_own = chip_first(*down_sums)
    up_both, up_own = chip_last(*up_sums)
    down_part, *down_parts = sum_far(down_own)
    up_part, *up_parts = sum_far(up_own)
    gates = [(down_sums[0], up_sums[0]), (down_chip, up_both), (down_own, up_own)]

    dts = []
    in_parts = []
    for s in range(stages):
        turn = gates[s] if s < len(gates) else gates[-1]
        turn = turn + ((back,) if s else ())
        (back,) = run_kernel(
            functools.partial(attend_back_kernel, count, scale),
            "attend_back",
            [ids, after(held[s], *turn), sent_grads[s]] + list(saved[s]),
            [SMEM] + [VMEM] * 4,
            [pair_shape],
            [
                pltpu.VMEM((count, size, tokens), BF16),
                pltpu.VMEM((count, tokens, size), BF16),
                pltpu.VMEM((count, size, tokens), BF16),
                pltpu.VMEM((count, tokens, size), BF16),
                pltpu.VMEM((count, tokens, size), BF16),
                pltpu.VMEM((count, size, tokens), BF16),
                pltpu.VMEM((count, tokens, size), BF16),
                pltpu.VMEM((count, 1, tokens), F32),
                pltpu.VMEM((2, streams_in, tokens, tokens), F32),
                pltpu.VMEM((2, streams_in, tokens, tokens), F32),
            ]
            + [pltpu.VMEM((2, size, tokens), F32)] * streams_in
            + [pltpu.VMEM((count, tokens, size), F32)] * (2 * streams_in),
            4 * 5 * one * tiles,
        )
        dt, keep, send = run_kernel(
            functools.partial(in_grad_kernel, count, hps),
            "in_grad",
            [scalars, cosine, sine, n1t, swapped(back)],
            [SMEM] + [VMEM] * 4,
            [shape_of((batches, 3, hps, size, tokens), BF16)]
            + [shape_of((2, count, thin, cols), BF16)] * 2,
            [pltpu.VMEM((width, rows), BF16)],
            2 * rows * width * cols,
        )
        dts.append(dt)
        in_parts.append(reduce_whole(keep, send))

    next_input, mix_last = run_kernel(
        functools.partial(result_kernel, (groups * share, inner // 4)),
        "result",
        [scalars, mixing, hidden, mid, prev, after(grad, back)] + weights,
        [SMEM, SMEM] + [VMEM] * 8,
        [shape_of((rows, width), BF16), shape_of((8, width), F32)],
        [pltpu.VMEM((rows, width), F32)],
        2 * rows * width * inner,
    )

    grad_input, norm1_grads = run_kernel(
        functools.partial(input_grad_kernel, stages, windows),
        "input_grad",
        [scalars, x, norms, dmid] + dts + first_in + rest_in * (stages - 1),
        [SMEM] + [VMEM] * (3 + stages) + [ANY] * (4 * stages),
        [shape_of((rows, width), BF16), shape_of((8, width), F32)],
        [pltpu.VMEM((stages, width, cols), BF16), pltpu.SemaphoreType.DMA((4 * stages,))],
        2 * rows * width * 3 * width,
    )

    small = jnp.concatenate(
        [norm1_grads[:2], norm2_grads[:2], mix_early[:streams], mix_last[:1]], axis=0
    )
    small = small + exchange(small, "fsdp", 1)
    small = small + exchange(small, "fsdp", 2)
    small = jnp.sum(spread(small, count), axis=0)
    norm_total = lax.dynamic_slice_in_dim(small[:4], place * share, share, 1)
    mix_total = jnp.sum(small[4:], axis=1)

    (grad_down,) = run_kernel(
        functools.partial(place_split_kernel, ((0, 0, sub, 0, width),)),
        "place_down",
        [scalars, *down_parts],
        [SMEM] + [VMEM] * 2,
        [shape_of((count, sub, width), F32)],
        [],
        0,
    )
    moves = tuple((0, g * thin, thin, g * width, width) for g in range(groups))
    grad_up, grad_out = run_kernel(
        functools.partial(place_split_kernel, moves + ((1, groups * thin, thin, 0, width),)),
        "place_up",
        [scalars, *up_parts],
        [SMEM] + [VMEM] * 2,
        [shape_of((count, thin, inner), F32), shape_of((count, thin, width), F32)],
        [],
        0,
    )
    (grad_in,) = run_kernel(
        functools.partial(place_in_kernel, width, hps * size),
        "place_in",
        in_parts,
        [VMEM] * stages,
        [shape_of((count, thin, 3 * width), F32)],
        [],
        0,
    )
    return (
        next_input.reshape(batches, tokens, width),
        grad_input.reshape(batches, tokens, width),
        grad_earlier.reshape(streams, batches, tokens, width),
        grad_in.reshape(share, 3 * width),
        grad_out.reshape(share, width),
        grad_up.reshape(share, inner),
        grad_down.reshape(inner // 4, width),
        norm_total[0],
        norm_total[1],
        norm_total[2],
        norm_total[3],
        mix_total,
    )


def heads_fit(batches):
    count = lax.axis_size("ctx")
    return (
        lax.axis_size("fsdp") == 4
        and count & (count - 1) == 0
        and count % batches == 0
        and HEADS % max(count // batches, 1) == 0
    )


def either_body(inputs, *rest):
    return (head_body if heads_fit(inputs.shape[0]) else body)(inputs, *rest)


def solution(mesh):
    placed = (
        P("fsdp", "ctx", None),
        P(None, "fsdp", "ctx", None),
        P("fsdp", None),
        P("fsdp", None),
        P("fsdp", None),
        P("fsdp", None),
        P("fsdp"),
        P("fsdp"),
        P("fsdp"),
        P("fsdp"),
        P(),
        P(),
        P("fsdp", "ctx", None),
    )
    return jax.shard_map(
        either_body,
        mesh=mesh,
        in_specs=placed,
        out_specs=(
            P("fsdp", "ctx", None),
            P("fsdp", "ctx", None),
            P(None, "fsdp", "ctx", None),
            P("fsdp", None),
            P("fsdp", None),
            P("fsdp", None),
            P("fsdp", None),
            P("fsdp"),
            P("fsdp"),
            P("fsdp"),
            P("fsdp"),
            P(),
        ),
        check_vma=False,
    )
```

```python
import functools
import math

import jax
import jax.numpy as jnp
from jax import lax
from jax.experimental import pallas as pl
from jax.experimental.pallas import tpu as pltpu
from jax.sharding import PartitionSpec as P

HEADS = 12


def passed_along(value, axis, steps):
    count = lax.axis_size(axis)
    pairs = [(source, (source + steps) % count) for source in range(count)]
    return lax.ppermute(value, axis, pairs)


def norm_parts(values, gain, bias):
    mean_value = jnp.mean(values, axis=-1, keepdims=True)
    centered = values - mean_value
    inv_std = lax.rsqrt(jnp.mean(centered * centered, axis=-1, keepdims=True) + 1e-05)
    normed = centered * inv_std
    return (normed * gain + bias, normed, inv_std)


def norm_back(grad_out, normed, inv_std, gain):
    scaled = grad_out * gain
    mean_one = jnp.mean(scaled, axis=-1, keepdims=True)
    mean_two = jnp.mean(scaled * normed, axis=-1, keepdims=True)
    return inv_std * (scaled - mean_one - normed * mean_two)


def rotary_tables(block_id, block_rows, head_dim):
    half_dim = head_dim // 2
    positions = (block_id * block_rows + lax.iota(jnp.int32, block_rows)).astype(jnp.float32)
    freqs = jnp.exp(lax.iota(jnp.float32, half_dim) * (-2.0 * math.log(10000.0) / head_dim))
    angle = positions[:, None] * freqs[None, :]
    return (jnp.cos(angle)[:, None, :], jnp.sin(angle)[:, None, :])


def rotate(values, cosine, sine_table):
    half_dim = values.shape[-1] // 2
    first_half = values[..., :half_dim]
    second_half = values[..., half_dim:]
    return jnp.concatenate(
        [
            first_half * cosine - second_half * sine_table,
            second_half * cosine + first_half * sine_table,
        ],
        axis=-1,
    )


def unrotate(grads, cosine, sine_table):
    half_dim = grads.shape[-1] // 2
    first_half = grads[..., :half_dim]
    second_half = grads[..., half_dim:]
    return jnp.concatenate(
        [
            first_half * cosine + second_half * sine_table,
            second_half * cosine - first_half * sine_table,
        ],
        axis=-1,
    )


def head_view(values, head_count):
    return values.reshape(values.shape[0], head_count, values.shape[1] // head_count)


def forward_visit(state, local_query, block_keys, block_values, head_count, score_scale):
    run_max, run_sum, accum = state
    query_heads = head_view(local_query, head_count)
    key_heads = head_view(block_keys, head_count)
    value_heads = head_view(block_values, head_count)
    scores = (
        jnp.einsum("qhe,khe->hqk", query_heads, key_heads, preferred_element_type=jnp.float32)
        * score_scale
    )
    new_max = jnp.maximum(run_max, jnp.max(scores, axis=-1))
    weights = jnp.exp(scores - new_max[:, :, None])
    factor = jnp.exp(run_max - new_max)
    new_sum = run_sum * factor + jnp.sum(weights, axis=-1)
    update = jnp.einsum(
        "hqk,khe->qhe",
        weights.astype(jnp.bfloat16),
        value_heads,
        preferred_element_type=jnp.float32,
    )
    return (new_max, new_sum, accum * jnp.transpose(factor)[:, :, None] + update)


def backward_pair(
    query_rows, key_rows, value_rows, grad_rows, log_total, row_delta, head_count, score_scale
):
    query_heads = head_view(query_rows, head_count)
    key_heads = head_view(key_rows, head_count)
    value_heads = head_view(value_rows, head_count)
    grad_heads = head_view(grad_rows, head_count)
    scores = (
        jnp.einsum("qhe,khe->hqk", query_heads, key_heads, preferred_element_type=jnp.float32)
        * score_scale
    )
    probs = jnp.exp(scores - log_total[:, :, None])
    grad_probs = jnp.einsum(
        "qhe,khe->hqk", grad_heads, value_heads, preferred_element_type=jnp.float32
    )
    grad_scores = (probs * (grad_probs - row_delta[:, :, None])).astype(jnp.bfloat16)
    grad_query = (
        jnp.einsum("hqk,khe->qhe", grad_scores, key_heads, preferred_element_type=jnp.float32)
        * score_scale
    )
    grad_keys = (
        jnp.einsum("hqk,qhe->khe", grad_scores, query_heads, preferred_element_type=jnp.float32)
        * score_scale
    )
    grad_values = jnp.einsum(
        "hqk,qhe->khe", probs.astype(jnp.bfloat16), grad_heads, preferred_element_type=jnp.float32
    )
    return (
        grad_query.reshape(query_rows.shape[0], -1),
        grad_keys.reshape(key_rows.shape[0], -1),
        grad_values.reshape(key_rows.shape[0], -1),
    )


def body(
    inputs,
    earlier,
    input_proj,
    output_proj,
    up_proj,
    down_proj,
    norm1_gain,
    norm1_bias,
    norm2_gain,
    norm2_bias,
    mixing,
    block_order,
    grad_next,
):
    head_count = HEADS
    batch_count = inputs.shape[0]
    block_rows = inputs.shape[1]
    model_width = inputs.shape[2]
    head_dim = model_width // head_count
    score_scale = head_dim ** (-0.5)
    stream_count = earlier.shape[0]
    cycle_size = lax.axis_size("ctx")
    cycle_place = lax.axis_index("ctx")
    norm_stack = jnp.stack([norm1_gain, norm1_bias, norm2_gain, norm2_bias])
    full_in, full_out, full_up, full_down, full_norms = (
        lax.all_gather(input_proj, "fsdp", axis=0, tiled=True),
        lax.all_gather(output_proj, "fsdp", axis=0, tiled=True),
        lax.all_gather(up_proj, "fsdp", axis=0, tiled=True),
        lax.all_gather(down_proj, "fsdp", axis=0, tiled=True),
        lax.all_gather(norm_stack.astype(jnp.bfloat16), "fsdp", axis=1, tiled=True).astype(
            norm_stack.dtype
        ),
    )
    gain_one = full_norms[0]
    bias_one = full_norms[1]
    gain_two = full_norms[2]
    bias_two = full_norms[3]
    next_list = []
    grad_in_list = []
    earlier_list = []
    totals = None
    for batch in range(batch_count):
        block_input = inputs[batch].astype(jnp.float32)
        order_row = block_order[batch]
        own_block = order_row[cycle_place]
        cosine, sine_table = rotary_tables(own_block, block_rows, head_dim)
        normed_in, normed_one, inv_one = norm_parts(block_input, gain_one, bias_one)
        normed_in_b = normed_in.astype(jnp.bfloat16)
        projected = jnp.dot(normed_in_b, full_in, preferred_element_type=jnp.float32)
        local_query = (
            rotate(head_view(projected[:, :model_width], head_count), cosine, sine_table)
            .reshape(block_rows, model_width)
            .astype(jnp.bfloat16)
        )
        local_keys = (
            rotate(
                head_view(projected[:, model_width : 2 * model_width], head_count),
                cosine,
                sine_table,
            )
            .reshape(block_rows, model_width)
            .astype(jnp.bfloat16)
        )
        local_values = projected[:, 2 * model_width :].astype(jnp.bfloat16)
        start_state = (
            jnp.full((head_count, block_rows), -1e30, jnp.float32),
            jnp.zeros((head_count, block_rows), jnp.float32),
            jnp.zeros((block_rows, head_count, head_dim), jnp.float32),
        )
        piece_keys = lax.all_gather(local_keys, "ctx", axis=0, tiled=True)
        piece_values = lax.all_gather(local_values, "ctx", axis=0, tiled=True)
        count = piece_keys.shape[0] // block_rows

        def one_block(index, state_now):
            block_keys = lax.dynamic_slice_in_dim(piece_keys, index * block_rows, block_rows, 0)
            block_values = lax.dynamic_slice_in_dim(piece_values, index * block_rows, block_rows, 0)
            return lax.cond(
                order_row[index] <= own_block,
                lambda held: forward_visit(
                    held, local_query, block_keys, block_values, head_count, score_scale
                ),
                lambda held: held,
                state_now,
            )

        run_max, run_sum, accum = lax.fori_loop(0, count, one_block, start_state)
        log_total = run_max + jnp.log(run_sum)
        attended = accum / jnp.transpose(run_sum)[:, :, None]
        attended_b = attended.reshape(block_rows, model_width).astype(jnp.bfloat16)
        middle = block_input + jnp.dot(attended_b, full_out, preferred_element_type=jnp.float32)
        normed_mid, normed_two, inv_two = norm_parts(middle, gain_two, bias_two)
        normed_mid_b = normed_mid.astype(jnp.bfloat16)
        hidden_pre = jnp.dot(normed_mid_b, full_up, preferred_element_type=jnp.float32)
        hidden_b = jax.nn.gelu(hidden_pre).astype(jnp.bfloat16)
        result = middle + jnp.dot(hidden_b, full_down, preferred_element_type=jnp.float32)
        previous = earlier[:, batch].astype(jnp.float32)
        mixed_out = (
            jnp.sum(mixing[:stream_count, None, None] * previous, axis=0)
            + mixing[stream_count] * result
        )
        next_list.append(mixed_out.astype(jnp.bfloat16))
        grad_out = grad_next[batch].astype(jnp.float32)
        earlier_list.append(
            (mixing[:stream_count, None, None] * grad_out[None]).astype(jnp.bfloat16)
        )
        mix_grad = jnp.concatenate(
            [jnp.sum(previous * grad_out[None], axis=(1, 2)), jnp.sum(result * grad_out)[None]]
        )
        grad_result = mixing[stream_count] * grad_out
        grad_result_b = grad_result.astype(jnp.bfloat16)
        grad_down = jnp.einsum(
            "rf,rd->fd", hidden_b, grad_result_b, preferred_element_type=jnp.float32
        )
        grad_hidden = jnp.einsum(
            "rd,fd->rf", grad_result_b, full_down, preferred_element_type=jnp.float32
        )
        grad_pre = jax.vjp(jax.nn.gelu, hidden_pre)[1](grad_hidden)[0]
        grad_pre_b = grad_pre.astype(jnp.bfloat16)
        grad_up = jnp.einsum(
            "rd,rf->df", normed_mid_b, grad_pre_b, preferred_element_type=jnp.float32
        )
        grad_norm_mid = jnp.einsum(
            "rf,df->rd", grad_pre_b, full_up, preferred_element_type=jnp.float32
        )
        grad_gain_two = jnp.sum(grad_norm_mid * normed_two, axis=0)
        grad_bias_two = jnp.sum(grad_norm_mid, axis=0)
        grad_middle = grad_result + norm_back(grad_norm_mid, normed_two, inv_two, gain_two)
        grad_middle_b = grad_middle.astype(jnp.bfloat16)
        grad_out_proj = jnp.einsum(
            "rd,re->de", attended_b, grad_middle_b, preferred_element_type=jnp.float32
        )
        grad_att_b = jnp.einsum(
            "re,de->rd", grad_middle_b, full_out, preferred_element_type=jnp.float32
        ).astype(jnp.bfloat16)
        row_delta = jnp.einsum(
            "qhe,qhe->hq", head_view(grad_att_b, head_count).astype(jnp.float32), attended
        )
        zero_rows = jnp.zeros((block_rows, model_width), jnp.float32)

        def key_visit(offset, grad_query, cycle_keys, cycle_values, cycle_dk, cycle_dv):
            their_block = order_row[(cycle_place - offset) % cycle_size]

            def add_pair(held):
                part_q, part_k, part_v = backward_pair(
                    local_query,
                    cycle_keys,
                    cycle_values,
                    grad_att_b,
                    log_total,
                    row_delta,
                    head_count,
                    score_scale,
                )
                return (held[0] + part_q, held[1] + part_k, held[2] + part_v)

            return lax.cond(
                their_block <= own_block,
                add_pair,
                lambda held: held,
                (grad_query, cycle_dk, cycle_dv),
            )

        def key_turn(offset, carry):
            grad_query, cycle_keys, cycle_values, cycle_dk, cycle_dv = carry
            grad_query, cycle_dk, cycle_dv = key_visit(
                offset, grad_query, cycle_keys, cycle_values, cycle_dk, cycle_dv
            )
            cycle_keys, cycle_values = passed_along((cycle_keys, cycle_values), "ctx", 1)
            cycle_dk, cycle_dv = (
                passed_along(cycle_dk.astype(jnp.bfloat16), "ctx", 1).astype(cycle_dk.dtype),
                passed_along(cycle_dv.astype(jnp.bfloat16), "ctx", 1).astype(cycle_dv.dtype),
            )
            return (grad_query, cycle_keys, cycle_values, cycle_dk, cycle_dv)

        grad_query, cycle_keys, cycle_values, cycle_dk, cycle_dv = lax.fori_loop(
            0, cycle_size - 1, key_turn, (zero_rows, local_keys, local_values, zero_rows, zero_rows)
        )
        grad_query, cycle_dk, cycle_dv = key_visit(
            cycle_size - 1, grad_query, cycle_keys, cycle_values, cycle_dk, cycle_dv
        )
        grad_keys, grad_values = (
            passed_along(cycle_dk.astype(jnp.bfloat16), "ctx", 1).astype(cycle_dk.dtype),
            passed_along(cycle_dv.astype(jnp.bfloat16), "ctx", 1).astype(cycle_dv.dtype),
        )
        grad_query_pre = unrotate(head_view(grad_query, head_count), cosine, sine_table).reshape(
            block_rows, model_width
        )
        grad_keys_pre = unrotate(head_view(grad_keys, head_count), cosine, sine_table).reshape(
            block_rows, model_width
        )
        grad_proj_b = jnp.concatenate([grad_query_pre, grad_keys_pre, grad_values], axis=1).astype(
            jnp.bfloat16
        )
        grad_in_proj = jnp.einsum(
            "rd,rf->df", normed_in_b, grad_proj_b, preferred_element_type=jnp.float32
        )
        grad_norm_in = jnp.einsum(
            "rf,df->rd", grad_proj_b, full_in, preferred_element_type=jnp.float32
        )
        grad_gain_one = jnp.sum(grad_norm_in * normed_one, axis=0)
        grad_bias_one = jnp.sum(grad_norm_in, axis=0)
        grad_block_in = grad_middle + norm_back(grad_norm_in, normed_one, inv_one, gain_one)
        grad_in_list.append(grad_block_in.astype(jnp.bfloat16))
        norm_grads = jnp.stack([grad_gain_one, grad_bias_one, grad_gain_two, grad_bias_two])
        mix_tiled = jnp.broadcast_to(mix_grad[None, :], (lax.axis_size("fsdp"), stream_count + 1))
        grad_terms = (grad_in_proj, grad_out_proj, grad_up, grad_down, norm_grads, mix_tiled)
        shares = (
            lax.psum_scatter(
                grad_terms[0].astype(jnp.bfloat16), "fsdp", scatter_dimension=0, tiled=True
            ).astype(jnp.float32),
            lax.psum_scatter(
                grad_terms[1].astype(jnp.bfloat16), "fsdp", scatter_dimension=0, tiled=True
            ).astype(jnp.float32),
            lax.psum_scatter(
                grad_terms[2].astype(jnp.bfloat16), "fsdp", scatter_dimension=0, tiled=True
            ).astype(jnp.float32),
            lax.psum_scatter(
                grad_terms[3].astype(jnp.bfloat16), "fsdp", scatter_dimension=0, tiled=True
            ).astype(jnp.float32),
            lax.psum_scatter(
                grad_terms[4].astype(jnp.bfloat16), "fsdp", scatter_dimension=1, tiled=True
            ).astype(jnp.float32),
            lax.psum_scatter(
                grad_terms[5].astype(jnp.bfloat16), "fsdp", scatter_dimension=0, tiled=True
            ).astype(jnp.float32),
        )
        totals = (
            shares
            if totals is None
            else tuple((first + second for first, second in zip(totals, shares)))
        )
    totals = lax.psum(totals, "ctx")
    norm_total = totals[4]
    return (
        jnp.stack(next_list),
        jnp.stack(grad_in_list),
        jnp.stack(earlier_list, axis=1),
        totals[0],
        totals[1],
        totals[2],
        totals[3],
        norm_total[0],
        norm_total[1],
        norm_total[2],
        norm_total[3],
        totals[5].reshape(-1),
    )


F32 = jnp.float32
BF16 = jnp.bfloat16
LOG2E = math.log2(math.e)
GELU_C = math.sqrt(2.0 / math.pi)
GELU_A = 0.044715
ANY = pl.ANY
VMEM = pltpu.VMEM
SMEM = pltpu.SMEM
MIB = 1 << 20


def mm(left, right, left_dim, right_dim):
    return lax.dot_general(
        left, right, (((left_dim,), (right_dim,)), ((), ())), preferred_element_type=F32
    )


def spec(space):
    return pl.BlockSpec(memory_space=space)


def shape_of(dims, kind):
    return jax.ShapeDtypeStruct(dims, kind)


def run_kernel(kernel, name, operands, spaces, outs, scratch, flops, limit=56):
    moved = sum(o.size * o.dtype.itemsize for o in operands) + sum(
        math.prod(o.shape) * jnp.dtype(o.dtype).itemsize for o in outs
    )
    return pl.pallas_call(
        kernel,
        name=name,
        in_specs=[spec(s) for s in spaces],
        out_specs=[spec(VMEM) for _ in outs],
        out_shape=outs,
        scratch_shapes=scratch,
        compiler_params=pltpu.CompilerParams(vmem_limit_bytes=limit * MIB),
        cost_estimate=pl.CostEstimate(
            flops=int(flops), bytes_accessed=int(moved), transcendentals=0
        ),
    )(*operands)


def block_index(scalars, order):
    place = scalars[1]
    return lax.bitwise_xor(place, jnp.int32((0, 2, 1, 3)[order]))


def early_kernel(mix, earlier, grad, out_grad, out_prev, out_mix):
    streams = earlier.shape[0]
    rows = grad.shape[0]
    step = 128

    out_mix[...] = jnp.zeros_like(out_mix)

    def one(index, carry):
        here = pl.ds(pl.multiple_of(index * step, step), step)
        g = grad[here, :].astype(F32)
        total = None
        for k in range(streams):
            e = earlier[k, here, :].astype(F32)
            out_grad[k, here, :] = (mix[k] * g).astype(BF16)
            out_mix[k : k + 1, :] += jnp.sum(e * g, axis=0, keepdims=True)
            total = mix[k] * e if total is None else total + mix[k] * e
        out_prev[here, :] = total
        return carry

    lax.fori_loop(0, rows // step, one, 0)


def full_rows(pieces, first, last):
    total = None
    for piece in pieces:
        term = piece[first:last, :].astype(F32)
        total = term if total is None else total + term
    return total


def qkv_kernel(hps, batches, has_x, offset, *refs):
    if has_x:
        scalars, x, cosine, sine, w0, w1, w2, w3 = refs[:8]
        out, n1t, norms, weight = refs[8:]
        rows = n1t.shape[0] // 4
        parts = full_rows((w0, w1, w2, w3), rows, rows + 16)
        norms[...] = parts[0:8, :] + parts[8:16, :]
        v = x[...].astype(F32)
        center = v - jnp.mean(v, axis=-1, keepdims=True)
        inv = lax.rsqrt(jnp.mean(center * center, axis=-1, keepdims=True) + 1e-05)
        n1 = center * inv * norms[0:1, :] + norms[1:2, :]
        n1t[...] = n1.astype(BF16).T
    else:
        scalars, n1t, cosine, sine, w0, w1, w2, w3 = refs[:8]
        out, weight = refs[8:]
        rows = n1t.shape[0] // 4
    for order, piece in enumerate((w0, w1, w2, w3)):
        start = pl.multiple_of(block_index(scalars, order) * rows, rows)
        weight[pl.ds(start, rows), :] = piece[offset : offset + rows, :]
    width = weight.shape[1] // 3
    size = width // hps
    half = size // 2
    tokens = n1t.shape[1] // batches
    for part in range(3):
        cols = mm(weight[:, part * width : (part + 1) * width], n1t[...], 0, 0)
        for head in range(hps):
            for batch in range(batches):
                lanes = slice(batch * tokens, (batch + 1) * tokens)
                top = cols[head * size : head * size + half, lanes]
                low = cols[head * size + half : (head + 1) * size, lanes]
                if part < 2:
                    c = cosine[batch]
                    s = sine[batch]
                    top, low = top * c - low * s, low * c + top * s
                slot = batch * hps + head
                out[slot, part * size : part * size + half, :] = top.astype(BF16)
                out[slot, part * size + half : (part + 1) * size, :] = low.astype(BF16)


def stream_tile(count, stream, step):
    long = count - stream
    late = step >= long
    query = jnp.where(late, stream, count - 1 - stream)
    return query, jnp.where(late, step - long, step)


def attend_kernel(count, scale, ids, ins, outs, ot, lse, qt, kk, vt, scores, *states):
    streams = count // 2
    tops, totals, accs = states[:streams], states[streams : 2 * streams], states[2 * streams :]
    size = qt.shape[1]
    factor = scale * LOG2E
    for d in range(count):
        slot = ids[d]
        qt[slot] = ins[d, 0:size, :]
        kk[slot] = ins[d, size : 2 * size, :].T
        vt[slot] = ins[d, 2 * size :, :]
    for r in range(streams):
        tops[r][...] = jnp.full_like(tops[r], -1e30)
        totals[r][...] = jnp.zeros_like(totals[r])
        accs[r][...] = jnp.zeros_like(accs[r])
        scores[0, r] = mm(kk[0], qt[count - 1 - r], 1, 0)

    def step(index, carry):
        for r in range(streams):
            i, j = stream_tile(count, r, jnp.minimum(index + 1, count))
            scores[(index + 1) % 2, r] = mm(kk[j], qt[i], 1, 0)
        for r in range(streams):
            i, j = stream_tile(count, r, index)
            half = jnp.where(index >= count - r, 1, 0)
            s = scores[index % 2, r]
            old = tops[r][half]
            new = jnp.maximum(old, jnp.max(s, axis=0, keepdims=True) * factor)
            shrink = jnp.exp2(old - new)
            p = jnp.exp2(s * factor - new)
            totals[r][half] = totals[r][half] * shrink + jnp.sum(p, axis=0, keepdims=True)
            accs[r][half] = accs[r][half] * shrink + mm(vt[j], p.astype(BF16), 1, 0)
            tops[r][half] = new
        return carry

    lax.fori_loop(0, count + 1, step, 0)
    for r in range(streams):
        for half, i in enumerate((count - 1 - r, r)):
            run = totals[r][half]
            ot[i] = accs[r][half] / run
            lse[i] = tops[r][half] + jnp.log2(run)
    for d in range(count):
        outs[d] = ot[ids[d]].astype(BF16)


def attend_back_kernel(
    count, scale, stage, ids, ins, grads, ot, lse, outs, qt, qq, kt, kk, vv, gt, gg, delta, scores, gains, *sums
):
    streams = count // 2
    dqs, dks, dvs = sums[:streams], sums[streams : 2 * streams], sums[2 * streams :]
    size = qt.shape[1]
    factor = scale * LOG2E
    for d in range(count):
        slot = ids[d]
        block = ins[d]
        q = block[0:size]
        k = block[size : 2 * size]
        qt[slot] = q
        kt[slot] = k
        qq[slot] = q.T
        kk[slot] = k.T
        vv[slot] = block[2 * size :].T
        g = grads[d, stage * size : (stage + 1) * size, :]
        gt[slot] = g
        gg[slot] = g.T
        delta[slot] = jnp.sum(g.astype(F32) * ot[slot], axis=0, keepdims=True)
    for r in range(streams):
        dqs[r][...] = jnp.zeros_like(dqs[r])
        dks[r][...] = jnp.zeros_like(dks[r])
        dvs[r][...] = jnp.zeros_like(dvs[r])
        scores[0, r] = mm(kk[0], qt[count - 1 - r], 1, 0)
        gains[0, r] = mm(vv[0], gt[count - 1 - r], 1, 0)

    def step(index, carry):
        for r in range(streams):
            i, j = stream_tile(count, r, jnp.minimum(index + 1, count))
            scores[(index + 1) % 2, r] = mm(kk[j], qt[i], 1, 0)
            gains[(index + 1) % 2, r] = mm(vv[j], gt[i], 1, 0)
        for r in range(streams):
            i, j = stream_tile(count, r, index)
            half = jnp.where(index >= count - r, 1, 0)
            p = jnp.exp2(scores[index % 2, r] * factor - lse[i])
            ds = (p * (gains[index % 2, r] - delta[i])).astype(BF16)
            dqs[r][half] += mm(kt[j], ds, 1, 0)
            dks[r][j] += mm(ds, qq[i], 1, 0)
            dvs[r][j] += mm(p.astype(BF16), gg[i], 1, 0)
        return carry

    lax.fori_loop(0, count + 1, step, 0)
    for r in range(streams):
        for half, i in enumerate((count - 1 - r, r)):
            qt[i] = (dqs[r][half] * scale).astype(BF16)
    for d in range(count):
        slot = ids[d]
        outs[d, 0:size, :] = qt[slot]
        dk = dks[0][slot]
        dv = dvs[0][slot]
        for r in range(1, streams):
            dk = dk + dks[r][slot]
            dv = dv + dvs[r][slot]
        outs[d, size : 2 * size, :] = (dk * scale).astype(BF16).T
        outs[d, 2 * size :, :] = dv.astype(BF16).T


def gather_rows(scalars, pieces, window, target, sems, base):
    copies = []
    first, rows = window
    for order, piece in enumerate(pieces):
        start = pl.multiple_of(block_index(scalars, order) * rows, rows)
        copy = pltpu.make_async_copy(
            piece.at[pl.ds(first, rows), :], target.at[pl.ds(start, rows), :], sems.at[base + order]
        )
        copy.start()
        copies.append(copy)
    return copies


def mlp_kernel(count, stages, hps, batches, scalars, mix, x, grad, norms, *refs):
    heads = refs[0]
    pieces = refs[1:5]
    refs = refs[5:]
    hidden, dhidden, n2_out, mid_out, dmid_out, dmid_low, ot, norm_grads = refs[:8]
    head_grads = refs[8]
    out_scr, up_scr, down_scr, dn2, got, sems = refs[9:]
    width = x.shape[1]
    size = ot.shape[2]
    share = width // 4
    groups = up_scr.shape[1] // width
    deep = down_scr.shape[0] // 4
    last = (groups * share) + deep
    copies_out = gather_rows(scalars, pieces, (last, share), out_scr, sems, 0)
    copies_up = []
    for group in range(groups):
        lanes = up_scr.at[:, pl.ds(group * width, width)]
        copies_up += gather_rows(scalars, pieces, (group * share, share), lanes, sems, 4 + 4 * group)
    copies_down = gather_rows(
        scalars, pieces, (groups * share, deep), down_scr, sems, 4 + 4 * groups
    )
    for stage in range(stages):
        for slot in range(count):
            ot[slot // hps, stage * hps + slot % hps] = heads[
                slot, stage * size : (stage + 1) * size, :
            ]
    for copy in copies_out:
        copy.wait()
    tokens = x.shape[0] // batches
    for batch in range(batches):
        rows = slice(batch * tokens, (batch + 1) * tokens)
        attended = ot[batch].reshape(width, tokens)
        middle = x[rows, :].astype(F32) + mm(attended, out_scr[...], 0, 0)
        mid_out[rows, :] = middle
        center = middle - jnp.mean(middle, axis=-1, keepdims=True)
        inv = lax.rsqrt(jnp.mean(center * center, axis=-1, keepdims=True) + 1e-05)
        n2_out[rows, :] = (center * inv * norms[2:3, :] + norms[3:4, :]).astype(BF16)
    for copy in copies_up + copies_down:
        copy.wait()
    dn2[...] = jnp.zeros_like(dn2)
    dy = (mix[mix.shape[0] - 1] * grad[...].astype(F32)).astype(BF16)
    step = 512 if up_scr.shape[1] % 512 == 0 else 128

    def one(index, carry):
        here = pl.ds(pl.multiple_of(index * step, step), step)
        up = up_scr[:, here]
        u = mm(n2_out[...], up, 1, 0)
        da = mm(dy, down_scr[here, :], 1, 1)
        square = u * u
        bend = jnp.tanh(u * (GELU_C + (GELU_C * GELU_A) * square))
        gate = 0.5 + 0.5 * bend
        hidden[:, here] = (u * gate).astype(BF16)
        slope = gate + (0.5 * u) * (1.0 - bend * bend) * (
            GELU_C + (3.0 * GELU_C * GELU_A) * square
        )
        du = (da * slope).astype(BF16)
        dhidden[:, here] = du
        dn2[...] += mm(du, up, 1, 1)
        return carry

    lax.fori_loop(0, up_scr.shape[1] // step, one, 0)
    gain_sum = None
    for batch in range(batches):
        rows = slice(batch * tokens, (batch + 1) * tokens)
        middle = mid_out[rows, :]
        center = middle - jnp.mean(middle, axis=-1, keepdims=True)
        inv = lax.rsqrt(jnp.mean(center * center, axis=-1, keepdims=True) + 1e-05)
        z = center * inv
        dn = dn2[rows, :]
        part_gain = jnp.sum(dn * z, axis=0, keepdims=True)
        part_bias = jnp.sum(dn, axis=0, keepdims=True)
        gain_sum = part_gain if gain_sum is None else gain_sum + part_gain
        bias_sum = part_bias if batch == 0 else bias_sum + part_bias
        h = dn * norms[2:3, :]
        back = inv * (
            h - jnp.mean(h, axis=-1, keepdims=True) - z * jnp.mean(h * z, axis=-1, keepdims=True)
        )
        dmid = mix[mix.shape[0] - 1] * grad[rows, :].astype(F32) + back
        dmid_out[rows, :] = dmid
        low = dmid.astype(BF16)
        dmid_low[rows, :] = low
        got[batch] = mm(out_scr[...], low, 1, 1).astype(BF16).reshape(got.shape[1:])
    norm_grads[...] = jnp.zeros_like(norm_grads)
    norm_grads[0:1, :] = gain_sum
    norm_grads[1:2, :] = bias_sum
    for stage in range(stages):
        for slot in range(count):
            head_grads[slot, stage * size : (stage + 1) * size, :] = got[
                slot // hps, stage * hps + slot % hps
            ]


def result_kernel(window, scalars, mix, hidden, mid, prev, grad, w0, w1, w2, w3, out, out_mix, acc):
    acc[...] = mid[...]
    first, rows = window
    for order, piece in enumerate((w0, w1, w2, w3)):
        start = pl.multiple_of(block_index(scalars, order) * rows, rows)
        acc[...] += mm(hidden[:, pl.ds(start, rows)], piece[first : first + rows, :], 1, 0)
    y = acc[...]
    out[...] = (prev[...] + mix[mix.shape[0] - 1] * y).astype(BF16)
    out_mix[...] = jnp.zeros_like(out_mix)
    out_mix[0:1, :] = jnp.sum(grad[...].astype(F32) * y, axis=0, keepdims=True)


def put_pieces(me, value, outs, order, count, first):
    target = outs[order // 2]
    rows = value.shape[0] // count
    low = value.astype(BF16)
    for sub in range(count):
        slot = lax.bitwise_xor(me, jnp.int32(sub))
        target[order % 2, lax.rem(slot, jnp.int32(2)), lax.div(slot, jnp.int32(2)), first : first + rows, :] = (
            low[sub * rows : (sub + 1) * rows, :]
        )


def down_grad_kernel(count, scalars, mix, hidden, grad, keep, send):
    dy = (mix[mix.shape[0] - 1] * grad[...].astype(F32)).astype(BF16)
    rows = count * keep.shape[3]
    for order in range(4):
        start = pl.multiple_of(block_index(scalars, order) * rows, rows)
        value = mm(hidden[:, pl.ds(start, rows)], dy, 0, 0)
        put_pieces(scalars[0], value, (keep, send), order, count, 0)


def up_out_grad_kernel(count, scalars, n2, dhidden, ot, dmid, keep, send, left, whole):
    batches = ot.shape[0]
    width = n2.shape[1]
    tokens = ot.shape[3]
    rows = width // 4
    thin = rows // count

    def arrange():
        for order in range(4):
            here = pl.ds(pl.multiple_of(block_index(scalars, order) * rows, rows), rows)
            left[order * rows : (order + 1) * rows, :] = whole[here, :]

    whole[...] = n2[...].T
    arrange()
    groups = dhidden.shape[1] // width
    for group in range(groups):
        value = mm(left[...], dhidden[:, group * width : (group + 1) * width], 1, 0)
        for order in range(4):
            put_pieces(
                scalars[0],
                value[order * rows : (order + 1) * rows, :],
                (keep, send),
                order,
                count,
                group * thin,
            )
    for batch in range(batches):
        whole[:, batch * tokens : (batch + 1) * tokens] = ot[batch].reshape(width, tokens)
    arrange()
    value = mm(left[...], dmid[...], 1, 0)
    for order in range(4):
        put_pieces(
            scalars[0],
            value[order * rows : (order + 1) * rows, :],
            (keep, send),
            order,
            count,
            groups * thin,
        )


def grads_kernel(count, window, scalars, mix, hidden, mid, prev, grad, w0, w1, w2, w3, n2, dhidden, ot, dmid, *refs):
    down, up, (out, out_mix), (acc, left, whole) = refs[:2], refs[2:4], refs[4:6], refs[6:]
    down_grad_kernel(count, scalars, mix, hidden, grad, *down)
    up_out_grad_kernel(count, scalars, n2, dhidden, ot, dmid, *up, left, whole)
    result_kernel(window, scalars, mix, hidden, mid, prev, grad, w0, w1, w2, w3, out, out_mix, acc)


def in_grad_kernel(count, hps, natural, scalars, cosine, sine, n1t, *refs):
    stages = (len(refs) - 3) // 2
    dts = refs[stages : 2 * stages]
    keep, send, left = refs[2 * stages :]
    batches = dts[0].shape[0]
    size = dts[0].shape[3]
    half = size // 2
    tokens = dts[0].shape[4]
    width = n1t.shape[0]
    rows = width // 4
    thin = rows // count
    for order in range(4):
        here = pl.ds(pl.multiple_of(block_index(scalars, order) * rows, rows), rows)
        left[order * rows : (order + 1) * rows, :] = n1t[here, :]
    cols = 3 * hps * size
    for stage in range(stages):
        grads = refs[stage]
        dt = dts[stage]
        for slot in range(count):
            batch, head = slot // hps, slot % hps
            c = cosine[batch]
            s = sine[batch]
            for part in range(2):
                top = grads[slot, part * size : part * size + half, :].astype(F32)
                low = grads[slot, part * size + half : (part + 1) * size, :].astype(F32)
                dt[batch, part, head, 0:half, :] = (top * c + low * s).astype(BF16)
                dt[batch, part, head, half:size, :] = (low * c - top * s).astype(BF16)
            dt[batch, 2, head] = grads[slot, 2 * size :, :]
        value = None
        for batch in range(batches):
            term = mm(
                left[:, batch * tokens : (batch + 1) * tokens],
                dt[batch].reshape(cols, tokens),
                1,
                1,
            )
            value = term if value is None else value + term
        low = value.astype(BF16)
        for order in range(4):
            if natural:
                target = (keep, send)[order // 2]
                for sub in range(count):
                    start = order * rows + sub * thin
                    target[order % 2, sub] = low[start : start + thin, :]
            else:
                put_pieces(
                    scalars[0],
                    low[order * rows : (order + 1) * rows, :],
                    (keep, send),
                    order,
                    count,
                    stage * thin,
                )


def input_grad_kernel(stages, windows, scalars, x, norms, dmid, *refs):
    dts = refs[:stages]
    pieces = refs[stages : stages + 4 * stages]
    out, norm_grads, weights, sems = refs[5 * stages :]
    copies = []
    for stage in range(stages):
        copies += gather_rows(
            scalars,
            pieces[4 * stage : 4 * stage + 4],
            windows[stage],
            weights.at[stage],
            sems,
            4 * stage,
        )
    for copy in copies:
        copy.wait()
    batches = dts[0].shape[0]
    tokens = dts[0].shape[4]
    cols = weights.shape[2]
    gain_sum = bias_sum = None
    for batch in range(batches):
        rows = slice(batch * tokens, (batch + 1) * tokens)
        dnt = None
        for stage in range(stages):
            term = mm(weights[stage], dts[stage][batch].reshape(cols, tokens), 1, 0)
            dnt = term if dnt is None else dnt + term
        dn = dnt.T
        v = x[rows, :].astype(F32)
        center = v - jnp.mean(v, axis=-1, keepdims=True)
        inv = lax.rsqrt(jnp.mean(center * center, axis=-1, keepdims=True) + 1e-05)
        z = center * inv
        part_gain = jnp.sum(dn * z, axis=0, keepdims=True)
        part_bias = jnp.sum(dn, axis=0, keepdims=True)
        gain_sum = part_gain if batch == 0 else gain_sum + part_gain
        bias_sum = part_bias if batch == 0 else bias_sum + part_bias
        h = dn * norms[0:1, :]
        back = inv * (
            h - jnp.mean(h, axis=-1, keepdims=True) - z * jnp.mean(h * z, axis=-1, keepdims=True)
        )
        out[rows, :] = (dmid[rows, :] + back).astype(BF16)
    norm_grads[...] = jnp.zeros_like(norm_grads)
    norm_grads[0:1, :] = gain_sum
    norm_grads[1:2, :] = bias_sum


def turned(index, count):
    result = 0
    while count > 1:
        result = 2 * result + index % 2
        index //= 2
        count //= 2
    return result


def place_kernel(moves, scalars, near, far, *outs):
    count = near.shape[0]
    for side, source in enumerate((near, far)):
        for sub in range(count):
            slot = lax.bitwise_xor(scalars[0], jnp.int32(2 * turned(sub, count) + side))
            for out, first, rows, begin, wide, to in moves:
                outs[out][slot, :, to : to + wide] = source[
                    sub, first : first + rows, begin : begin + wide
                ].astype(F32)


def place_in_kernel(moves, width, wide, thin, scalars, near, far, last, out):
    place_kernel(moves, scalars, near, far, out)
    final = len(moves) // 3
    for sub in range(last.shape[0]):
        for part in range(3):
            to = part * width + final * wide
            out[sub, :, to : to + wide] = last[sub, :, part * wide : (part + 1) * wide].astype(F32)


def exchange(value, axis, bit):
    size = lax.axis_size(axis)
    return lax.ppermute(value, axis, [(i, i ^ bit) for i in range(size)])


def added(left, right):
    return (left.astype(F32) + right.astype(F32)).astype(BF16)


def swapped(value, groups=None):
    return lax.all_to_all(value, "ctx", 0, 0, axis_index_groups=groups)


def summed(value):
    return jnp.sum(value.astype(F32), axis=0).astype(BF16)


def spread(own, count, groups=None):
    return swapped(jnp.broadcast_to(own[None], (count, *own.shape)), groups)


def total(terms):
    value = terms[0].astype(F32)
    for term in terms[1:]:
        value = value + term.astype(F32)
    return value.astype(BF16)


def reduce_blocks(keep, send, order):
    count = lax.axis_size("ctx")
    labels = ["x", 1]
    bit = count // 2
    while bit > 1:
        labels.append(bit)
        bit //= 2
    dims = (2,) * len(labels) + keep.shape[3:]
    terms = [keep.reshape(dims), exchange(send, "fsdp", 1).reshape(dims)]
    sent = []
    for label in order:
        axis = labels.index(label)
        sent.append(total([lax.index_in_dim(t, 1, axis, keepdims=False) for t in terms]))
        got = exchange(sent[-1], *(("fsdp", 2) if label == "x" else ("ctx", label)))
        terms = [lax.index_in_dim(t, 0, axis, keepdims=False) for t in terms] + [got]
        labels.pop(axis)
    return total(terms), sent


def gather_blocks(own):
    held = own[None]
    bit = lax.axis_size("ctx") // 2
    while bit > 1:
        held = jnp.concatenate([held, exchange(held, "ctx", bit)])
        bit //= 2
    return held, exchange(held, "ctx", 1)


def halved(keep, send):
    got = exchange(send, "fsdp", 1)
    passed = added(keep[1], got[1])
    return total([keep[0], got[0], exchange(passed, "fsdp", 2)])


def reduce_whole(keep, send):
    return spread(summed(swapped(halved(keep, send))), lax.axis_size("ctx"))


def after(value, *others):
    return lax.optimization_barrier((value, *others))[0]


def gathered(shard):
    other_chip = exchange(shard, "fsdp", 2)
    return [shard, other_chip, exchange(shard, "fsdp", 1), exchange(other_chip, "fsdp", 1)]


def head_body(
    inputs,
    earlier,
    input_proj,
    output_proj,
    up_proj,
    down_proj,
    norm1_gain,
    norm1_bias,
    norm2_gain,
    norm2_bias,
    mixing,
    block_order,
    grad_next,
):
    batches, tokens, width = inputs.shape
    rows = batches * tokens
    heads = HEADS
    size = width // heads
    scale = size ** (-0.5)
    streams = earlier.shape[0]
    count = lax.axis_size("ctx")
    hps = count // batches
    stages = heads // hps
    inner = down_proj.shape[0] * 4
    me = lax.axis_index("ctx").astype(jnp.int32)
    place = lax.axis_index("fsdp").astype(jnp.int32)
    scalars = jnp.stack([me, place])
    ids = block_order[me // hps].astype(jnp.int32)
    x = inputs.reshape(rows, width)
    grad = grad_next.reshape(rows, width)

    share = width // 4
    cols = 3 * hps * size
    norm_stack = jnp.stack([norm1_gain, norm1_bias, norm2_gain, norm2_bias])
    coarse = lax.reduce_precision(norm_stack, 8, 7)
    norm_rows = jnp.zeros((16, width), BF16)
    norm_rows = lax.dynamic_update_slice(norm_rows, coarse.astype(BF16), (0, place * share))
    norm_rows = lax.dynamic_update_slice(
        norm_rows, (norm_stack - coarse).astype(BF16), (8, place * share)
    )
    wide = hps * size
    chunks = [
        jnp.concatenate(
            [input_proj[:, p * width + s * wide : p * width + (s + 1) * wide] for p in range(3)], 1
        )
        for s in range(stages)
    ]
    first_in = gathered(jnp.concatenate([chunks[0], jnp.pad(norm_rows, ((0, 0), (0, cols - width)))]))
    rest_in = gathered(after(jnp.concatenate(chunks[1:]), first_in[1]))
    groups = inner // width
    up_rows = jnp.moveaxis(up_proj.reshape(share, groups, width), 1, 0).reshape(-1, width)
    packed = jnp.concatenate([up_rows, down_proj, output_proj])

    half = size // 2
    own_blocks = block_order[:, me]
    positions = (own_blocks[:, None] * tokens + lax.iota(jnp.int32, tokens)[None]).astype(F32)
    freqs = jnp.exp(lax.iota(F32, half) * (-2.0 * math.log(10000.0) / size))
    angle = freqs[None, :, None] * positions[:, None, :]
    cosine = jnp.cos(angle)
    sine = jnp.sin(angle)

    grad_earlier, prev, mix_early = run_kernel(
        early_kernel,
        "early",
        [mixing, earlier.reshape(streams, rows, width), grad],
        [SMEM, VMEM, VMEM],
        [
            shape_of((streams, rows, width), BF16),
            shape_of((rows, width), F32),
            shape_of((8, width), F32),
        ],
        [],
        6 * streams * rows * width,
    )

    pair_shape = shape_of((count, 3 * size, tokens), BF16)
    x = after(x, mix_early)
    packed = after(packed, rest_in[1])
    weights = [packed, exchange(packed, "fsdp", 2), exchange(packed, "fsdp", 1)]
    made = []
    n1t = norms = None
    windows = [(0, share)] + [(share * s, share) for s in range(stages - 1)]
    for s in range(stages):
        first = s == 0
        operands = [scalars] + ([x] if first else [n1t]) + [cosine, sine]
        operands += first_in if first else rest_in
        outs = [pair_shape]
        if first:
            outs += [shape_of((width, rows), BF16), shape_of((8, width), F32)]
        result = run_kernel(
            functools.partial(qkv_kernel, hps, batches, first, windows[s][0]),
            "qkv",
            operands,
            [SMEM] + [VMEM] * (len(operands) - 1),
            outs,
            [pltpu.VMEM((width, cols), BF16)],
            2 * rows * width * cols,
        )
        if first:
            n1t, norms = result[1:]
        made.append(result[0])

    tiles = count * (count + 1) // 2
    one = tokens * tokens * size * 2
    streams_in = count // 2
    head_shape = shape_of((count, size, tokens), BF16)
    held = []
    attended = []
    saved = []
    for s in range(stages):
        while len(held) < min(s + 2, stages):
            held.append(swapped(after(made[len(held)], *([saved[-1][1]] if saved else []))))
        result = run_kernel(
            functools.partial(attend_kernel, count, scale),
            "attend",
            [after(ids, saved[-1][1]) if saved else ids, held[s]],
            [SMEM, VMEM],
            [head_shape, shape_of((count, size, tokens), F32), shape_of((count, 1, tokens), F32)],
            [
                pltpu.VMEM((count, size, tokens), BF16),
                pltpu.VMEM((count, tokens, size), BF16),
                pltpu.VMEM((count, size, tokens), BF16),
                pltpu.VMEM((2, streams_in, tokens, tokens), F32),
            ]
            + [pltpu.VMEM((2, 1, tokens), F32)] * (2 * streams_in)
            + [pltpu.VMEM((2, size, tokens), F32)] * streams_in,
            4 * 2 * one * tiles,
        )
        saved.append(result[1:])
        attended.append(result[0])

    weights.append(exchange(after(weights[1], saved[-2][1]), "fsdp", 1))
    result = run_kernel(
        functools.partial(mlp_kernel, count, stages, hps, batches),
        "mlp",
        [scalars, mixing, x, grad, norms, swapped(jnp.concatenate(attended, axis=1))] + weights,
        [SMEM, SMEM, VMEM, VMEM, VMEM, VMEM] + [ANY] * 4,
        [
            shape_of((rows, inner), BF16),
            shape_of((rows, inner), BF16),
            shape_of((rows, width), BF16),
            shape_of((rows, width), F32),
            shape_of((rows, width), F32),
            shape_of((rows, width), BF16),
            shape_of((batches, heads, size, tokens), BF16),
            shape_of((8, width), F32),
            shape_of((count, stages * size, tokens), BF16),
        ],
        [
            pltpu.VMEM((width, width), BF16),
            pltpu.VMEM((width, inner), BF16),
            pltpu.VMEM((inner, width), BF16),
            pltpu.VMEM((rows, width), F32),
            pltpu.VMEM((batches, heads, size, tokens), BF16),
            pltpu.SemaphoreType.DMA((8 + 4 * groups,)),
        ],
        6 * rows * width * inner,
    )
    hidden, dhidden, n2, mid, dmid, dmid_low, ot, norm2_grads = result[:8]
    head_grads = swapped(result[8])

    sub = inner // 4 // count
    thin = share // count
    result = run_kernel(
        functools.partial(grads_kernel, count, (groups * share, inner // 4)),
        "grads",
        [scalars, mixing, hidden, mid, prev, grad] + weights + [n2, dhidden, ot, dmid_low],
        [SMEM, SMEM] + [VMEM] * 12,
        [shape_of((2, 2, count // 2, sub, width), BF16)] * 2
        + [shape_of((2, 2, count // 2, thin * (groups + 1), width), BF16)] * 2
        + [shape_of((rows, width), BF16), shape_of((8, width), F32)],
        [
            pltpu.VMEM((rows, width), F32),
            pltpu.VMEM((width, rows), BF16),
            pltpu.VMEM((width, rows), BF16),
        ],
        2 * rows * width * (3 * inner + width),
    )
    down_sums, up_sums, (next_input, mix_last) = result[:2], result[2:4], result[4:]

    def in_grads(arrived, natural):
        few = len(arrived)
        lead = (2, count, thin) if natural else (2, 2, count // 2, few * thin)
        result = run_kernel(
            functools.partial(in_grad_kernel, count, hps, natural),
            "in_grad",
            [scalars, cosine, sine, n1t] + arrived,
            [SMEM] + [VMEM] * (3 + few),
            [shape_of((batches, 3, hps, size, tokens), BF16)] * few
            + [shape_of((*lead, cols), BF16)] * 2,
            [pltpu.VMEM((width, rows), BF16)],
            2 * few * rows * width * cols,
        )
        return list(result[:few]), result[few:]

    far_bits = [1 << k for k in range(1, count.bit_length() - 1)]
    down_own, down_sent = reduce_blocks(*down_sums, ["x", 1] + far_bits)
    up_own, up_sent = reduce_blocks(*up_sums, [1, "x"] + far_bits)
    down_parts = gather_blocks(down_own)
    up_parts = gather_blocks(up_own)

    dts = []
    back = [mix_last]
    moved = []
    ready = {0: (down_sent[0], up_sent[0]), stages - 1: ()}
    for s in range(stages):
        if s == stages - 1:
            ready[s] += (moved[0],)
        (value,) = run_kernel(
            functools.partial(attend_back_kernel, count, scale, s),
            "attend_back",
            [ids, after(held[s], back[-1], *ready.get(s, ())), head_grads] + list(saved[s]),
            [SMEM] + [VMEM] * 4,
            [pair_shape],
            [
                pltpu.VMEM((count, size, tokens), BF16),
                pltpu.VMEM((count, tokens, size), BF16),
                pltpu.VMEM((count, size, tokens), BF16),
                pltpu.VMEM((count, tokens, size), BF16),
                pltpu.VMEM((count, tokens, size), BF16),
                pltpu.VMEM((count, size, tokens), BF16),
                pltpu.VMEM((count, tokens, size), BF16),
                pltpu.VMEM((count, 1, tokens), F32),
                pltpu.VMEM((2, streams_in, tokens, tokens), F32),
                pltpu.VMEM((2, streams_in, tokens, tokens), F32),
            ]
            + [pltpu.VMEM((2, size, tokens), F32)] * streams_in
            + [pltpu.VMEM((count, tokens, size), F32)] * (2 * streams_in),
            4 * 5 * one * tiles,
        )
        back.append(value)
        moved.append(swapped(value))
    early_dts, early_sums = in_grads([after(moved[0], back[-1])] + moved[1:-1], False)
    last_dts, last_sums = in_grads(moved[-1:], True)
    dts = early_dts + last_dts
    early_own, early_sent = reduce_blocks(*early_sums, ["x", 1] + far_bits)
    early_parts = gather_blocks(early_own)
    last_parts = reduce_whole(*last_sums)

    grad_input, norm1_grads = run_kernel(
        functools.partial(input_grad_kernel, stages, windows),
        "input_grad",
        [scalars, x, norms, dmid] + dts + first_in + rest_in * (stages - 1),
        [SMEM] + [VMEM] * (3 + stages) + [ANY] * (4 * stages),
        [shape_of((rows, width), BF16), shape_of((8, width), F32)],
        [pltpu.VMEM((stages, width, cols), BF16), pltpu.SemaphoreType.DMA((4 * stages,))],
        2 * rows * width * 3 * width,
    )

    small = jnp.concatenate(
        [norm1_grads[:2], norm2_grads[:2], mix_early[:streams], mix_last[:1]], axis=0
    )
    small = small + exchange(small, "fsdp", 1)
    small = small + exchange(small, "fsdp", 2)
    for bit in [1] + far_bits:
        small = small + exchange(small, "ctx", bit)
    norm_total = lax.dynamic_slice_in_dim(small[:4], place * share, share, 1)
    mix_total = jnp.sum(small[4:], axis=1)

    (grad_down,) = run_kernel(
        functools.partial(place_kernel, ((0, 0, sub, 0, width, 0),)),
        "place_down",
        [scalars, *down_parts],
        [SMEM] + [VMEM] * 2,
        [shape_of((count, sub, width), F32)],
        [],
        0,
    )
    moves = tuple((0, g * thin, thin, 0, width, g * width) for g in range(groups))
    grad_up, grad_out = run_kernel(
        functools.partial(place_kernel, moves + ((1, groups * thin, thin, 0, width, 0),)),
        "place_up",
        [scalars, *up_parts],
        [SMEM] + [VMEM] * 2,
        [shape_of((count, thin, inner), F32), shape_of((count, thin, width), F32)],
        [],
        0,
    )
    wide = hps * size
    moves = tuple(
        (0, g * thin, thin, part * wide, wide, part * width + g * wide)
        for g in range(stages - 1)
        for part in range(3)
    )
    (grad_in,) = run_kernel(
        functools.partial(place_in_kernel, moves, width, wide, thin),
        "place_in",
        [scalars, *early_parts, last_parts],
        [SMEM] + [VMEM] * 3,
        [shape_of((count, thin, 3 * width), F32)],
        [],
        0,
    )
    return (
        next_input.reshape(batches, tokens, width),
        grad_input.reshape(batches, tokens, width),
        grad_earlier.reshape(streams, batches, tokens, width),
        grad_in.reshape(share, 3 * width),
        grad_out.reshape(share, width),
        grad_up.reshape(share, inner),
        grad_down.reshape(inner // 4, width),
        norm_total[0],
        norm_total[1],
        norm_total[2],
        norm_total[3],
        mix_total,
    )


def heads_fit(batches):
    count = lax.axis_size("ctx")
    return (
        lax.axis_size("fsdp") == 4
        and count & (count - 1) == 0
        and count % batches == 0
        and HEADS % max(count // batches, 1) == 0
    )


def either_body(inputs, *rest):
    return (head_body if heads_fit(inputs.shape[0]) else body)(inputs, *rest)


def solution(mesh):
    placed = (
        P("fsdp", "ctx", None),
        P(None, "fsdp", "ctx", None),
        P("fsdp", None),
        P("fsdp", None),
        P("fsdp", None),
        P("fsdp", None),
        P("fsdp"),
        P("fsdp"),
        P("fsdp"),
        P("fsdp"),
        P(),
        P(),
        P("fsdp", "ctx", None),
    )
    return jax.shard_map(
        either_body,
        mesh=mesh,
        in_specs=placed,
        out_specs=(
            P("fsdp", "ctx", None),
            P("fsdp", "ctx", None),
            P(None, "fsdp", "ctx", None),
            P("fsdp", None),
            P("fsdp", None),
            P("fsdp", None),
            P("fsdp", None),
            P("fsdp"),
            P("fsdp"),
            P("fsdp"),
            P("fsdp"),
            P(),
        ),
        check_vma=False,
    )
```

```python
import functools
import math

import jax
import jax.numpy as jnp
from jax import lax
from jax.experimental import pallas as pl
from jax.experimental.pallas import tpu as pltpu
from jax.sharding import PartitionSpec as P

HEADS = 12


def passed_along(value, axis, steps):
    count = lax.axis_size(axis)
    pairs = [(source, (source + steps) % count) for source in range(count)]
    return lax.ppermute(value, axis, pairs)


def norm_parts(values, gain, bias):
    mean_value = jnp.mean(values, axis=-1, keepdims=True)
    centered = values - mean_value
    inv_std = lax.rsqrt(jnp.mean(centered * centered, axis=-1, keepdims=True) + 1e-05)
    normed = centered * inv_std
    return (normed * gain + bias, normed, inv_std)


def norm_back(grad_out, normed, inv_std, gain):
    scaled = grad_out * gain
    mean_one = jnp.mean(scaled, axis=-1, keepdims=True)
    mean_two = jnp.mean(scaled * normed, axis=-1, keepdims=True)
    return inv_std * (scaled - mean_one - normed * mean_two)


def rotary_tables(block_id, block_rows, head_dim):
    half_dim = head_dim // 2
    positions = (block_id * block_rows + lax.iota(jnp.int32, block_rows)).astype(jnp.float32)
    freqs = jnp.exp(lax.iota(jnp.float32, half_dim) * (-2.0 * math.log(10000.0) / head_dim))
    angle = positions[:, None] * freqs[None, :]
    return (jnp.cos(angle)[:, None, :], jnp.sin(angle)[:, None, :])


def rotate(values, cosine, sine_table):
    half_dim = values.shape[-1] // 2
    first_half = values[..., :half_dim]
    second_half = values[..., half_dim:]
    return jnp.concatenate(
        [
            first_half * cosine - second_half * sine_table,
            second_half * cosine + first_half * sine_table,
        ],
        axis=-1,
    )


def unrotate(grads, cosine, sine_table):
    half_dim = grads.shape[-1] // 2
    first_half = grads[..., :half_dim]
    second_half = grads[..., half_dim:]
    return jnp.concatenate(
        [
            first_half * cosine + second_half * sine_table,
            second_half * cosine - first_half * sine_table,
        ],
        axis=-1,
    )


def head_view(values, head_count):
    return values.reshape(values.shape[0], head_count, values.shape[1] // head_count)


def forward_visit(state, local_query, block_keys, block_values, head_count, score_scale):
    run_max, run_sum, accum = state
    query_heads = head_view(local_query, head_count)
    key_heads = head_view(block_keys, head_count)
    value_heads = head_view(block_values, head_count)
    scores = (
        jnp.einsum("qhe,khe->hqk", query_heads, key_heads, preferred_element_type=jnp.float32)
        * score_scale
    )
    new_max = jnp.maximum(run_max, jnp.max(scores, axis=-1))
    weights = jnp.exp(scores - new_max[:, :, None])
    factor = jnp.exp(run_max - new_max)
    new_sum = run_sum * factor + jnp.sum(weights, axis=-1)
    update = jnp.einsum(
        "hqk,khe->qhe",
        weights.astype(jnp.bfloat16),
        value_heads,
        preferred_element_type=jnp.float32,
    )
    return (new_max, new_sum, accum * jnp.transpose(factor)[:, :, None] + update)


def backward_pair(
    query_rows, key_rows, value_rows, grad_rows, log_total, row_delta, head_count, score_scale
):
    query_heads = head_view(query_rows, head_count)
    key_heads = head_view(key_rows, head_count)
    value_heads = head_view(value_rows, head_count)
    grad_heads = head_view(grad_rows, head_count)
    scores = (
        jnp.einsum("qhe,khe->hqk", query_heads, key_heads, preferred_element_type=jnp.float32)
        * score_scale
    )
    probs = jnp.exp(scores - log_total[:, :, None])
    grad_probs = jnp.einsum(
        "qhe,khe->hqk", grad_heads, value_heads, preferred_element_type=jnp.float32
    )
    grad_scores = (probs * (grad_probs - row_delta[:, :, None])).astype(jnp.bfloat16)
    grad_query = (
        jnp.einsum("hqk,khe->qhe", grad_scores, key_heads, preferred_element_type=jnp.float32)
        * score_scale
    )
    grad_keys = (
        jnp.einsum("hqk,qhe->khe", grad_scores, query_heads, preferred_element_type=jnp.float32)
        * score_scale
    )
    grad_values = jnp.einsum(
        "hqk,qhe->khe", probs.astype(jnp.bfloat16), grad_heads, preferred_element_type=jnp.float32
    )
    return (
        grad_query.reshape(query_rows.shape[0], -1),
        grad_keys.reshape(key_rows.shape[0], -1),
        grad_values.reshape(key_rows.shape[0], -1),
    )


def body(
    inputs,
    earlier,
    input_proj,
    output_proj,
    up_proj,
    down_proj,
    norm1_gain,
    norm1_bias,
    norm2_gain,
    norm2_bias,
    mixing,
    block_order,
    grad_next,
):
    head_count = HEADS
    batch_count = inputs.shape[0]
    block_rows = inputs.shape[1]
    model_width = inputs.shape[2]
    head_dim = model_width // head_count
    score_scale = head_dim ** (-0.5)
    stream_count = earlier.shape[0]
    cycle_size = lax.axis_size("ctx")
    cycle_place = lax.axis_index("ctx")
    norm_stack = jnp.stack([norm1_gain, norm1_bias, norm2_gain, norm2_bias])
    full_in, full_out, full_up, full_down, full_norms = (
        lax.all_gather(input_proj, "fsdp", axis=0, tiled=True),
        lax.all_gather(output_proj, "fsdp", axis=0, tiled=True),
        lax.all_gather(up_proj, "fsdp", axis=0, tiled=True),
        lax.all_gather(down_proj, "fsdp", axis=0, tiled=True),
        lax.all_gather(norm_stack.astype(jnp.bfloat16), "fsdp", axis=1, tiled=True).astype(
            norm_stack.dtype
        ),
    )
    gain_one = full_norms[0]
    bias_one = full_norms[1]
    gain_two = full_norms[2]
    bias_two = full_norms[3]
    next_list = []
    grad_in_list = []
    earlier_list = []
    totals = None
    for batch in range(batch_count):
        block_input = inputs[batch].astype(jnp.float32)
        order_row = block_order[batch]
        own_block = order_row[cycle_place]
        cosine, sine_table = rotary_tables(own_block, block_rows, head_dim)
        normed_in, normed_one, inv_one = norm_parts(block_input, gain_one, bias_one)
        normed_in_b = normed_in.astype(jnp.bfloat16)
        projected = jnp.dot(normed_in_b, full_in, preferred_element_type=jnp.float32)
        local_query = (
            rotate(head_view(projected[:, :model_width], head_count), cosine, sine_table)
            .reshape(block_rows, model_width)
            .astype(jnp.bfloat16)
        )
        local_keys = (
            rotate(
                head_view(projected[:, model_width : 2 * model_width], head_count),
                cosine,
                sine_table,
            )
            .reshape(block_rows, model_width)
            .astype(jnp.bfloat16)
        )
        local_values = projected[:, 2 * model_width :].astype(jnp.bfloat16)
        start_state = (
            jnp.full((head_count, block_rows), -1e30, jnp.float32),
            jnp.zeros((head_count, block_rows), jnp.float32),
            jnp.zeros((block_rows, head_count, head_dim), jnp.float32),
        )
        piece_keys = lax.all_gather(local_keys, "ctx", axis=0, tiled=True)
        piece_values = lax.all_gather(local_values, "ctx", axis=0, tiled=True)
        count = piece_keys.shape[0] // block_rows

        def one_block(index, state_now):
            block_keys = lax.dynamic_slice_in_dim(piece_keys, index * block_rows, block_rows, 0)
            block_values = lax.dynamic_slice_in_dim(piece_values, index * block_rows, block_rows, 0)
            return lax.cond(
                order_row[index] <= own_block,
                lambda held: forward_visit(
                    held, local_query, block_keys, block_values, head_count, score_scale
                ),
                lambda held: held,
                state_now,
            )

        run_max, run_sum, accum = lax.fori_loop(0, count, one_block, start_state)
        log_total = run_max + jnp.log(run_sum)
        attended = accum / jnp.transpose(run_sum)[:, :, None]
        attended_b = attended.reshape(block_rows, model_width).astype(jnp.bfloat16)
        middle = block_input + jnp.dot(attended_b, full_out, preferred_element_type=jnp.float32)
        normed_mid, normed_two, inv_two = norm_parts(middle, gain_two, bias_two)
        normed_mid_b = normed_mid.astype(jnp.bfloat16)
        hidden_pre = jnp.dot(normed_mid_b, full_up, preferred_element_type=jnp.float32)
        hidden_b = jax.nn.gelu(hidden_pre).astype(jnp.bfloat16)
        result = middle + jnp.dot(hidden_b, full_down, preferred_element_type=jnp.float32)
        previous = earlier[:, batch].astype(jnp.float32)
        mixed_out = (
            jnp.sum(mixing[:stream_count, None, None] * previous, axis=0)
            + mixing[stream_count] * result
        )
        next_list.append(mixed_out.astype(jnp.bfloat16))
        grad_out = grad_next[batch].astype(jnp.float32)
        earlier_list.append(
            (mixing[:stream_count, None, None] * grad_out[None]).astype(jnp.bfloat16)
        )
        mix_grad = jnp.concatenate(
            [jnp.sum(previous * grad_out[None], axis=(1, 2)), jnp.sum(result * grad_out)[None]]
        )
        grad_result = mixing[stream_count] * grad_out
        grad_result_b = grad_result.astype(jnp.bfloat16)
        grad_down = jnp.einsum(
            "rf,rd->fd", hidden_b, grad_result_b, preferred_element_type=jnp.float32
        )
        grad_hidden = jnp.einsum(
            "rd,fd->rf", grad_result_b, full_down, preferred_element_type=jnp.float32
        )
        grad_pre = jax.vjp(jax.nn.gelu, hidden_pre)[1](grad_hidden)[0]
        grad_pre_b = grad_pre.astype(jnp.bfloat16)
        grad_up = jnp.einsum(
            "rd,rf->df", normed_mid_b, grad_pre_b, preferred_element_type=jnp.float32
        )
        grad_norm_mid = jnp.einsum(
            "rf,df->rd", grad_pre_b, full_up, preferred_element_type=jnp.float32
        )
        grad_gain_two = jnp.sum(grad_norm_mid * normed_two, axis=0)
        grad_bias_two = jnp.sum(grad_norm_mid, axis=0)
        grad_middle = grad_result + norm_back(grad_norm_mid, normed_two, inv_two, gain_two)
        grad_middle_b = grad_middle.astype(jnp.bfloat16)
        grad_out_proj = jnp.einsum(
            "rd,re->de", attended_b, grad_middle_b, preferred_element_type=jnp.float32
        )
        grad_att_b = jnp.einsum(
            "re,de->rd", grad_middle_b, full_out, preferred_element_type=jnp.float32
        ).astype(jnp.bfloat16)
        row_delta = jnp.einsum(
            "qhe,qhe->hq", head_view(grad_att_b, head_count).astype(jnp.float32), attended
        )
        zero_rows = jnp.zeros((block_rows, model_width), jnp.float32)

        def key_visit(offset, grad_query, cycle_keys, cycle_values, cycle_dk, cycle_dv):
            their_block = order_row[(cycle_place - offset) % cycle_size]

            def add_pair(held):
                part_q, part_k, part_v = backward_pair(
                    local_query,
                    cycle_keys,
                    cycle_values,
                    grad_att_b,
                    log_total,
                    row_delta,
                    head_count,
                    score_scale,
                )
                return (held[0] + part_q, held[1] + part_k, held[2] + part_v)

            return lax.cond(
                their_block <= own_block,
                add_pair,
                lambda held: held,
                (grad_query, cycle_dk, cycle_dv),
            )

        def key_turn(offset, carry):
            grad_query, cycle_keys, cycle_values, cycle_dk, cycle_dv = carry
            grad_query, cycle_dk, cycle_dv = key_visit(
                offset, grad_query, cycle_keys, cycle_values, cycle_dk, cycle_dv
            )
            cycle_keys, cycle_values = passed_along((cycle_keys, cycle_values), "ctx", 1)
            cycle_dk, cycle_dv = (
                passed_along(cycle_dk.astype(jnp.bfloat16), "ctx", 1).astype(cycle_dk.dtype),
                passed_along(cycle_dv.astype(jnp.bfloat16), "ctx", 1).astype(cycle_dv.dtype),
            )
            return (grad_query, cycle_keys, cycle_values, cycle_dk, cycle_dv)

        grad_query, cycle_keys, cycle_values, cycle_dk, cycle_dv = lax.fori_loop(
            0, cycle_size - 1, key_turn, (zero_rows, local_keys, local_values, zero_rows, zero_rows)
        )
        grad_query, cycle_dk, cycle_dv = key_visit(
            cycle_size - 1, grad_query, cycle_keys, cycle_values, cycle_dk, cycle_dv
        )
        grad_keys, grad_values = (
            passed_along(cycle_dk.astype(jnp.bfloat16), "ctx", 1).astype(cycle_dk.dtype),
            passed_along(cycle_dv.astype(jnp.bfloat16), "ctx", 1).astype(cycle_dv.dtype),
        )
        grad_query_pre = unrotate(head_view(grad_query, head_count), cosine, sine_table).reshape(
            block_rows, model_width
        )
        grad_keys_pre = unrotate(head_view(grad_keys, head_count), cosine, sine_table).reshape(
            block_rows, model_width
        )
        grad_proj_b = jnp.concatenate([grad_query_pre, grad_keys_pre, grad_values], axis=1).astype(
            jnp.bfloat16
        )
        grad_in_proj = jnp.einsum(
            "rd,rf->df", normed_in_b, grad_proj_b, preferred_element_type=jnp.float32
        )
        grad_norm_in = jnp.einsum(
            "rf,df->rd", grad_proj_b, full_in, preferred_element_type=jnp.float32
        )
        grad_gain_one = jnp.sum(grad_norm_in * normed_one, axis=0)
        grad_bias_one = jnp.sum(grad_norm_in, axis=0)
        grad_block_in = grad_middle + norm_back(grad_norm_in, normed_one, inv_one, gain_one)
        grad_in_list.append(grad_block_in.astype(jnp.bfloat16))
        norm_grads = jnp.stack([grad_gain_one, grad_bias_one, grad_gain_two, grad_bias_two])
        mix_tiled = jnp.broadcast_to(mix_grad[None, :], (lax.axis_size("fsdp"), stream_count + 1))
        grad_terms = (grad_in_proj, grad_out_proj, grad_up, grad_down, norm_grads, mix_tiled)
        shares = (
            lax.psum_scatter(
                grad_terms[0].astype(jnp.bfloat16), "fsdp", scatter_dimension=0, tiled=True
            ).astype(jnp.float32),
            lax.psum_scatter(
                grad_terms[1].astype(jnp.bfloat16), "fsdp", scatter_dimension=0, tiled=True
            ).astype(jnp.float32),
            lax.psum_scatter(
                grad_terms[2].astype(jnp.bfloat16), "fsdp", scatter_dimension=0, tiled=True
            ).astype(jnp.float32),
            lax.psum_scatter(
                grad_terms[3].astype(jnp.bfloat16), "fsdp", scatter_dimension=0, tiled=True
            ).astype(jnp.float32),
            lax.psum_scatter(
                grad_terms[4].astype(jnp.bfloat16), "fsdp", scatter_dimension=1, tiled=True
            ).astype(jnp.float32),
            lax.psum_scatter(
                grad_terms[5].astype(jnp.bfloat16), "fsdp", scatter_dimension=0, tiled=True
            ).astype(jnp.float32),
        )
        totals = (
            shares
            if totals is None
            else tuple((first + second for first, second in zip(totals, shares)))
        )
    totals = lax.psum(totals, "ctx")
    norm_total = totals[4]
    return (
        jnp.stack(next_list),
        jnp.stack(grad_in_list),
        jnp.stack(earlier_list, axis=1),
        totals[0],
        totals[1],
        totals[2],
        totals[3],
        norm_total[0],
        norm_total[1],
        norm_total[2],
        norm_total[3],
        totals[5].reshape(-1),
    )


F32 = jnp.float32
BF16 = jnp.bfloat16
LOG2E = math.log2(math.e)
GELU_C = math.sqrt(2.0 / math.pi)
GELU_A = 0.044715
ANY = pl.ANY
VMEM = pltpu.VMEM
SMEM = pltpu.SMEM
MIB = 1 << 20


def mm(left, right, left_dim, right_dim):
    return lax.dot_general(
        left, right, (((left_dim,), (right_dim,)), ((), ())), preferred_element_type=F32
    )


def spec(space):
    return pl.BlockSpec(memory_space=space)


def shape_of(dims, kind):
    return jax.ShapeDtypeStruct(dims, kind)


def run_kernel(kernel, name, operands, spaces, outs, scratch, flops, limit=56):
    moved = sum(o.size * o.dtype.itemsize for o in operands) + sum(
        math.prod(o.shape) * jnp.dtype(o.dtype).itemsize for o in outs
    )
    return pl.pallas_call(
        kernel,
        name=name,
        in_specs=[spec(s) for s in spaces],
        out_specs=[spec(VMEM) for _ in outs],
        out_shape=outs,
        scratch_shapes=scratch,
        compiler_params=pltpu.CompilerParams(vmem_limit_bytes=limit * MIB),
        cost_estimate=pl.CostEstimate(
            flops=int(flops), bytes_accessed=int(moved), transcendentals=0
        ),
    )(*operands)


def block_index(scalars, order):
    place = scalars[1]
    return lax.bitwise_xor(place, jnp.int32((0, 2, 1, 3)[order]))


def early_kernel(mix, earlier, grad, out_grad, out_prev, out_mix):
    streams = earlier.shape[0]
    rows = grad.shape[0]
    step = 128

    out_mix[...] = jnp.zeros_like(out_mix)

    def one(index, carry):
        here = pl.ds(pl.multiple_of(index * step, step), step)
        g = grad[here, :].astype(F32)
        total = None
        for k in range(streams):
            e = earlier[k, here, :].astype(F32)
            out_grad[k, here, :] = (mix[k] * g).astype(BF16)
            out_mix[k : k + 1, :] += jnp.sum(e * g, axis=0, keepdims=True)
            total = mix[k] * e if total is None else total + mix[k] * e
        out_prev[here, :] = total
        return carry

    lax.fori_loop(0, rows // step, one, 0)


def full_rows(pieces, first, last):
    total = None
    for piece in pieces:
        term = piece[first:last, :].astype(F32)
        total = term if total is None else total + term
    return total


def qkv_kernel(hps, batches, has_x, offset, *refs):
    if has_x:
        scalars, x, cosine, sine, w0, w1, w2, w3 = refs[:8]
        out, n1t, norms, weight = refs[8:]
        rows = n1t.shape[0] // 4
        parts = full_rows((w0, w1, w2, w3), rows, rows + 16)
        norms[...] = parts[0:8, :] + parts[8:16, :]
        v = x[...].astype(F32)
        center = v - jnp.mean(v, axis=-1, keepdims=True)
        inv = lax.rsqrt(jnp.mean(center * center, axis=-1, keepdims=True) + 1e-05)
        n1 = center * inv * norms[0:1, :] + norms[1:2, :]
        n1t[...] = n1.astype(BF16).T
    else:
        scalars, n1t, cosine, sine, w0, w1, w2, w3 = refs[:8]
        out, weight = refs[8:]
        rows = n1t.shape[0] // 4
    for order, piece in enumerate((w0, w1, w2, w3)):
        start = pl.multiple_of(block_index(scalars, order) * rows, rows)
        weight[pl.ds(start, rows), :] = piece[offset : offset + rows, :]
    width = weight.shape[1] // 3
    size = width // hps
    half = size // 2
    tokens = n1t.shape[1] // batches
    for part in range(3):
        cols = mm(weight[:, part * width : (part + 1) * width], n1t[...], 0, 0)
        for head in range(hps):
            for batch in range(batches):
                lanes = slice(batch * tokens, (batch + 1) * tokens)
                top = cols[head * size : head * size + half, lanes]
                low = cols[head * size + half : (head + 1) * size, lanes]
                if part < 2:
                    c = cosine[batch]
                    s = sine[batch]
                    top, low = top * c - low * s, low * c + top * s
                slot = batch * hps + head
                out[slot, part * size : part * size + half, :] = top.astype(BF16)
                out[slot, part * size + half : (part + 1) * size, :] = low.astype(BF16)


def stream_tile(count, stream, step):
    long = count - stream
    late = step >= long
    query = jnp.where(late, stream, count - 1 - stream)
    return query, jnp.where(late, step - long, step)


def attend_kernel(count, scale, ids, ins, outs, ot, lse, qt, kk, vt, scores, *states):
    streams = count // 2
    tops, totals, accs = states[:streams], states[streams : 2 * streams], states[2 * streams :]
    size = qt.shape[1]
    factor = scale * LOG2E
    for d in range(count):
        slot = ids[d]
        qt[slot] = ins[d, 0:size, :]
        kk[slot] = ins[d, size : 2 * size, :].T
        vt[slot] = ins[d, 2 * size :, :]
    for r in range(streams):
        tops[r][...] = jnp.full_like(tops[r], -1e30)
        totals[r][...] = jnp.zeros_like(totals[r])
        accs[r][...] = jnp.zeros_like(accs[r])
        scores[0, r] = mm(kk[0], qt[count - 1 - r], 1, 0)

    def step(index, carry):
        for r in range(streams):
            i, j = stream_tile(count, r, jnp.minimum(index + 1, count))
            scores[(index + 1) % 2, r] = mm(kk[j], qt[i], 1, 0)
        for r in range(streams):
            i, j = stream_tile(count, r, index)
            half = jnp.where(index >= count - r, 1, 0)
            s = scores[index % 2, r]
            old = tops[r][half]
            new = jnp.maximum(old, jnp.max(s, axis=0, keepdims=True) * factor)
            shrink = jnp.exp2(old - new)
            p = jnp.exp2(s * factor - new)
            totals[r][half] = totals[r][half] * shrink + jnp.sum(p, axis=0, keepdims=True)
            accs[r][half] = accs[r][half] * shrink + mm(vt[j], p.astype(BF16), 1, 0)
            tops[r][half] = new
        return carry

    lax.fori_loop(0, count + 1, step, 0)
    for r in range(streams):
        for half, i in enumerate((count - 1 - r, r)):
            run = totals[r][half]
            ot[i] = accs[r][half] / run
            lse[i] = tops[r][half] + jnp.log2(run)
    for d in range(count):
        outs[d] = ot[ids[d]].astype(BF16)


def attend_back_kernel(
    count, scale, stage, ids, ins, grads, ot, lse, outs, qt, qq, kt, kk, vv, gt, gg, delta, scores, gains, *sums
):
    streams = count // 2
    dqs, dks, dvs = sums[:streams], sums[streams : 2 * streams], sums[2 * streams :]
    size = qt.shape[1]
    factor = scale * LOG2E
    for d in range(count):
        slot = ids[d]
        block = ins[d]
        q = block[0:size]
        k = block[size : 2 * size]
        qt[slot] = q
        kt[slot] = k
        qq[slot] = q.T
        kk[slot] = k.T
        vv[slot] = block[2 * size :].T
        g = grads[d, stage * size : (stage + 1) * size, :]
        gt[slot] = g
        gg[slot] = g.T
        delta[slot] = jnp.sum(g.astype(F32) * ot[slot], axis=0, keepdims=True)
    for r in range(streams):
        dqs[r][...] = jnp.zeros_like(dqs[r])
        dks[r][...] = jnp.zeros_like(dks[r])
        dvs[r][...] = jnp.zeros_like(dvs[r])
        scores[0, r] = mm(kk[0], qt[count - 1 - r], 1, 0)
        gains[0, r] = mm(vv[0], gt[count - 1 - r], 1, 0)

    def step(index, carry):
        for r in range(streams):
            i, j = stream_tile(count, r, jnp.minimum(index + 1, count))
            scores[(index + 1) % 2, r] = mm(kk[j], qt[i], 1, 0)
            gains[(index + 1) % 2, r] = mm(vv[j], gt[i], 1, 0)
        for r in range(streams):
            i, j = stream_tile(count, r, index)
            half = jnp.where(index >= count - r, 1, 0)
            p = jnp.exp2(scores[index % 2, r] * factor - lse[i])
            ds = (p * (gains[index % 2, r] - delta[i])).astype(BF16)
            dqs[r][half] += mm(kt[j], ds, 1, 0)
            dks[r][j] += mm(ds, qq[i], 1, 0)
            dvs[r][j] += mm(p.astype(BF16), gg[i], 1, 0)
        return carry

    lax.fori_loop(0, count + 1, step, 0)
    for r in range(streams):
        for half, i in enumerate((count - 1 - r, r)):
            qt[i] = (dqs[r][half] * scale).astype(BF16)
    for d in range(count):
        slot = ids[d]
        outs[d, 0:size, :] = qt[slot]
        dk = dks[0][slot]
        dv = dvs[0][slot]
        for r in range(1, streams):
            dk = dk + dks[r][slot]
            dv = dv + dvs[r][slot]
        outs[d, size : 2 * size, :] = (dk * scale).astype(BF16).T
        outs[d, 2 * size :, :] = dv.astype(BF16).T


def gather_rows(scalars, pieces, window, target, sems, base):
    copies = []
    first, rows = window
    for order, piece in enumerate(pieces):
        start = pl.multiple_of(block_index(scalars, order) * rows, rows)
        copy = pltpu.make_async_copy(
            piece.at[pl.ds(first, rows), :], target.at[pl.ds(start, rows), :], sems.at[base + order]
        )
        copy.start()
        copies.append(copy)
    return copies


def mlp_kernel(count, stages, hps, batches, scalars, mix, x, grad, norms, *refs):
    heads = refs[0]
    pieces = refs[1:5]
    refs = refs[5:]
    hidden, dhidden, n2_out, mid_out, dmid_out, dmid_low, ot, norm_grads = refs[:8]
    head_grads = refs[8]
    out_scr, up_scr, down_scr, dn2, got, sems = refs[9:]
    width = x.shape[1]
    size = ot.shape[2]
    share = width // 4
    groups = up_scr.shape[1] // width
    deep = down_scr.shape[0] // 4
    last = (groups * share) + deep
    copies_out = gather_rows(scalars, pieces, (last, share), out_scr, sems, 0)
    copies_up = []
    for group in range(groups):
        lanes = up_scr.at[:, pl.ds(group * width, width)]
        copies_up += gather_rows(scalars, pieces, (group * share, share), lanes, sems, 4 + 4 * group)
    copies_down = gather_rows(
        scalars, pieces, (groups * share, deep), down_scr, sems, 4 + 4 * groups
    )
    for stage in range(stages):
        for slot in range(count):
            ot[slot // hps, stage * hps + slot % hps] = heads[
                slot, stage * size : (stage + 1) * size, :
            ]
    for copy in copies_out:
        copy.wait()
    tokens = x.shape[0] // batches
    for batch in range(batches):
        rows = slice(batch * tokens, (batch + 1) * tokens)
        attended = ot[batch].reshape(width, tokens)
        middle = x[rows, :].astype(F32) + mm(attended, out_scr[...], 0, 0)
        mid_out[rows, :] = middle
        center = middle - jnp.mean(middle, axis=-1, keepdims=True)
        inv = lax.rsqrt(jnp.mean(center * center, axis=-1, keepdims=True) + 1e-05)
        n2_out[rows, :] = (center * inv * norms[2:3, :] + norms[3:4, :]).astype(BF16)
    for copy in copies_up + copies_down:
        copy.wait()
    dn2[...] = jnp.zeros_like(dn2)
    dy = (mix[mix.shape[0] - 1] * grad[...].astype(F32)).astype(BF16)
    step = 512 if up_scr.shape[1] % 512 == 0 else 128

    def one(index, carry):
        here = pl.ds(pl.multiple_of(index * step, step), step)
        up = up_scr[:, here]
        u = mm(n2_out[...], up, 1, 0)
        da = mm(dy, down_scr[here, :], 1, 1)
        square = u * u
        bend = jnp.tanh(u * (GELU_C + (GELU_C * GELU_A) * square))
        gate = 0.5 + 0.5 * bend
        hidden[:, here] = (u * gate).astype(BF16)
        slope = gate + (0.5 * u) * (1.0 - bend * bend) * (
            GELU_C + (3.0 * GELU_C * GELU_A) * square
        )
        du = (da * slope).astype(BF16)
        dhidden[:, here] = du
        dn2[...] += mm(du, up, 1, 1)
        return carry

    lax.fori_loop(0, up_scr.shape[1] // step, one, 0)
    gain_sum = None
    for batch in range(batches):
        rows = slice(batch * tokens, (batch + 1) * tokens)
        middle = mid_out[rows, :]
        center = middle - jnp.mean(middle, axis=-1, keepdims=True)
        inv = lax.rsqrt(jnp.mean(center * center, axis=-1, keepdims=True) + 1e-05)
        z = center * inv
        dn = dn2[rows, :]
        part_gain = jnp.sum(dn * z, axis=0, keepdims=True)
        part_bias = jnp.sum(dn, axis=0, keepdims=True)
        gain_sum = part_gain if gain_sum is None else gain_sum + part_gain
        bias_sum = part_bias if batch == 0 else bias_sum + part_bias
        h = dn * norms[2:3, :]
        back = inv * (
            h - jnp.mean(h, axis=-1, keepdims=True) - z * jnp.mean(h * z, axis=-1, keepdims=True)
        )
        dmid = mix[mix.shape[0] - 1] * grad[rows, :].astype(F32) + back
        dmid_out[rows, :] = dmid
        low = dmid.astype(BF16)
        dmid_low[rows, :] = low
        got[batch] = mm(out_scr[...], low, 1, 1).astype(BF16).reshape(got.shape[1:])
    norm_grads[...] = jnp.zeros_like(norm_grads)
    norm_grads[0:1, :] = gain_sum
    norm_grads[1:2, :] = bias_sum
    for stage in range(stages):
        for slot in range(count):
            head_grads[slot, stage * size : (stage + 1) * size, :] = got[
                slot // hps, stage * hps + slot % hps
            ]


def result_kernel(window, scalars, mix, hidden, mid, prev, grad, w0, w1, w2, w3, out, out_mix, acc):
    acc[...] = mid[...]
    first, rows = window
    for order, piece in enumerate((w0, w1, w2, w3)):
        start = pl.multiple_of(block_index(scalars, order) * rows, rows)
        acc[...] += mm(hidden[:, pl.ds(start, rows)], piece[first : first + rows, :], 1, 0)
    y = acc[...]
    out[...] = (prev[...] + mix[mix.shape[0] - 1] * y).astype(BF16)
    out_mix[...] = jnp.zeros_like(out_mix)
    out_mix[0:1, :] = jnp.sum(grad[...].astype(F32) * y, axis=0, keepdims=True)


def put_pieces(me, value, outs, order, count, first):
    target = outs[order // 2]
    rows = value.shape[0] // count
    low = value.astype(BF16)
    for sub in range(count):
        slot = lax.bitwise_xor(me, jnp.int32(sub))
        target[order % 2, lax.rem(slot, jnp.int32(2)), lax.div(slot, jnp.int32(2)), first : first + rows, :] = (
            low[sub * rows : (sub + 1) * rows, :]
        )


def down_grad_kernel(count, scalars, mix, hidden, grad, keep, send):
    dy = (mix[mix.shape[0] - 1] * grad[...].astype(F32)).astype(BF16)
    rows = count * keep.shape[3]
    for order in range(4):
        start = pl.multiple_of(block_index(scalars, order) * rows, rows)
        value = mm(hidden[:, pl.ds(start, rows)], dy, 0, 0)
        put_pieces(scalars[0], value, (keep, send), order, count, 0)


def up_out_grad_kernel(count, scalars, n2, dhidden, ot, dmid, keep, send, left, whole):
    batches = ot.shape[0]
    width = n2.shape[1]
    tokens = ot.shape[3]
    rows = width // 4
    thin = rows // count

    def arrange():
        for order in range(4):
            here = pl.ds(pl.multiple_of(block_index(scalars, order) * rows, rows), rows)
            left[order * rows : (order + 1) * rows, :] = whole[here, :]

    whole[...] = n2[...].T
    arrange()
    groups = dhidden.shape[1] // width
    for group in range(groups):
        value = mm(left[...], dhidden[:, group * width : (group + 1) * width], 1, 0)
        for order in range(4):
            put_pieces(
                scalars[0],
                value[order * rows : (order + 1) * rows, :],
                (keep, send),
                order,
                count,
                group * thin,
            )
    for batch in range(batches):
        whole[:, batch * tokens : (batch + 1) * tokens] = ot[batch].reshape(width, tokens)
    arrange()
    value = mm(left[...], dmid[...], 1, 0)
    for order in range(4):
        put_pieces(
            scalars[0],
            value[order * rows : (order + 1) * rows, :],
            (keep, send),
            order,
            count,
            groups * thin,
        )


def grads_kernel(count, window, scalars, mix, hidden, mid, prev, grad, w0, w1, w2, w3, n2, dhidden, ot, dmid, *refs):
    down, up, (out, out_mix), (acc, left, whole) = refs[:2], refs[2:4], refs[4:6], refs[6:]
    down_grad_kernel(count, scalars, mix, hidden, grad, *down)
    up_out_grad_kernel(count, scalars, n2, dhidden, ot, dmid, *up, left, whole)
    result_kernel(window, scalars, mix, hidden, mid, prev, grad, w0, w1, w2, w3, out, out_mix, acc)


def in_grad_kernel(count, hps, natural, scalars, cosine, sine, n1t, *refs):
    stages = (len(refs) - 3) // 2
    dts = refs[stages : 2 * stages]
    keep, send, left = refs[2 * stages :]
    batches = dts[0].shape[0]
    size = dts[0].shape[3]
    half = size // 2
    tokens = dts[0].shape[4]
    width = n1t.shape[0]
    rows = width // 4
    thin = rows // count
    for order in range(4):
        here = pl.ds(pl.multiple_of(block_index(scalars, order) * rows, rows), rows)
        left[order * rows : (order + 1) * rows, :] = n1t[here, :]
    cols = 3 * hps * size
    for stage in range(stages):
        grads = refs[stage]
        dt = dts[stage]
        for slot in range(count):
            batch, head = slot // hps, slot % hps
            c = cosine[batch]
            s = sine[batch]
            for part in range(2):
                top = grads[slot, part * size : part * size + half, :].astype(F32)
                low = grads[slot, part * size + half : (part + 1) * size, :].astype(F32)
                dt[batch, part, head, 0:half, :] = (top * c + low * s).astype(BF16)
                dt[batch, part, head, half:size, :] = (low * c - top * s).astype(BF16)
            dt[batch, 2, head] = grads[slot, 2 * size :, :]
        value = None
        for batch in range(batches):
            term = mm(
                left[:, batch * tokens : (batch + 1) * tokens],
                dt[batch].reshape(cols, tokens),
                1,
                1,
            )
            value = term if value is None else value + term
        low = value.astype(BF16)
        for order in range(4):
            if natural:
                target = (keep, send)[order // 2]
                for sub in range(count):
                    start = order * rows + sub * thin
                    target[order % 2, sub] = low[start : start + thin, :]
            else:
                put_pieces(
                    scalars[0],
                    low[order * rows : (order + 1) * rows, :],
                    (keep, send),
                    order,
                    count,
                    stage * thin,
                )


def input_grad_kernel(stages, windows, scalars, x, norms, dmid, *refs):
    dts = refs[:stages]
    pieces = refs[stages : stages + 4 * stages]
    out, norm_grads, weights, sems = refs[5 * stages :]
    copies = []
    for stage in range(stages):
        copies += gather_rows(
            scalars,
            pieces[4 * stage : 4 * stage + 4],
            windows[stage],
            weights.at[stage],
            sems,
            4 * stage,
        )
    for copy in copies:
        copy.wait()
    batches = dts[0].shape[0]
    tokens = dts[0].shape[4]
    cols = weights.shape[2]
    gain_sum = bias_sum = None
    for batch in range(batches):
        rows = slice(batch * tokens, (batch + 1) * tokens)
        dnt = None
        for stage in range(stages):
            term = mm(weights[stage], dts[stage][batch].reshape(cols, tokens), 1, 0)
            dnt = term if dnt is None else dnt + term
        dn = dnt.T
        v = x[rows, :].astype(F32)
        center = v - jnp.mean(v, axis=-1, keepdims=True)
        inv = lax.rsqrt(jnp.mean(center * center, axis=-1, keepdims=True) + 1e-05)
        z = center * inv
        part_gain = jnp.sum(dn * z, axis=0, keepdims=True)
        part_bias = jnp.sum(dn, axis=0, keepdims=True)
        gain_sum = part_gain if batch == 0 else gain_sum + part_gain
        bias_sum = part_bias if batch == 0 else bias_sum + part_bias
        h = dn * norms[0:1, :]
        back = inv * (
            h - jnp.mean(h, axis=-1, keepdims=True) - z * jnp.mean(h * z, axis=-1, keepdims=True)
        )
        out[rows, :] = (dmid[rows, :] + back).astype(BF16)
    norm_grads[...] = jnp.zeros_like(norm_grads)
    norm_grads[0:1, :] = gain_sum
    norm_grads[1:2, :] = bias_sum


def far_offsets(count):
    offsets = [0]
    bit = count // 2
    while bit > 2:
        offsets += [offset ^ bit for offset in offsets]
        bit //= 2
    return offsets


def place_kernel(count, moves, scalars, *refs):
    parts = refs[: min(count, 4)]
    outs = refs[len(parts) :]
    for low, source in enumerate(parts):
        for sub, offset in enumerate(far_offsets(count)):
            slot = lax.bitwise_xor(scalars[0], jnp.int32(offset + low))
            for out, first, rows, begin, wide, to in moves:
                outs[out][slot, :, to : to + wide] = source[
                    sub, first : first + rows, begin : begin + wide
                ].astype(F32)


def place_in_kernel(count, moves, width, wide, thin, scalars, *refs):
    *parts, last, out = refs
    place_kernel(count, moves, scalars, *parts, out)
    final = len(moves) // 3
    for sub in range(last.shape[0]):
        for part in range(3):
            to = part * width + final * wide
            out[sub, :, to : to + wide] = last[sub, :, part * wide : (part + 1) * wide].astype(F32)


def exchange(value, axis, bit):
    size = lax.axis_size(axis)
    return lax.ppermute(value, axis, [(i, i ^ bit) for i in range(size)])


def added(left, right):
    return (left.astype(F32) + right.astype(F32)).astype(BF16)


def swapped(value, groups=None):
    return lax.all_to_all(value, "ctx", 0, 0, axis_index_groups=groups)


def summed(value):
    return jnp.sum(value.astype(F32), axis=0).astype(BF16)


def spread(own, count, groups=None):
    return swapped(jnp.broadcast_to(own[None], (count, *own.shape)), groups)


def total(terms):
    value = terms[0].astype(F32)
    for term in terms[1:]:
        value = value + term.astype(F32)
    return value.astype(BF16)


class Chain:
    def __init__(self, keep, send, order):
        count = lax.axis_size("ctx")
        self.labels = ["x", 1]
        bit = count // 2
        while bit > 1:
            self.labels.append(bit)
            bit //= 2
        dims = (2,) * len(self.labels) + keep.shape[3:]
        self.terms = [keep.reshape(dims), exchange(send, "fsdp", 1).reshape(dims)]
        self.order = list(order)

    def step(self, *holds):
        label = self.order.pop(0)
        axis = self.labels.index(label)
        if holds:
            self.terms[-1] = after(self.terms[-1], *holds)
        sent = total([lax.index_in_dim(t, 1, axis, keepdims=False) for t in self.terms])
        got = exchange(sent, *(("fsdp", 2) if label == "x" else ("ctx", label)))
        self.terms = [lax.index_in_dim(t, 0, axis, keepdims=False) for t in self.terms] + [got]
        self.labels.pop(axis)
        return sent

    def finish(self):
        while self.order:
            self.step()
        return total(self.terms)


def gather_blocks(own, last):
    count = lax.axis_size("ctx")
    held = own[None]
    bit = count // 2
    while bit > 2:
        held = jnp.concatenate([held, exchange(held, "ctx", bit)])
        bit //= 2
    parts = [held] + [exchange(held, "ctx", bit) for bit in (1, 2) if bit < count]
    if count > 2:
        parts.append(exchange(parts[3 - last], "ctx", last))
    return parts


def halved(keep, send):
    got = exchange(send, "fsdp", 1)
    passed = added(keep[1], got[1])
    return total([keep[0], got[0], exchange(passed, "fsdp", 2)]), passed


def reduce_whole(blocks, extra):
    count, rows = blocks.shape[:2]
    extra = jnp.broadcast_to(extra.astype(BF16)[None], (count, *extra.shape))
    sums = jnp.sum(swapped(jnp.concatenate([blocks, extra], axis=1)).astype(F32), axis=0)
    return spread(sums[:rows].astype(BF16), count), sums[rows:]


def after(value, *others):
    return lax.optimization_barrier((value, *others))[0]


def gathered(shard):
    other_chip = exchange(shard, "fsdp", 2)
    return [shard, other_chip, exchange(shard, "fsdp", 1), exchange(other_chip, "fsdp", 1)]


def head_body(
    inputs,
    earlier,
    input_proj,
    output_proj,
    up_proj,
    down_proj,
    norm1_gain,
    norm1_bias,
    norm2_gain,
    norm2_bias,
    mixing,
    block_order,
    grad_next,
):
    batches, tokens, width = inputs.shape
    rows = batches * tokens
    heads = HEADS
    size = width // heads
    scale = size ** (-0.5)
    streams = earlier.shape[0]
    count = lax.axis_size("ctx")
    hps = count // batches
    stages = heads // hps
    inner = down_proj.shape[0] * 4
    me = lax.axis_index("ctx").astype(jnp.int32)
    place = lax.axis_index("fsdp").astype(jnp.int32)
    scalars = jnp.stack([me, place])
    ids = block_order[me // hps].astype(jnp.int32)
    x = inputs.reshape(rows, width)
    grad = grad_next.reshape(rows, width)

    share = width // 4
    cols = 3 * hps * size
    norm_stack = jnp.stack([norm1_gain, norm1_bias, norm2_gain, norm2_bias])
    coarse = lax.reduce_precision(norm_stack, 8, 7)
    norm_rows = jnp.zeros((16, width), BF16)
    norm_rows = lax.dynamic_update_slice(norm_rows, coarse.astype(BF16), (0, place * share))
    norm_rows = lax.dynamic_update_slice(
        norm_rows, (norm_stack - coarse).astype(BF16), (8, place * share)
    )
    wide = hps * size
    chunks = [
        jnp.concatenate(
            [input_proj[:, p * width + s * wide : p * width + (s + 1) * wide] for p in range(3)], 1
        )
        for s in range(stages)
    ]
    first_in = gathered(jnp.concatenate([chunks[0], jnp.pad(norm_rows, ((0, 0), (0, cols - width)))]))
    rest_in = gathered(after(jnp.concatenate(chunks[1:]), first_in[1]))
    groups = inner // width
    up_rows = jnp.moveaxis(up_proj.reshape(share, groups, width), 1, 0).reshape(-1, width)
    packed = jnp.concatenate([up_rows, down_proj, output_proj])

    half = size // 2
    own_blocks = block_order[:, me]
    positions = (own_blocks[:, None] * tokens + lax.iota(jnp.int32, tokens)[None]).astype(F32)
    freqs = jnp.exp(lax.iota(F32, half) * (-2.0 * math.log(10000.0) / size))
    angle = freqs[None, :, None] * positions[:, None, :]
    cosine = jnp.cos(angle)
    sine = jnp.sin(angle)

    grad_earlier, prev, mix_early = run_kernel(
        early_kernel,
        "early",
        [mixing, earlier.reshape(streams, rows, width), grad],
        [SMEM, VMEM, VMEM],
        [
            shape_of((streams, rows, width), BF16),
            shape_of((rows, width), F32),
            shape_of((8, width), F32),
        ],
        [],
        6 * streams * rows * width,
    )

    pair_shape = shape_of((count, 3 * size, tokens), BF16)
    x = after(x, mix_early)
    packed = after(packed, rest_in[1])
    weights = [packed, exchange(packed, "fsdp", 2), exchange(packed, "fsdp", 1)]
    made = []
    n1t = norms = None
    windows = [(0, share)] + [(share * s, share) for s in range(stages - 1)]
    for s in range(stages):
        first = s == 0
        operands = [scalars] + ([x] if first else [n1t]) + [cosine, sine]
        operands += first_in if first else rest_in
        outs = [pair_shape]
        if first:
            outs += [shape_of((width, rows), BF16), shape_of((8, width), F32)]
        result = run_kernel(
            functools.partial(qkv_kernel, hps, batches, first, windows[s][0]),
            "qkv",
            operands,
            [SMEM] + [VMEM] * (len(operands) - 1),
            outs,
            [pltpu.VMEM((width, cols), BF16)],
            2 * rows * width * cols,
        )
        if first:
            n1t, norms = result[1:]
        made.append(result[0])

    tiles = count * (count + 1) // 2
    one = tokens * tokens * size * 2
    streams_in = count // 2
    head_shape = shape_of((count, size, tokens), BF16)
    held = []
    attended = []
    saved = []
    for s in range(stages):
        while len(held) < min(s + 2, stages):
            held.append(swapped(after(made[len(held)], *([saved[-1][1]] if saved else []))))
        result = run_kernel(
            functools.partial(attend_kernel, count, scale),
            "attend",
            [after(ids, saved[-1][1]) if saved else ids, held[s]],
            [SMEM, VMEM],
            [head_shape, shape_of((count, size, tokens), F32), shape_of((count, 1, tokens), F32)],
            [
                pltpu.VMEM((count, size, tokens), BF16),
                pltpu.VMEM((count, tokens, size), BF16),
                pltpu.VMEM((count, size, tokens), BF16),
                pltpu.VMEM((2, streams_in, tokens, tokens), F32),
            ]
            + [pltpu.VMEM((2, 1, tokens), F32)] * (2 * streams_in)
            + [pltpu.VMEM((2, size, tokens), F32)] * streams_in,
            4 * 2 * one * tiles,
        )
        saved.append(result[1:])
        attended.append(result[0])

    weights.append(exchange(after(weights[1], saved[-2][1]), "fsdp", 1))
    result = run_kernel(
        functools.partial(mlp_kernel, count, stages, hps, batches),
        "mlp",
        [scalars, mixing, x, grad, norms, swapped(jnp.concatenate(attended, axis=1))] + weights,
        [SMEM, SMEM, VMEM, VMEM, VMEM, VMEM] + [ANY] * 4,
        [
            shape_of((rows, inner), BF16),
            shape_of((rows, inner), BF16),
            shape_of((rows, width), BF16),
            shape_of((rows, width), F32),
            shape_of((rows, width), F32),
            shape_of((rows, width), BF16),
            shape_of((batches, heads, size, tokens), BF16),
            shape_of((8, width), F32),
            shape_of((count, stages * size, tokens), BF16),
        ],
        [
            pltpu.VMEM((width, width), BF16),
            pltpu.VMEM((width, inner), BF16),
            pltpu.VMEM((inner, width), BF16),
            pltpu.VMEM((rows, width), F32),
            pltpu.VMEM((batches, heads, size, tokens), BF16),
            pltpu.SemaphoreType.DMA((8 + 4 * groups,)),
        ],
        6 * rows * width * inner,
    )
    hidden, dhidden, n2, mid, dmid, dmid_low, ot, norm2_grads = result[:8]
    head_grads = swapped(result[8])

    sub = inner // 4 // count
    thin = share // count
    result = run_kernel(
        functools.partial(grads_kernel, count, (groups * share, inner // 4)),
        "grads",
        [scalars, mixing, hidden, mid, prev, grad] + weights + [n2, dhidden, ot, dmid_low],
        [SMEM, SMEM] + [VMEM] * 12,
        [shape_of((2, 2, count // 2, sub, width), BF16)] * 2
        + [shape_of((2, 2, count // 2, thin * (groups + 1), width), BF16)] * 2
        + [shape_of((rows, width), BF16), shape_of((8, width), F32)],
        [
            pltpu.VMEM((rows, width), F32),
            pltpu.VMEM((width, rows), BF16),
            pltpu.VMEM((width, rows), BF16),
        ],
        2 * rows * width * (3 * inner + width),
    )
    down_sums, up_sums, (next_input, mix_last) = result[:2], result[2:4], result[4:]

    def in_grads(arrived, natural):
        few = len(arrived)
        lead = (2, count, thin) if natural else (2, 2, count // 2, few * thin)
        result = run_kernel(
            functools.partial(in_grad_kernel, count, hps, natural),
            "in_grad",
            [scalars, cosine, sine, n1t] + arrived,
            [SMEM] + [VMEM] * (3 + few),
            [shape_of((batches, 3, hps, size, tokens), BF16)] * few
            + [shape_of((*lead, cols), BF16)] * 2,
            [pltpu.VMEM((width, rows), BF16)],
            2 * few * rows * width * cols,
        )
        return list(result[:few]), result[few:]

    far_bits = [1 << k for k in range(1, count.bit_length() - 1)]
    down_chain = Chain(down_sums[0], after(down_sums[1], head_grads), ["x", 1] + far_bits)
    up_chain = Chain(up_sums[0], after(up_sums[1], head_grads), [1, "x"] + far_bits)

    dts = []
    back = [mix_last]
    moved = []
    for s in range(stages):
        turn = [back[-1]]
        if s:
            turn.append(down_chain.step(back[-1]))
        if s == 1:
            turn.append(up_chain.step(back[-1]))
        if s > 1:
            turn.append(moved[s - 2])
        (value,) = run_kernel(
            functools.partial(attend_back_kernel, count, scale, s),
            "attend_back",
            [ids, after(held[s], *turn), head_grads] + list(saved[s]),
            [SMEM] + [VMEM] * 4,
            [pair_shape],
            [
                pltpu.VMEM((count, size, tokens), BF16),
                pltpu.VMEM((count, tokens, size), BF16),
                pltpu.VMEM((count, size, tokens), BF16),
                pltpu.VMEM((count, tokens, size), BF16),
                pltpu.VMEM((count, tokens, size), BF16),
                pltpu.VMEM((count, size, tokens), BF16),
                pltpu.VMEM((count, tokens, size), BF16),
                pltpu.VMEM((count, 1, tokens), F32),
                pltpu.VMEM((2, streams_in, tokens, tokens), F32),
                pltpu.VMEM((2, streams_in, tokens, tokens), F32),
            ]
            + [pltpu.VMEM((2, size, tokens), F32)] * streams_in
            + [pltpu.VMEM((count, tokens, size), F32)] * (2 * streams_in),
            4 * 5 * one * tiles,
        )
        back.append(value)
        moved.append(swapped(after(value, *moved[-1:])))
    early_dts, early_sums = in_grads([after(moved[0], back[-1])] + moved[1:-1], False)
    last_dts, last_sums = in_grads(moved[-1:], True)
    dts = early_dts + last_dts
    up_chain.step(back[-1])
    down_chain.step(moved[-1])
    up_chain.step(moved[-1])
    early_chain = Chain(*early_sums, ["x", 1] + far_bits)
    last_blocks, last_passed = halved(*last_sums)
    early_chain.step(moved[-1])
    down_chain.step(last_passed)
    up_chain.step(last_passed)
    early_parts = gather_blocks(early_chain.finish(), 1)
    down_parts = gather_blocks(down_chain.finish(), 1)
    up_parts = gather_blocks(up_chain.finish(), 2)

    grad_input, norm1_grads = run_kernel(
        functools.partial(input_grad_kernel, stages, windows),
        "input_grad",
        [scalars, x, norms, dmid] + dts + first_in + rest_in * (stages - 1),
        [SMEM] + [VMEM] * (3 + stages) + [ANY] * (4 * stages),
        [shape_of((rows, width), BF16), shape_of((8, width), F32)],
        [pltpu.VMEM((stages, width, cols), BF16), pltpu.SemaphoreType.DMA((4 * stages,))],
        2 * rows * width * 3 * width,
    )

    mix_sums = jnp.sum(jnp.concatenate([mix_early[:streams], mix_last[:1]], axis=0), axis=1)
    mix_row = jnp.pad(mix_sums, (0, width - streams - 1))
    small = jnp.concatenate([norm1_grads[:2], norm2_grads[:2], mix_row[None]], axis=0)
    small = small + exchange(small, "fsdp", 1)
    small = small + exchange(small, "fsdp", 2)
    mix_high = lax.reduce_precision(small[4:], 8, 7)
    zeros = jnp.zeros((2, width), F32)
    small = jnp.concatenate([small[:4], mix_high, small[4:] - mix_high, zeros], axis=0)
    last_parts, small = reduce_whole(last_blocks, small)
    norm_total = lax.dynamic_slice_in_dim(small[:4], place * share, share, 1)
    mix_total = small[4, : streams + 1] + small[5, : streams + 1]

    (grad_down,) = run_kernel(
        functools.partial(place_kernel, count, ((0, 0, sub, 0, width, 0),)),
        "place_down",
        [scalars, *down_parts],
        [SMEM] + [VMEM] * len(down_parts),
        [shape_of((count, sub, width), F32)],
        [],
        0,
    )
    moves = tuple((0, g * thin, thin, 0, width, g * width) for g in range(groups))
    grad_up, grad_out = run_kernel(
        functools.partial(place_kernel, count, moves + ((1, groups * thin, thin, 0, width, 0),)),
        "place_up",
        [scalars, *up_parts],
        [SMEM] + [VMEM] * len(up_parts),
        [shape_of((count, thin, inner), F32), shape_of((count, thin, width), F32)],
        [],
        0,
    )
    wide = hps * size
    moves = tuple(
        (0, g * thin, thin, part * wide, wide, part * width + g * wide)
        for g in range(stages - 1)
        for part in range(3)
    )
    (grad_in,) = run_kernel(
        functools.partial(place_in_kernel, count, moves, width, wide, thin),
        "place_in",
        [scalars, *early_parts, last_parts],
        [SMEM] + [VMEM] * (len(early_parts) + 1),
        [shape_of((count, thin, 3 * width), F32)],
        [],
        0,
    )
    return (
        next_input.reshape(batches, tokens, width),
        grad_input.reshape(batches, tokens, width),
        grad_earlier.reshape(streams, batches, tokens, width),
        grad_in.reshape(share, 3 * width),
        grad_out.reshape(share, width),
        grad_up.reshape(share, inner),
        grad_down.reshape(inner // 4, width),
        norm_total[0],
        norm_total[1],
        norm_total[2],
        norm_total[3],
        mix_total,
    )


def heads_fit(batches):
    count = lax.axis_size("ctx")
    return (
        lax.axis_size("fsdp") == 4
        and count & (count - 1) == 0
        and count % batches == 0
        and HEADS % max(count // batches, 1) == 0
    )


def either_body(inputs, *rest):
    return (head_body if heads_fit(inputs.shape[0]) else body)(inputs, *rest)


def solution(mesh):
    placed = (
        P("fsdp", "ctx", None),
        P(None, "fsdp", "ctx", None),
        P("fsdp", None),
        P("fsdp", None),
        P("fsdp", None),
        P("fsdp", None),
        P("fsdp"),
        P("fsdp"),
        P("fsdp"),
        P("fsdp"),
        P(),
        P(),
        P("fsdp", "ctx", None),
    )
    return jax.shard_map(
        either_body,
        mesh=mesh,
        in_specs=placed,
        out_specs=(
            P("fsdp", "ctx", None),
            P("fsdp", "ctx", None),
            P(None, "fsdp", "ctx", None),
            P("fsdp", None),
            P("fsdp", None),
            P("fsdp", None),
            P("fsdp", None),
            P("fsdp"),
            P("fsdp"),
            P("fsdp"),
            P("fsdp"),
            P(),
        ),
        check_vma=False,
    )
```

```python
import functools
import math

import jax
import jax.numpy as jnp
from jax import lax
from jax.experimental import pallas as pl
from jax.experimental.pallas import tpu as pltpu
from jax.sharding import PartitionSpec as P

HEADS = 12


def passed_along(value, axis, steps):
    count = lax.axis_size(axis)
    pairs = [(source, (source + steps) % count) for source in range(count)]
    return lax.ppermute(value, axis, pairs)


def norm_parts(values, gain, bias):
    mean_value = jnp.mean(values, axis=-1, keepdims=True)
    centered = values - mean_value
    inv_std = lax.rsqrt(jnp.mean(centered * centered, axis=-1, keepdims=True) + 1e-05)
    normed = centered * inv_std
    return (normed * gain + bias, normed, inv_std)


def norm_back(grad_out, normed, inv_std, gain):
    scaled = grad_out * gain
    mean_one = jnp.mean(scaled, axis=-1, keepdims=True)
    mean_two = jnp.mean(scaled * normed, axis=-1, keepdims=True)
    return inv_std * (scaled - mean_one - normed * mean_two)


def rotary_tables(block_id, block_rows, head_dim):
    half_dim = head_dim // 2
    positions = (block_id * block_rows + lax.iota(jnp.int32, block_rows)).astype(jnp.float32)
    freqs = jnp.exp(lax.iota(jnp.float32, half_dim) * (-2.0 * math.log(10000.0) / head_dim))
    angle = positions[:, None] * freqs[None, :]
    return (jnp.cos(angle)[:, None, :], jnp.sin(angle)[:, None, :])


def rotate(values, cosine, sine_table):
    half_dim = values.shape[-1] // 2
    first_half = values[..., :half_dim]
    second_half = values[..., half_dim:]
    return jnp.concatenate(
        [
            first_half * cosine - second_half * sine_table,
            second_half * cosine + first_half * sine_table,
        ],
        axis=-1,
    )


def unrotate(grads, cosine, sine_table):
    half_dim = grads.shape[-1] // 2
    first_half = grads[..., :half_dim]
    second_half = grads[..., half_dim:]
    return jnp.concatenate(
        [
            first_half * cosine + second_half * sine_table,
            second_half * cosine - first_half * sine_table,
        ],
        axis=-1,
    )


def head_view(values, head_count):
    return values.reshape(values.shape[0], head_count, values.shape[1] // head_count)


def forward_visit(state, local_query, block_keys, block_values, head_count, score_scale):
    run_max, run_sum, accum = state
    query_heads = head_view(local_query, head_count)
    key_heads = head_view(block_keys, head_count)
    value_heads = head_view(block_values, head_count)
    scores = (
        jnp.einsum("qhe,khe->hqk", query_heads, key_heads, preferred_element_type=jnp.float32)
        * score_scale
    )
    new_max = jnp.maximum(run_max, jnp.max(scores, axis=-1))
    weights = jnp.exp(scores - new_max[:, :, None])
    factor = jnp.exp(run_max - new_max)
    new_sum = run_sum * factor + jnp.sum(weights, axis=-1)
    update = jnp.einsum(
        "hqk,khe->qhe",
        weights.astype(jnp.bfloat16),
        value_heads,
        preferred_element_type=jnp.float32,
    )
    return (new_max, new_sum, accum * jnp.transpose(factor)[:, :, None] + update)


def backward_pair(
    query_rows, key_rows, value_rows, grad_rows, log_total, row_delta, head_count, score_scale
):
    query_heads = head_view(query_rows, head_count)
    key_heads = head_view(key_rows, head_count)
    value_heads = head_view(value_rows, head_count)
    grad_heads = head_view(grad_rows, head_count)
    scores = (
        jnp.einsum("qhe,khe->hqk", query_heads, key_heads, preferred_element_type=jnp.float32)
        * score_scale
    )
    probs = jnp.exp(scores - log_total[:, :, None])
    grad_probs = jnp.einsum(
        "qhe,khe->hqk", grad_heads, value_heads, preferred_element_type=jnp.float32
    )
    grad_scores = (probs * (grad_probs - row_delta[:, :, None])).astype(jnp.bfloat16)
    grad_query = (
        jnp.einsum("hqk,khe->qhe", grad_scores, key_heads, preferred_element_type=jnp.float32)
        * score_scale
    )
    grad_keys = (
        jnp.einsum("hqk,qhe->khe", grad_scores, query_heads, preferred_element_type=jnp.float32)
        * score_scale
    )
    grad_values = jnp.einsum(
        "hqk,qhe->khe", probs.astype(jnp.bfloat16), grad_heads, preferred_element_type=jnp.float32
    )
    return (
        grad_query.reshape(query_rows.shape[0], -1),
        grad_keys.reshape(key_rows.shape[0], -1),
        grad_values.reshape(key_rows.shape[0], -1),
    )


def body(
    inputs,
    earlier,
    input_proj,
    output_proj,
    up_proj,
    down_proj,
    norm1_gain,
    norm1_bias,
    norm2_gain,
    norm2_bias,
    mixing,
    block_order,
    grad_next,
):
    head_count = HEADS
    batch_count = inputs.shape[0]
    block_rows = inputs.shape[1]
    model_width = inputs.shape[2]
    head_dim = model_width // head_count
    score_scale = head_dim ** (-0.5)
    stream_count = earlier.shape[0]
    cycle_size = lax.axis_size("ctx")
    cycle_place = lax.axis_index("ctx")
    norm_stack = jnp.stack([norm1_gain, norm1_bias, norm2_gain, norm2_bias])
    full_in, full_out, full_up, full_down, full_norms = (
        lax.all_gather(input_proj, "fsdp", axis=0, tiled=True),
        lax.all_gather(output_proj, "fsdp", axis=0, tiled=True),
        lax.all_gather(up_proj, "fsdp", axis=0, tiled=True),
        lax.all_gather(down_proj, "fsdp", axis=0, tiled=True),
        lax.all_gather(norm_stack.astype(jnp.bfloat16), "fsdp", axis=1, tiled=True).astype(
            norm_stack.dtype
        ),
    )
    gain_one = full_norms[0]
    bias_one = full_norms[1]
    gain_two = full_norms[2]
    bias_two = full_norms[3]
    next_list = []
    grad_in_list = []
    earlier_list = []
    totals = None
    for batch in range(batch_count):
        block_input = inputs[batch].astype(jnp.float32)
        order_row = block_order[batch]
        own_block = order_row[cycle_place]
        cosine, sine_table = rotary_tables(own_block, block_rows, head_dim)
        normed_in, normed_one, inv_one = norm_parts(block_input, gain_one, bias_one)
        normed_in_b = normed_in.astype(jnp.bfloat16)
        projected = jnp.dot(normed_in_b, full_in, preferred_element_type=jnp.float32)
        local_query = (
            rotate(head_view(projected[:, :model_width], head_count), cosine, sine_table)
            .reshape(block_rows, model_width)
            .astype(jnp.bfloat16)
        )
        local_keys = (
            rotate(
                head_view(projected[:, model_width : 2 * model_width], head_count),
                cosine,
                sine_table,
            )
            .reshape(block_rows, model_width)
            .astype(jnp.bfloat16)
        )
        local_values = projected[:, 2 * model_width :].astype(jnp.bfloat16)
        start_state = (
            jnp.full((head_count, block_rows), -1e30, jnp.float32),
            jnp.zeros((head_count, block_rows), jnp.float32),
            jnp.zeros((block_rows, head_count, head_dim), jnp.float32),
        )
        piece_keys = lax.all_gather(local_keys, "ctx", axis=0, tiled=True)
        piece_values = lax.all_gather(local_values, "ctx", axis=0, tiled=True)
        count = piece_keys.shape[0] // block_rows

        def one_block(index, state_now):
            block_keys = lax.dynamic_slice_in_dim(piece_keys, index * block_rows, block_rows, 0)
            block_values = lax.dynamic_slice_in_dim(piece_values, index * block_rows, block_rows, 0)
            return lax.cond(
                order_row[index] <= own_block,
                lambda held: forward_visit(
                    held, local_query, block_keys, block_values, head_count, score_scale
                ),
                lambda held: held,
                state_now,
            )

        run_max, run_sum, accum = lax.fori_loop(0, count, one_block, start_state)
        log_total = run_max + jnp.log(run_sum)
        attended = accum / jnp.transpose(run_sum)[:, :, None]
        attended_b = attended.reshape(block_rows, model_width).astype(jnp.bfloat16)
        middle = block_input + jnp.dot(attended_b, full_out, preferred_element_type=jnp.float32)
        normed_mid, normed_two, inv_two = norm_parts(middle, gain_two, bias_two)
        normed_mid_b = normed_mid.astype(jnp.bfloat16)
        hidden_pre = jnp.dot(normed_mid_b, full_up, preferred_element_type=jnp.float32)
        hidden_b = jax.nn.gelu(hidden_pre).astype(jnp.bfloat16)
        result = middle + jnp.dot(hidden_b, full_down, preferred_element_type=jnp.float32)
        previous = earlier[:, batch].astype(jnp.float32)
        mixed_out = (
            jnp.sum(mixing[:stream_count, None, None] * previous, axis=0)
            + mixing[stream_count] * result
        )
        next_list.append(mixed_out.astype(jnp.bfloat16))
        grad_out = grad_next[batch].astype(jnp.float32)
        earlier_list.append(
            (mixing[:stream_count, None, None] * grad_out[None]).astype(jnp.bfloat16)
        )
        mix_grad = jnp.concatenate(
            [jnp.sum(previous * grad_out[None], axis=(1, 2)), jnp.sum(result * grad_out)[None]]
        )
        grad_result = mixing[stream_count] * grad_out
        grad_result_b = grad_result.astype(jnp.bfloat16)
        grad_down = jnp.einsum(
            "rf,rd->fd", hidden_b, grad_result_b, preferred_element_type=jnp.float32
        )
        grad_hidden = jnp.einsum(
            "rd,fd->rf", grad_result_b, full_down, preferred_element_type=jnp.float32
        )
        grad_pre = jax.vjp(jax.nn.gelu, hidden_pre)[1](grad_hidden)[0]
        grad_pre_b = grad_pre.astype(jnp.bfloat16)
        grad_up = jnp.einsum(
            "rd,rf->df", normed_mid_b, grad_pre_b, preferred_element_type=jnp.float32
        )
        grad_norm_mid = jnp.einsum(
            "rf,df->rd", grad_pre_b, full_up, preferred_element_type=jnp.float32
        )
        grad_gain_two = jnp.sum(grad_norm_mid * normed_two, axis=0)
        grad_bias_two = jnp.sum(grad_norm_mid, axis=0)
        grad_middle = grad_result + norm_back(grad_norm_mid, normed_two, inv_two, gain_two)
        grad_middle_b = grad_middle.astype(jnp.bfloat16)
        grad_out_proj = jnp.einsum(
            "rd,re->de", attended_b, grad_middle_b, preferred_element_type=jnp.float32
        )
        grad_att_b = jnp.einsum(
            "re,de->rd", grad_middle_b, full_out, preferred_element_type=jnp.float32
        ).astype(jnp.bfloat16)
        row_delta = jnp.einsum(
            "qhe,qhe->hq", head_view(grad_att_b, head_count).astype(jnp.float32), attended
        )
        zero_rows = jnp.zeros((block_rows, model_width), jnp.float32)

        def key_visit(offset, grad_query, cycle_keys, cycle_values, cycle_dk, cycle_dv):
            their_block = order_row[(cycle_place - offset) % cycle_size]

            def add_pair(held):
                part_q, part_k, part_v = backward_pair(
                    local_query,
                    cycle_keys,
                    cycle_values,
                    grad_att_b,
                    log_total,
                    row_delta,
                    head_count,
                    score_scale,
                )
                return (held[0] + part_q, held[1] + part_k, held[2] + part_v)

            return lax.cond(
                their_block <= own_block,
                add_pair,
                lambda held: held,
                (grad_query, cycle_dk, cycle_dv),
            )

        def key_turn(offset, carry):
            grad_query, cycle_keys, cycle_values, cycle_dk, cycle_dv = carry
            grad_query, cycle_dk, cycle_dv = key_visit(
                offset, grad_query, cycle_keys, cycle_values, cycle_dk, cycle_dv
            )
            cycle_keys, cycle_values = passed_along((cycle_keys, cycle_values), "ctx", 1)
            cycle_dk, cycle_dv = (
                passed_along(cycle_dk.astype(jnp.bfloat16), "ctx", 1).astype(cycle_dk.dtype),
                passed_along(cycle_dv.astype(jnp.bfloat16), "ctx", 1).astype(cycle_dv.dtype),
            )
            return (grad_query, cycle_keys, cycle_values, cycle_dk, cycle_dv)

        grad_query, cycle_keys, cycle_values, cycle_dk, cycle_dv = lax.fori_loop(
            0, cycle_size - 1, key_turn, (zero_rows, local_keys, local_values, zero_rows, zero_rows)
        )
        grad_query, cycle_dk, cycle_dv = key_visit(
            cycle_size - 1, grad_query, cycle_keys, cycle_values, cycle_dk, cycle_dv
        )
        grad_keys, grad_values = (
            passed_along(cycle_dk.astype(jnp.bfloat16), "ctx", 1).astype(cycle_dk.dtype),
            passed_along(cycle_dv.astype(jnp.bfloat16), "ctx", 1).astype(cycle_dv.dtype),
        )
        grad_query_pre = unrotate(head_view(grad_query, head_count), cosine, sine_table).reshape(
            block_rows, model_width
        )
        grad_keys_pre = unrotate(head_view(grad_keys, head_count), cosine, sine_table).reshape(
            block_rows, model_width
        )
        grad_proj_b = jnp.concatenate([grad_query_pre, grad_keys_pre, grad_values], axis=1).astype(
            jnp.bfloat16
        )
        grad_in_proj = jnp.einsum(
            "rd,rf->df", normed_in_b, grad_proj_b, preferred_element_type=jnp.float32
        )
        grad_norm_in = jnp.einsum(
            "rf,df->rd", grad_proj_b, full_in, preferred_element_type=jnp.float32
        )
        grad_gain_one = jnp.sum(grad_norm_in * normed_one, axis=0)
        grad_bias_one = jnp.sum(grad_norm_in, axis=0)
        grad_block_in = grad_middle + norm_back(grad_norm_in, normed_one, inv_one, gain_one)
        grad_in_list.append(grad_block_in.astype(jnp.bfloat16))
        norm_grads = jnp.stack([grad_gain_one, grad_bias_one, grad_gain_two, grad_bias_two])
        mix_tiled = jnp.broadcast_to(mix_grad[None, :], (lax.axis_size("fsdp"), stream_count + 1))
        grad_terms = (grad_in_proj, grad_out_proj, grad_up, grad_down, norm_grads, mix_tiled)
        shares = (
            lax.psum_scatter(
                grad_terms[0].astype(jnp.bfloat16), "fsdp", scatter_dimension=0, tiled=True
            ).astype(jnp.float32),
            lax.psum_scatter(
                grad_terms[1].astype(jnp.bfloat16), "fsdp", scatter_dimension=0, tiled=True
            ).astype(jnp.float32),
            lax.psum_scatter(
                grad_terms[2].astype(jnp.bfloat16), "fsdp", scatter_dimension=0, tiled=True
            ).astype(jnp.float32),
            lax.psum_scatter(
                grad_terms[3].astype(jnp.bfloat16), "fsdp", scatter_dimension=0, tiled=True
            ).astype(jnp.float32),
            lax.psum_scatter(
                grad_terms[4].astype(jnp.bfloat16), "fsdp", scatter_dimension=1, tiled=True
            ).astype(jnp.float32),
            lax.psum_scatter(
                grad_terms[5].astype(jnp.bfloat16), "fsdp", scatter_dimension=0, tiled=True
            ).astype(jnp.float32),
        )
        totals = (
            shares
            if totals is None
            else tuple((first + second for first, second in zip(totals, shares)))
        )
    totals = lax.psum(totals, "ctx")
    norm_total = totals[4]
    return (
        jnp.stack(next_list),
        jnp.stack(grad_in_list),
        jnp.stack(earlier_list, axis=1),
        totals[0],
        totals[1],
        totals[2],
        totals[3],
        norm_total[0],
        norm_total[1],
        norm_total[2],
        norm_total[3],
        totals[5].reshape(-1),
    )


F32 = jnp.float32
BF16 = jnp.bfloat16
LOG2E = math.log2(math.e)
GELU_C = math.sqrt(2.0 / math.pi)
GELU_A = 0.044715
ANY = pl.ANY
VMEM = pltpu.VMEM
SMEM = pltpu.SMEM
MIB = 1 << 20


def mm(left, right, left_dim, right_dim):
    return lax.dot_general(
        left, right, (((left_dim,), (right_dim,)), ((), ())), preferred_element_type=F32
    )


def spec(space):
    return pl.BlockSpec(memory_space=space)


def shape_of(dims, kind):
    return jax.ShapeDtypeStruct(dims, kind)


def run_kernel(kernel, name, operands, spaces, outs, scratch, flops, limit=56):
    moved = sum(o.size * o.dtype.itemsize for o in operands) + sum(
        math.prod(o.shape) * jnp.dtype(o.dtype).itemsize for o in outs
    )
    return pl.pallas_call(
        kernel,
        name=name,
        in_specs=[spec(s) for s in spaces],
        out_specs=[spec(VMEM) for _ in outs],
        out_shape=outs,
        scratch_shapes=scratch,
        compiler_params=pltpu.CompilerParams(vmem_limit_bytes=limit * MIB),
        cost_estimate=pl.CostEstimate(
            flops=int(flops), bytes_accessed=int(moved), transcendentals=0
        ),
    )(*operands)


def block_index(scalars, order):
    place = scalars[1]
    return lax.bitwise_xor(place, jnp.int32((0, 2, 1, 3)[order]))


def early_kernel(mix, earlier, grad, out_grad, out_prev, out_mix):
    streams = earlier.shape[0]
    rows = grad.shape[0]
    step = 128

    out_mix[...] = jnp.zeros_like(out_mix)

    def one(index, carry):
        here = pl.ds(pl.multiple_of(index * step, step), step)
        g = grad[here, :].astype(F32)
        total = None
        for k in range(streams):
            e = earlier[k, here, :].astype(F32)
            out_grad[k, here, :] = (mix[k] * g).astype(BF16)
            out_mix[k : k + 1, :] += jnp.sum(e * g, axis=0, keepdims=True)
            total = mix[k] * e if total is None else total + mix[k] * e
        out_prev[here, :] = total
        return carry

    lax.fori_loop(0, rows // step, one, 0)


def full_rows(pieces, first, last):
    total = None
    for piece in pieces:
        term = piece[first:last, :].astype(F32)
        total = term if total is None else total + term
    return total


def qkv_kernel(hps, batches, has_x, offset, *refs):
    if has_x:
        scalars, x, cosine, sine, w0, w1, w2, w3 = refs[:8]
        out, n1t, norms, weight = refs[8:]
        rows = n1t.shape[0] // 4
        parts = full_rows((w0, w1, w2, w3), rows, rows + 16)
        norms[...] = parts[0:8, :] + parts[8:16, :]
        v = x[...].astype(F32)
        center = v - jnp.mean(v, axis=-1, keepdims=True)
        inv = lax.rsqrt(jnp.mean(center * center, axis=-1, keepdims=True) + 1e-05)
        n1 = center * inv * norms[0:1, :] + norms[1:2, :]
        n1t[...] = n1.astype(BF16).T
    else:
        scalars, n1t, cosine, sine, w0, w1, w2, w3 = refs[:8]
        out, weight = refs[8:]
        rows = n1t.shape[0] // 4
    for order, piece in enumerate((w0, w1, w2, w3)):
        start = pl.multiple_of(block_index(scalars, order) * rows, rows)
        weight[pl.ds(start, rows), :] = piece[offset : offset + rows, :]
    width = weight.shape[1] // 3
    size = width // hps
    half = size // 2
    tokens = n1t.shape[1] // batches
    for part in range(3):
        cols = mm(weight[:, part * width : (part + 1) * width], n1t[...], 0, 0)
        for head in range(hps):
            for batch in range(batches):
                lanes = slice(batch * tokens, (batch + 1) * tokens)
                top = cols[head * size : head * size + half, lanes]
                low = cols[head * size + half : (head + 1) * size, lanes]
                if part < 2:
                    c = cosine[batch]
                    s = sine[batch]
                    top, low = top * c - low * s, low * c + top * s
                slot = batch * hps + head
                out[slot, part * size : part * size + half, :] = top.astype(BF16)
                out[slot, part * size + half : (part + 1) * size, :] = low.astype(BF16)


def stream_tile(count, stream, step):
    long = count - stream
    late = step >= long
    query = jnp.where(late, stream, count - 1 - stream)
    return query, jnp.where(late, step - long, step)


def attend_kernel(count, scale, ids, ins, outs, ot, lse, qt, kk, vt, scores, *states):
    streams = count // 2
    tops, totals, accs = states[:streams], states[streams : 2 * streams], states[2 * streams :]
    size = qt.shape[1]
    factor = scale * LOG2E
    for d in range(count):
        slot = ids[d]
        qt[slot] = ins[d, 0:size, :]
        kk[slot] = ins[d, size : 2 * size, :].T
        vt[slot] = ins[d, 2 * size :, :]
    for r in range(streams):
        tops[r][...] = jnp.full_like(tops[r], -1e30)
        totals[r][...] = jnp.zeros_like(totals[r])
        accs[r][...] = jnp.zeros_like(accs[r])
        scores[0, r] = mm(kk[0], qt[count - 1 - r], 1, 0)

    def step(index, carry):
        for r in range(streams):
            i, j = stream_tile(count, r, jnp.minimum(index + 1, count))
            scores[(index + 1) % 2, r] = mm(kk[j], qt[i], 1, 0)
        for r in range(streams):
            i, j = stream_tile(count, r, index)
            half = jnp.where(index >= count - r, 1, 0)
            s = scores[index % 2, r]
            old = tops[r][half]
            new = jnp.maximum(old, jnp.max(s, axis=0, keepdims=True) * factor)
            shrink = jnp.exp2(old - new)
            p = jnp.exp2(s * factor - new)
            totals[r][half] = totals[r][half] * shrink + jnp.sum(p, axis=0, keepdims=True)
            accs[r][half] = accs[r][half] * shrink + mm(vt[j], p.astype(BF16), 1, 0)
            tops[r][half] = new
        return carry

    lax.fori_loop(0, count + 1, step, 0)
    for r in range(streams):
        for half, i in enumerate((count - 1 - r, r)):
            run = totals[r][half]
            ot[i] = accs[r][half] / run
            lse[i] = tops[r][half] + jnp.log2(run)
    for d in range(count):
        outs[d] = ot[ids[d]].astype(BF16)


def attend_back_kernel(
    count, scale, stage, ids, ins, grads, ot, lse, outs, qt, qq, kt, kk, vv, gt, gg, delta, scores, gains, *sums
):
    streams = count // 2
    dqs, dks, dvs = sums[:streams], sums[streams : 2 * streams], sums[2 * streams :]
    size = qt.shape[1]
    factor = scale * LOG2E
    for d in range(count):
        slot = ids[d]
        block = ins[d]
        q = block[0:size]
        k = block[size : 2 * size]
        qt[slot] = q
        kt[slot] = k
        qq[slot] = q.T
        kk[slot] = k.T
        vv[slot] = block[2 * size :].T
        g = grads[d, stage * size : (stage + 1) * size, :]
        gt[slot] = g
        gg[slot] = g.T
        delta[slot] = jnp.sum(g.astype(F32) * ot[slot], axis=0, keepdims=True)
    for r in range(streams):
        dqs[r][...] = jnp.zeros_like(dqs[r])
        dks[r][...] = jnp.zeros_like(dks[r])
        dvs[r][...] = jnp.zeros_like(dvs[r])
        scores[0, r] = mm(kk[0], qt[count - 1 - r], 1, 0)
        gains[0, r] = mm(vv[0], gt[count - 1 - r], 1, 0)

    def step(index, carry):
        for r in range(streams):
            i, j = stream_tile(count, r, jnp.minimum(index + 1, count))
            scores[(index + 1) % 2, r] = mm(kk[j], qt[i], 1, 0)
            gains[(index + 1) % 2, r] = mm(vv[j], gt[i], 1, 0)
        for r in range(streams):
            i, j = stream_tile(count, r, index)
            half = jnp.where(index >= count - r, 1, 0)
            p = jnp.exp2(scores[index % 2, r] * factor - lse[i])
            ds = (p * (gains[index % 2, r] - delta[i])).astype(BF16)
            dqs[r][half] += mm(kt[j], ds, 1, 0)
            dks[r][j] += mm(ds, qq[i], 1, 0)
            dvs[r][j] += mm(p.astype(BF16), gg[i], 1, 0)
        return carry

    lax.fori_loop(0, count + 1, step, 0)
    for r in range(streams):
        for half, i in enumerate((count - 1 - r, r)):
            qt[i] = (dqs[r][half] * scale).astype(BF16)
    for d in range(count):
        slot = ids[d]
        outs[d, 0:size, :] = qt[slot]
        dk = dks[0][slot]
        dv = dvs[0][slot]
        for r in range(1, streams):
            dk = dk + dks[r][slot]
            dv = dv + dvs[r][slot]
        outs[d, size : 2 * size, :] = (dk * scale).astype(BF16).T
        outs[d, 2 * size :, :] = dv.astype(BF16).T


def gather_rows(scalars, pieces, window, target, sems, base):
    copies = []
    first, rows = window
    for order, piece in enumerate(pieces):
        start = pl.multiple_of(block_index(scalars, order) * rows, rows)
        copy = pltpu.make_async_copy(
            piece.at[pl.ds(first, rows), :], target.at[pl.ds(start, rows), :], sems.at[base + order]
        )
        copy.start()
        copies.append(copy)
    return copies


def mlp_kernel(count, stages, hps, batches, scalars, mix, x, grad, norms, *refs):
    heads = refs[0]
    pieces = refs[1:5]
    refs = refs[5:]
    hidden, dhidden, n2_out, mid_out, dmid_out, dmid_low, ot, norm_grads = refs[:8]
    head_grads = refs[8]
    out_scr, up_scr, down_scr, dn2, got, sems = refs[9:]
    width = x.shape[1]
    size = ot.shape[2]
    share = width // 4
    groups = up_scr.shape[1] // width
    deep = down_scr.shape[0] // 4
    last = (groups * share) + deep
    copies_out = gather_rows(scalars, pieces, (last, share), out_scr, sems, 0)
    copies_up = []
    for group in range(groups):
        lanes = up_scr.at[:, pl.ds(group * width, width)]
        copies_up += gather_rows(scalars, pieces, (group * share, share), lanes, sems, 4 + 4 * group)
    copies_down = gather_rows(
        scalars, pieces, (groups * share, deep), down_scr, sems, 4 + 4 * groups
    )
    for stage in range(stages):
        for slot in range(count):
            ot[slot // hps, stage * hps + slot % hps] = heads[
                slot, stage * size : (stage + 1) * size, :
            ]
    for copy in copies_out:
        copy.wait()
    tokens = x.shape[0] // batches
    for batch in range(batches):
        rows = slice(batch * tokens, (batch + 1) * tokens)
        attended = ot[batch].reshape(width, tokens)
        middle = x[rows, :].astype(F32) + mm(attended, out_scr[...], 0, 0)
        mid_out[rows, :] = middle
        center = middle - jnp.mean(middle, axis=-1, keepdims=True)
        inv = lax.rsqrt(jnp.mean(center * center, axis=-1, keepdims=True) + 1e-05)
        n2_out[rows, :] = (center * inv * norms[2:3, :] + norms[3:4, :]).astype(BF16)
    for copy in copies_up + copies_down:
        copy.wait()
    dn2[...] = jnp.zeros_like(dn2)
    dy = (mix[mix.shape[0] - 1] * grad[...].astype(F32)).astype(BF16)
    step = 512 if up_scr.shape[1] % 512 == 0 else 128

    def one(index, carry):
        here = pl.ds(pl.multiple_of(index * step, step), step)
        up = up_scr[:, here]
        u = mm(n2_out[...], up, 1, 0)
        da = mm(dy, down_scr[here, :], 1, 1)
        square = u * u
        bend = jnp.tanh(u * (GELU_C + (GELU_C * GELU_A) * square))
        gate = 0.5 + 0.5 * bend
        hidden[:, here] = (u * gate).astype(BF16)
        slope = gate + (0.5 * u) * (1.0 - bend * bend) * (
            GELU_C + (3.0 * GELU_C * GELU_A) * square
        )
        du = (da * slope).astype(BF16)
        dhidden[:, here] = du
        dn2[...] += mm(du, up, 1, 1)
        return carry

    lax.fori_loop(0, up_scr.shape[1] // step, one, 0)
    gain_sum = None
    for batch in range(batches):
        rows = slice(batch * tokens, (batch + 1) * tokens)
        middle = mid_out[rows, :]
        center = middle - jnp.mean(middle, axis=-1, keepdims=True)
        inv = lax.rsqrt(jnp.mean(center * center, axis=-1, keepdims=True) + 1e-05)
        z = center * inv
        dn = dn2[rows, :]
        part_gain = jnp.sum(dn * z, axis=0, keepdims=True)
        part_bias = jnp.sum(dn, axis=0, keepdims=True)
        gain_sum = part_gain if gain_sum is None else gain_sum + part_gain
        bias_sum = part_bias if batch == 0 else bias_sum + part_bias
        h = dn * norms[2:3, :]
        back = inv * (
            h - jnp.mean(h, axis=-1, keepdims=True) - z * jnp.mean(h * z, axis=-1, keepdims=True)
        )
        dmid = mix[mix.shape[0] - 1] * grad[rows, :].astype(F32) + back
        dmid_out[rows, :] = dmid
        low = dmid.astype(BF16)
        dmid_low[rows, :] = low
        got[batch] = mm(out_scr[...], low, 1, 1).astype(BF16).reshape(got.shape[1:])
    norm_grads[...] = jnp.zeros_like(norm_grads)
    norm_grads[0:1, :] = gain_sum
    norm_grads[1:2, :] = bias_sum
    for stage in range(stages):
        for slot in range(count):
            head_grads[slot, stage * size : (stage + 1) * size, :] = got[
                slot // hps, stage * hps + slot % hps
            ]


def result_kernel(window, scalars, mix, hidden, mid, prev, grad, w0, w1, w2, w3, out, out_mix, acc):
    acc[...] = mid[...]
    first, rows = window
    for order, piece in enumerate((w0, w1, w2, w3)):
        start = pl.multiple_of(block_index(scalars, order) * rows, rows)
        acc[...] += mm(hidden[:, pl.ds(start, rows)], piece[first : first + rows, :], 1, 0)
    y = acc[...]
    out[...] = (prev[...] + mix[mix.shape[0] - 1] * y).astype(BF16)
    out_mix[...] = jnp.zeros_like(out_mix)
    out_mix[0:1, :] = jnp.sum(grad[...].astype(F32) * y, axis=0, keepdims=True)


def put_pieces(me, value, outs, order, count, first):
    target = outs[order // 2]
    rows = value.shape[0] // count
    low = value.astype(BF16)
    for sub in range(count):
        slot = lax.bitwise_xor(me, jnp.int32(sub))
        target[order % 2, lax.rem(slot, jnp.int32(2)), lax.div(slot, jnp.int32(2)), first : first + rows, :] = (
            low[sub * rows : (sub + 1) * rows, :]
        )


def down_grad_kernel(count, scalars, mix, hidden, grad, keep, send):
    dy = (mix[mix.shape[0] - 1] * grad[...].astype(F32)).astype(BF16)
    rows = count * keep.shape[3]
    for order in range(4):
        start = pl.multiple_of(block_index(scalars, order) * rows, rows)
        value = mm(hidden[:, pl.ds(start, rows)], dy, 0, 0)
        put_pieces(scalars[0], value, (keep, send), order, count, 0)


def up_out_grad_kernel(count, scalars, n2, dhidden, ot, dmid, keep, send, left, whole):
    batches = ot.shape[0]
    width = n2.shape[1]
    tokens = ot.shape[3]
    rows = width // 4
    thin = rows // count

    def arrange():
        for order in range(4):
            here = pl.ds(pl.multiple_of(block_index(scalars, order) * rows, rows), rows)
            left[order * rows : (order + 1) * rows, :] = whole[here, :]

    whole[...] = n2[...].T
    arrange()
    groups = dhidden.shape[1] // width
    for group in range(groups):
        value = mm(left[...], dhidden[:, group * width : (group + 1) * width], 1, 0)
        for order in range(4):
            put_pieces(
                scalars[0],
                value[order * rows : (order + 1) * rows, :],
                (keep, send),
                order,
                count,
                group * thin,
            )
    for batch in range(batches):
        whole[:, batch * tokens : (batch + 1) * tokens] = ot[batch].reshape(width, tokens)
    arrange()
    value = mm(left[...], dmid[...], 1, 0)
    for order in range(4):
        put_pieces(
            scalars[0],
            value[order * rows : (order + 1) * rows, :],
            (keep, send),
            order,
            count,
            groups * thin,
        )


def grads_kernel(count, window, scalars, mix, hidden, mid, prev, grad, w0, w1, w2, w3, n2, dhidden, ot, dmid, *refs):
    down, up, (out, out_mix), (acc, left, whole) = refs[:2], refs[2:4], refs[4:6], refs[6:]
    down_grad_kernel(count, scalars, mix, hidden, grad, *down)
    up_out_grad_kernel(count, scalars, n2, dhidden, ot, dmid, *up, left, whole)
    result_kernel(window, scalars, mix, hidden, mid, prev, grad, w0, w1, w2, w3, out, out_mix, acc)


def in_grad_kernel(count, hps, natural, scalars, cosine, sine, n1t, *refs):
    stages = (len(refs) - 3) // 2
    dts = refs[stages : 2 * stages]
    keep, send, left = refs[2 * stages :]
    batches = dts[0].shape[0]
    size = dts[0].shape[3]
    half = size // 2
    tokens = dts[0].shape[4]
    width = n1t.shape[0]
    rows = width // 4
    thin = rows // count
    for order in range(4):
        here = pl.ds(pl.multiple_of(block_index(scalars, order) * rows, rows), rows)
        left[order * rows : (order + 1) * rows, :] = n1t[here, :]
    cols = 3 * hps * size
    for stage in range(stages):
        grads = refs[stage]
        dt = dts[stage]
        for slot in range(count):
            batch, head = slot // hps, slot % hps
            c = cosine[batch]
            s = sine[batch]
            for part in range(2):
                top = grads[slot, part * size : part * size + half, :].astype(F32)
                low = grads[slot, part * size + half : (part + 1) * size, :].astype(F32)
                dt[batch, part, head, 0:half, :] = (top * c + low * s).astype(BF16)
                dt[batch, part, head, half:size, :] = (low * c - top * s).astype(BF16)
            dt[batch, 2, head] = grads[slot, 2 * size :, :]
        value = None
        for batch in range(batches):
            term = mm(
                left[:, batch * tokens : (batch + 1) * tokens],
                dt[batch].reshape(cols, tokens),
                1,
                1,
            )
            value = term if value is None else value + term
        low = value.astype(BF16)
        for order in range(4):
            if natural:
                target = (keep, send)[order // 2]
                for sub in range(count):
                    start = order * rows + sub * thin
                    target[order % 2, sub] = low[start : start + thin, :]
            else:
                put_pieces(
                    scalars[0],
                    low[order * rows : (order + 1) * rows, :],
                    (keep, send),
                    order,
                    count,
                    stage * thin,
                )


def input_grad_kernel(stages, windows, scalars, x, norms, dmid, *refs):
    dts = refs[:stages]
    pieces = refs[stages : stages + 4 * stages]
    out, norm_grads, weights, sems = refs[5 * stages :]
    copies = []
    for stage in range(stages):
        copies += gather_rows(
            scalars,
            pieces[4 * stage : 4 * stage + 4],
            windows[stage],
            weights.at[stage],
            sems,
            4 * stage,
        )
    for copy in copies:
        copy.wait()
    batches = dts[0].shape[0]
    tokens = dts[0].shape[4]
    cols = weights.shape[2]
    gain_sum = bias_sum = None
    for batch in range(batches):
        rows = slice(batch * tokens, (batch + 1) * tokens)
        dnt = None
        for stage in range(stages):
            term = mm(weights[stage], dts[stage][batch].reshape(cols, tokens), 1, 0)
            dnt = term if dnt is None else dnt + term
        dn = dnt.T
        v = x[rows, :].astype(F32)
        center = v - jnp.mean(v, axis=-1, keepdims=True)
        inv = lax.rsqrt(jnp.mean(center * center, axis=-1, keepdims=True) + 1e-05)
        z = center * inv
        part_gain = jnp.sum(dn * z, axis=0, keepdims=True)
        part_bias = jnp.sum(dn, axis=0, keepdims=True)
        gain_sum = part_gain if batch == 0 else gain_sum + part_gain
        bias_sum = part_bias if batch == 0 else bias_sum + part_bias
        h = dn * norms[0:1, :]
        back = inv * (
            h - jnp.mean(h, axis=-1, keepdims=True) - z * jnp.mean(h * z, axis=-1, keepdims=True)
        )
        out[rows, :] = (dmid[rows, :] + back).astype(BF16)
    norm_grads[...] = jnp.zeros_like(norm_grads)
    norm_grads[0:1, :] = gain_sum
    norm_grads[1:2, :] = bias_sum


def far_offsets(count):
    offsets = [0]
    bit = count // 2
    while bit > 2:
        offsets += [offset ^ bit for offset in offsets]
        bit //= 2
    return offsets


def place_kernel(count, moves, scalars, *refs):
    parts = refs[: min(count, 4)]
    outs = refs[len(parts) :]
    for low, source in enumerate(parts):
        for sub, offset in enumerate(far_offsets(count)):
            slot = lax.bitwise_xor(scalars[0], jnp.int32(offset + low))
            for out, first, rows, begin, wide, to in moves:
                outs[out][slot, :, to : to + wide] = source[
                    sub, first : first + rows, begin : begin + wide
                ].astype(F32)


def place_in_kernel(count, moves, width, wide, thin, scalars, *refs):
    *parts, last, out = refs
    place_kernel(count, moves, scalars, *parts, out)
    final = len(moves) // 3
    for sub in range(last.shape[0]):
        for part in range(3):
            to = part * width + final * wide
            out[sub, :, to : to + wide] = last[sub, :, part * wide : (part + 1) * wide].astype(F32)


def exchange(value, axis, bit):
    size = lax.axis_size(axis)
    return lax.ppermute(value, axis, [(i, i ^ bit) for i in range(size)])


def added(left, right):
    return (left.astype(F32) + right.astype(F32)).astype(BF16)


def swapped(value, groups=None):
    return lax.all_to_all(value, "ctx", 0, 0, axis_index_groups=groups)


def summed(value):
    return jnp.sum(value.astype(F32), axis=0).astype(BF16)


def spread(own, count, groups=None):
    return swapped(jnp.broadcast_to(own[None], (count, *own.shape)), groups)


def total(terms):
    value = terms[0].astype(F32)
    for term in terms[1:]:
        value = value + term.astype(F32)
    return value.astype(BF16)


class Chain:
    def __init__(self, keep, send, order):
        count = lax.axis_size("ctx")
        self.labels = ["x", 1]
        bit = count // 2
        while bit > 1:
            self.labels.append(bit)
            bit //= 2
        dims = (2,) * len(self.labels) + keep.shape[3:]
        self.terms = [keep.reshape(dims), exchange(send, "fsdp", 1).reshape(dims)]
        self.order = list(order)

    def step(self, *holds):
        label = self.order.pop(0)
        axis = self.labels.index(label)
        if holds:
            self.terms[-1] = after(self.terms[-1], *holds)
        sent = total([lax.index_in_dim(t, 1, axis, keepdims=False) for t in self.terms])
        got = exchange(sent, *(("fsdp", 2) if label == "x" else ("ctx", label)))
        self.terms = [lax.index_in_dim(t, 0, axis, keepdims=False) for t in self.terms] + [got]
        self.labels.pop(axis)
        return sent

    def finish(self):
        while self.order:
            self.step()
        return total(self.terms)


def gather_blocks(own, last):
    count = lax.axis_size("ctx")
    held = own[None]
    bit = count // 2
    while bit > 2:
        held = jnp.concatenate([held, exchange(held, "ctx", bit)])
        bit //= 2
    parts = [held] + [exchange(held, "ctx", bit) for bit in (1, 2) if bit < count]
    if count > 2:
        parts.append(exchange(parts[3 - last], "ctx", last))
    return parts


def halved(keep, send):
    got = exchange(send, "fsdp", 1)
    passed = added(keep[1], got[1])
    return total([keep[0], got[0], exchange(passed, "fsdp", 2)]), passed


def reduce_whole(blocks, extra):
    count, rows = blocks.shape[:2]
    extra = jnp.broadcast_to(extra.astype(BF16)[None], (count, *extra.shape))
    sums = jnp.sum(swapped(jnp.concatenate([blocks, extra], axis=1)).astype(F32), axis=0)
    return spread(sums[:rows].astype(BF16), count), sums[rows:]


def after(value, *others):
    return lax.optimization_barrier((value, *others))[0]


def gathered(shard):
    other_chip = exchange(shard, "fsdp", 2)
    return [shard, other_chip, exchange(shard, "fsdp", 1), exchange(other_chip, "fsdp", 1)]


def head_body(
    inputs,
    earlier,
    input_proj,
    output_proj,
    up_proj,
    down_proj,
    norm1_gain,
    norm1_bias,
    norm2_gain,
    norm2_bias,
    mixing,
    block_order,
    grad_next,
):
    batches, tokens, width = inputs.shape
    rows = batches * tokens
    heads = HEADS
    size = width // heads
    scale = size ** (-0.5)
    streams = earlier.shape[0]
    count = lax.axis_size("ctx")
    hps = count // batches
    stages = heads // hps
    inner = down_proj.shape[0] * 4
    me = lax.axis_index("ctx").astype(jnp.int32)
    place = lax.axis_index("fsdp").astype(jnp.int32)
    scalars = jnp.stack([me, place])
    ids = block_order[me // hps].astype(jnp.int32)
    x = inputs.reshape(rows, width)
    grad = grad_next.reshape(rows, width)

    share = width // 4
    cols = 3 * hps * size
    norm_stack = jnp.stack([norm1_gain, norm1_bias, norm2_gain, norm2_bias])
    coarse = lax.reduce_precision(norm_stack, 8, 7)
    norm_rows = jnp.zeros((16, width), BF16)
    norm_rows = lax.dynamic_update_slice(norm_rows, coarse.astype(BF16), (0, place * share))
    norm_rows = lax.dynamic_update_slice(
        norm_rows, (norm_stack - coarse).astype(BF16), (8, place * share)
    )
    wide = hps * size
    chunks = [
        jnp.concatenate(
            [input_proj[:, p * width + s * wide : p * width + (s + 1) * wide] for p in range(3)], 1
        )
        for s in range(stages)
    ]
    first_in = gathered(jnp.concatenate([chunks[0], jnp.pad(norm_rows, ((0, 0), (0, cols - width)))]))
    rest_in = gathered(after(jnp.concatenate(chunks[1:]), first_in[1]))
    groups = inner // width
    up_rows = jnp.moveaxis(up_proj.reshape(share, groups, width), 1, 0).reshape(-1, width)
    packed = jnp.concatenate([up_rows, down_proj, output_proj])

    half = size // 2
    own_blocks = block_order[:, me]
    positions = (own_blocks[:, None] * tokens + lax.iota(jnp.int32, tokens)[None]).astype(F32)
    freqs = jnp.exp(lax.iota(F32, half) * (-2.0 * math.log(10000.0) / size))
    angle = freqs[None, :, None] * positions[:, None, :]
    cosine = jnp.cos(angle)
    sine = jnp.sin(angle)

    grad_earlier, prev, mix_early = run_kernel(
        early_kernel,
        "early",
        [mixing, earlier.reshape(streams, rows, width), grad],
        [SMEM, VMEM, VMEM],
        [
            shape_of((streams, rows, width), BF16),
            shape_of((rows, width), F32),
            shape_of((8, width), F32),
        ],
        [],
        6 * streams * rows * width,
    )

    pair_shape = shape_of((count, 3 * size, tokens), BF16)
    x = after(x, mix_early)
    packed = after(packed, rest_in[1])
    weights = [packed, exchange(packed, "fsdp", 2), exchange(packed, "fsdp", 1)]
    made = []
    n1t = norms = None
    windows = [(0, share)] + [(share * s, share) for s in range(stages - 1)]
    for s in range(stages):
        first = s == 0
        operands = [scalars] + ([x] if first else [n1t]) + [cosine, sine]
        operands += first_in if first else rest_in
        outs = [pair_shape]
        if first:
            outs += [shape_of((width, rows), BF16), shape_of((8, width), F32)]
        result = run_kernel(
            functools.partial(qkv_kernel, hps, batches, first, windows[s][0]),
            "qkv",
            operands,
            [SMEM] + [VMEM] * (len(operands) - 1),
            outs,
            [pltpu.VMEM((width, cols), BF16)],
            2 * rows * width * cols,
        )
        if first:
            n1t, norms = result[1:]
        made.append(result[0])

    tiles = count * (count + 1) // 2
    one = tokens * tokens * size * 2
    streams_in = count // 2
    head_shape = shape_of((count, size, tokens), BF16)
    held = []
    attended = []
    saved = []
    for s in range(stages):
        while len(held) < min(s + 2, stages):
            held.append(swapped(after(made[len(held)], *([saved[-1][1]] if saved else []))))
        result = run_kernel(
            functools.partial(attend_kernel, count, scale),
            "attend",
            [after(ids, saved[-1][1]) if saved else ids, held[s]],
            [SMEM, VMEM],
            [head_shape, shape_of((count, size, tokens), F32), shape_of((count, 1, tokens), F32)],
            [
                pltpu.VMEM((count, size, tokens), BF16),
                pltpu.VMEM((count, tokens, size), BF16),
                pltpu.VMEM((count, size, tokens), BF16),
                pltpu.VMEM((2, streams_in, tokens, tokens), F32),
            ]
            + [pltpu.VMEM((2, 1, tokens), F32)] * (2 * streams_in)
            + [pltpu.VMEM((2, size, tokens), F32)] * streams_in,
            4 * 2 * one * tiles,
        )
        saved.append(result[1:])
        attended.append(result[0])

    weights.append(exchange(after(weights[1], saved[-2][1]), "fsdp", 1))
    result = run_kernel(
        functools.partial(mlp_kernel, count, stages, hps, batches),
        "mlp",
        [scalars, mixing, x, grad, norms, swapped(jnp.concatenate(attended, axis=1))] + weights,
        [SMEM, SMEM, VMEM, VMEM, VMEM, VMEM] + [ANY] * 4,
        [
            shape_of((rows, inner), BF16),
            shape_of((rows, inner), BF16),
            shape_of((rows, width), BF16),
            shape_of((rows, width), F32),
            shape_of((rows, width), F32),
            shape_of((rows, width), BF16),
            shape_of((batches, heads, size, tokens), BF16),
            shape_of((8, width), F32),
            shape_of((count, stages * size, tokens), BF16),
        ],
        [
            pltpu.VMEM((width, width), BF16),
            pltpu.VMEM((width, inner), BF16),
            pltpu.VMEM((inner, width), BF16),
            pltpu.VMEM((rows, width), F32),
            pltpu.VMEM((batches, heads, size, tokens), BF16),
            pltpu.SemaphoreType.DMA((8 + 4 * groups,)),
        ],
        6 * rows * width * inner,
    )
    hidden, dhidden, n2, mid, dmid, dmid_low, ot, norm2_grads = result[:8]
    head_grads = swapped(result[8])

    sub = inner // 4 // count
    thin = share // count
    result = run_kernel(
        functools.partial(grads_kernel, count, (groups * share, inner // 4)),
        "grads",
        [scalars, mixing, hidden, mid, prev, grad] + weights + [n2, dhidden, ot, dmid_low],
        [SMEM, SMEM] + [VMEM] * 12,
        [shape_of((2, 2, count // 2, sub, width), BF16)] * 2
        + [shape_of((2, 2, count // 2, thin * (groups + 1), width), BF16)] * 2
        + [shape_of((rows, width), BF16), shape_of((8, width), F32)],
        [
            pltpu.VMEM((rows, width), F32),
            pltpu.VMEM((width, rows), BF16),
            pltpu.VMEM((width, rows), BF16),
        ],
        2 * rows * width * (3 * inner + width),
    )
    down_sums, up_sums, (next_input, mix_last) = result[:2], result[2:4], result[4:]

    def in_grads(arrived, natural):
        few = len(arrived)
        lead = (2, count, thin) if natural else (2, 2, count // 2, few * thin)
        result = run_kernel(
            functools.partial(in_grad_kernel, count, hps, natural),
            "in_grad",
            [scalars, cosine, sine, n1t] + arrived,
            [SMEM] + [VMEM] * (3 + few),
            [shape_of((batches, 3, hps, size, tokens), BF16)] * few
            + [shape_of((*lead, cols), BF16)] * 2,
            [pltpu.VMEM((width, rows), BF16)],
            2 * few * rows * width * cols,
        )
        return list(result[:few]), result[few:]

    far_bits = [1 << k for k in range(1, count.bit_length() - 1)]
    down_chain = Chain(down_sums[0], after(down_sums[1], head_grads), ["x", 1] + far_bits)
    up_chain = Chain(up_sums[0], after(up_sums[1], head_grads), [1, "x"] + far_bits)

    dts = []
    back = [mix_last]
    moved = []
    for s in range(stages):
        turn = [back[-1]]
        if s:
            turn.append(down_chain.step(back[-1]))
        if s == 1:
            turn.append(up_chain.step(back[-1]))
        if s > 1:
            turn.append(moved[s - 2])
        (value,) = run_kernel(
            functools.partial(attend_back_kernel, count, scale, s),
            "attend_back",
            [ids, after(held[s], *turn), head_grads] + list(saved[s]),
            [SMEM] + [VMEM] * 4,
            [pair_shape],
            [
                pltpu.VMEM((count, size, tokens), BF16),
                pltpu.VMEM((count, tokens, size), BF16),
                pltpu.VMEM((count, size, tokens), BF16),
                pltpu.VMEM((count, tokens, size), BF16),
                pltpu.VMEM((count, tokens, size), BF16),
                pltpu.VMEM((count, size, tokens), BF16),
                pltpu.VMEM((count, tokens, size), BF16),
                pltpu.VMEM((count, 1, tokens), F32),
                pltpu.VMEM((2, streams_in, tokens, tokens), F32),
                pltpu.VMEM((2, streams_in, tokens, tokens), F32),
            ]
            + [pltpu.VMEM((2, size, tokens), F32)] * streams_in
            + [pltpu.VMEM((count, tokens, size), F32)] * (2 * streams_in),
            4 * 5 * one * tiles,
        )
        back.append(value)
        moved.append(swapped(after(value, *moved[-1:])))
    early_dts, early_sums = in_grads([after(moved[0], back[-1])] + moved[1:-1], False)
    last_dts, last_sums = in_grads(moved[-1:], True)
    dts = early_dts + last_dts
    up_chain.step(back[-1])
    down_chain.step(last_dts[0])
    up_chain.step(last_dts[0])
    early_chain = Chain(*early_sums, ["x", 1] + far_bits)
    last_blocks, last_passed = halved(*last_sums)
    early_chain.step()
    down_chain.step(last_passed)
    up_chain.step(last_passed)
    early_parts = gather_blocks(early_chain.finish(), 1)
    down_parts = gather_blocks(down_chain.finish(), 1)
    up_parts = gather_blocks(up_chain.finish(), 2)

    grad_input, norm1_grads = run_kernel(
        functools.partial(input_grad_kernel, stages, windows),
        "input_grad",
        [scalars, x, norms, dmid] + dts + first_in + rest_in * (stages - 1),
        [SMEM] + [VMEM] * (3 + stages) + [ANY] * (4 * stages),
        [shape_of((rows, width), BF16), shape_of((8, width), F32)],
        [pltpu.VMEM((stages, width, cols), BF16), pltpu.SemaphoreType.DMA((4 * stages,))],
        2 * rows * width * 3 * width,
    )

    mix_sums = jnp.sum(jnp.concatenate([mix_early[:streams], mix_last[:1]], axis=0), axis=1)
    mix_row = jnp.pad(mix_sums, (0, width - streams - 1))
    small = jnp.concatenate([norm1_grads[:2], norm2_grads[:2], mix_row[None]], axis=0)
    small = small + exchange(small, "fsdp", 1)
    small = small + exchange(small, "fsdp", 2)
    mix_high = lax.reduce_precision(small[4:], 8, 7)
    zeros = jnp.zeros((2, width), F32)
    small = jnp.concatenate([small[:4], mix_high, small[4:] - mix_high, zeros], axis=0)
    last_parts, small = reduce_whole(last_blocks, small)
    norm_total = lax.dynamic_slice_in_dim(small[:4], place * share, share, 1)
    mix_total = small[4, : streams + 1] + small[5, : streams + 1]

    (grad_down,) = run_kernel(
        functools.partial(place_kernel, count, ((0, 0, sub, 0, width, 0),)),
        "place_down",
        [scalars, *down_parts],
        [SMEM] + [VMEM] * len(down_parts),
        [shape_of((count, sub, width), F32)],
        [],
        0,
    )
    moves = tuple((0, g * thin, thin, 0, width, g * width) for g in range(groups))
    grad_up, grad_out = run_kernel(
        functools.partial(place_kernel, count, moves + ((1, groups * thin, thin, 0, width, 0),)),
        "place_up",
        [scalars, *up_parts],
        [SMEM] + [VMEM] * len(up_parts),
        [shape_of((count, thin, inner), F32), shape_of((count, thin, width), F32)],
        [],
        0,
    )
    wide = hps * size
    moves = tuple(
        (0, g * thin, thin, part * wide, wide, part * width + g * wide)
        for g in range(stages - 1)
        for part in range(3)
    )
    (grad_in,) = run_kernel(
        functools.partial(place_in_kernel, count, moves, width, wide, thin),
        "place_in",
        [scalars, *early_parts, last_parts],
        [SMEM] + [VMEM] * (len(early_parts) + 1),
        [shape_of((count, thin, 3 * width), F32)],
        [],
        0,
    )
    return (
        next_input.reshape(batches, tokens, width),
        grad_input.reshape(batches, tokens, width),
        grad_earlier.reshape(streams, batches, tokens, width),
        grad_in.reshape(share, 3 * width),
        grad_out.reshape(share, width),
        grad_up.reshape(share, inner),
        grad_down.reshape(inner // 4, width),
        norm_total[0],
        norm_total[1],
        norm_total[2],
        norm_total[3],
        mix_total,
    )


def heads_fit(batches):
    count = lax.axis_size("ctx")
    return (
        lax.axis_size("fsdp") == 4
        and count & (count - 1) == 0
        and count % batches == 0
        and HEADS % max(count // batches, 1) == 0
    )


def either_body(inputs, *rest):
    return (head_body if heads_fit(inputs.shape[0]) else body)(inputs, *rest)


def solution(mesh):
    placed = (
        P("fsdp", "ctx", None),
        P(None, "fsdp", "ctx", None),
        P("fsdp", None),
        P("fsdp", None),
        P("fsdp", None),
        P("fsdp", None),
        P("fsdp"),
        P("fsdp"),
        P("fsdp"),
        P("fsdp"),
        P(),
        P(),
        P("fsdp", "ctx", None),
    )
    return jax.shard_map(
        either_body,
        mesh=mesh,
        in_specs=placed,
        out_specs=(
            P("fsdp", "ctx", None),
            P("fsdp", "ctx", None),
            P(None, "fsdp", "ctx", None),
            P("fsdp", None),
            P("fsdp", None),
            P("fsdp", None),
            P("fsdp", None),
            P("fsdp"),
            P("fsdp"),
            P("fsdp"),
            P("fsdp"),
            P(),
        ),
        check_vma=False,
    )
```
